32 devices in a mesh: pos: 8 (over z, y), fr: 4 (over x, core).
Axes of the slice: x: 2, y: 2, z: 4, core: 2. Of those that a mesh axis runs over, the one named last changes fastest.
Arguments:
- inputs: bfloat16 [8, 2048, 1024], P('pos', 'fr'), may hold values from -6 to 6
- delays: int32 [32, 8], P('fr', 'pos'), may hold values from 0 to 2
- query_weight: bfloat16 [8, 1024, 1024], P('pos', 'fr'), may hold values from -0.1875 to 0.1875
- key_weight: bfloat16 [8, 1024, 1024], P('pos', 'fr'), may hold values from -0.1875 to 0.1875
- value_weight: bfloat16 [8, 1024, 1024], P('pos', 'fr'), may hold values from -0.1875 to 0.1875
- out_weight: bfloat16 [8, 1024, 1024], P('pos', 'fr'), may hold values from -0.375 to 0.375
- gate_weight: bfloat16 [8, 1024, 2816], P('pos', 'fr'), may hold values from -0.1875 to 0.1875
- up_weight: bfloat16 [8, 1024, 2816], P('pos', 'fr'), may hold values from -0.1875 to 0.1875
- down_weight: bfloat16 [8, 2816, 1024], P('pos', 'fr'), may hold values from -0.109375 to 0.109375
- attention_gain: bfloat16 [8, 1024], P('pos', 'fr'), may hold values from 0.099609375 to 1.8984375
- feed_gain: bfloat16 [8, 1024], P('pos', 'fr'), may hold values from 0.099609375 to 1.8984375
- cotangent: bfloat16 [8, 2048, 1024], P('pos', 'fr'), may hold values from -6 to 6
Outputs:
- output: bfloat16 [8, 2048, 1024], P('pos', 'fr')
- input_grad: bfloat16 [8, 2048, 1024], P('pos', 'fr')
- query_weight_grad: float32 [8, 1024, 1024], P('pos', 'fr')
- key_weight_grad: float32 [8, 1024, 1024], P('pos', 'fr')
- value_weight_grad: float32 [8, 1024, 1024], P('pos', 'fr')
- out_weight_grad: float32 [8, 1024, 1024], P('pos', 'fr')
- gate_weight_grad: float32 [8, 1024, 2816], P('pos', 'fr')
- up_weight_grad: float32 [8, 1024, 2816], P('pos', 'fr')
- down_weight_grad: float32 [8, 2816, 1024], P('pos', 'fr')
- attention_gain_grad: float32 [8, 1024], P('pos', 'fr')
- feed_gain_grad: float32 [8, 1024], P('pos', 'fr')
The draws below stay inside these ranges and needn't reach their ends.
All inputs are finite; a program needn't handle non-finite values.
Results may differ from the reference program's by a relative error of at most 0.02.
Values may be sent and summed in bfloat16 or wider, within the bound.
A program may use at most 256 MiB of HBM per device.

```python
import jax
import jax.numpy as jnp
from jax import lax

D = 1024
HEAD = 64
FF = 2816
POS = 8
F_DEV = 512
ITEM_FR = 64
FRAMES = 2048
ITEMS = 32
N_FR = 4


def set_ends(drawn, rng, low, high):
    index_at = [jax.random.randint(jax.random.fold_in(rng, axis), (), 0, length) for axis, length in enumerate(drawn.shape)]
    longest = drawn.shape.index(max(drawn.shape))
    beside = index_at[:longest] + [(index_at[longest] + 1) % drawn.shape[longest]] + index_at[longest + 1:]
    return drawn.at[tuple(index_at)].set(low).at[tuple(beside)].set(high)


def block_levels(key, shape, split, smallest, largest):
    loudness = 1.0
    for axis_at, shards_of in split:
        heights = jax.random.uniform(jax.random.fold_in(jax.random.fold_in(key, 6), axis_at), (shards_of,), jnp.float32, smallest / len(split), largest / len(split))
        loudness = loudness * jnp.repeat(jnp.exp(heights), shape[axis_at] // shards_of).reshape((-1,) + (1,) * (len(shape) - 1 - axis_at))
    return loudness


def normal_values(rng, shape, width, reach, cuts=(), kind=jnp.bfloat16):
    entries = width * jax.random.normal(rng, shape, jnp.float32)
    if cuts:
        entries = entries * block_levels(rng, shape, cuts, -0.22, 0.18)
    return jnp.clip(entries, -reach, reach).astype(kind)


def setup_inputs(seed: int = 0) -> dict:
    key_of = jax.random.split(jax.random.key(seed), 13)
    return {
        "inputs": normal_values(key_of[0], (POS, FRAMES, D), 1.0, 6.0, ((0, 8), (1, 4))),
        "delays": set_ends(jax.random.randint(key_of[1], (ITEMS, POS), 0, 3), jax.random.fold_in(key_of[1], 1), 0, 2).astype(jnp.int32),
        "query_weight": normal_values(key_of[2], (POS, D, D), D ** -0.5, 0.1875, ((0, 8), (1, 4))),
        "key_weight": normal_values(key_of[3], (POS, D, D), D ** -0.5, 0.1875, ((0, 8), (1, 4))),
        "value_weight": normal_values(key_of[4], (POS, D, D), D ** -0.5, 0.1875, ((0, 8), (1, 4))),
        "out_weight": normal_values(key_of[5], (POS, D, D), (D // 4) ** -0.5, 0.375, ((0, 8), (1, 4))),
        "gate_weight": normal_values(key_of[6], (POS, D, FF), D ** -0.5, 0.1875, ((0, 8), (1, 4))),
        "up_weight": normal_values(key_of[7], (POS, D, FF), D ** -0.5, 0.1875, ((0, 8), (1, 4))),
        "down_weight": normal_values(key_of[8], (POS, FF, D), FF ** -0.5, 0.109375, ((0, 8), (1, 4))),
        "attention_gain": jnp.clip(1.0 + 0.18 * jax.random.normal(key_of[9], (POS, D), jnp.float32), 0.099609375, 1.8984375).astype(jnp.bfloat16),
        "feed_gain": jnp.clip(1.0 + 0.18 * jax.random.normal(key_of[10], (POS, D), jnp.float32), 0.099609375, 1.8984375).astype(jnp.bfloat16),
        "cotangent": normal_values(key_of[11], (POS, FRAMES, D), 1.0, 6.0, ((0, 8), (1, 4))),
    }


@jax.custom_vjp
def low(v):
    return lax.optimization_barrier(v.astype(jnp.bfloat16)).astype(jnp.float32)

@jax.custom_vjp
def low_back(v):
    return v

def low_keep(v):
    return (low(v), None)

def low_pass(kept, grad):
    return (grad,)

def back_keep(v):
    return (v, None)

def back_low(kept, grad):
    return (low(grad),)
low.defvjp(low_keep, low_pass)
low_back.defvjp(back_keep, back_low)
EPSILON = 1e-06
NEGATIVE = -1e+30
PRECISE = lax.Precision.HIGHEST

def rms_norm(values, gain_row):
    scaling = lax.rsqrt(lax.optimization_barrier(jnp.mean(values * values, -1, keepdims=True)) + EPSILON)
    return values * scaling * gain_row[:, None, :]

def per_position(operand, weight):
    return jnp.einsum('pbd,pde->pbe', operand, weight, precision=PRECISE)

def layer_block(hidden, query_weight, key_weight, value_weight, out_weight, gate_weight, up_weight, down_weight, attention_gain, feed_gain):
    positions, frames, features = hidden.shape
    head_count = features // HEAD
    normed = low(rms_norm(hidden, attention_gain))
    queries = low_back(low(per_position(normed, query_weight))).reshape(positions, frames, head_count, HEAD)
    key_rows = low_back(low(per_position(normed, key_weight))).reshape(positions, frames, head_count, HEAD)
    value_rows = low_back(low(per_position(normed, value_weight))).reshape(positions, frames, head_count, HEAD)
    scores = low_back(jnp.einsum('pbhe,jbhe->bhpj', queries, key_rows, precision=PRECISE) * HEAD ** (-0.5))
    allowed = jnp.arange(positions)[:, None] >= jnp.arange(positions)[None, :]
    scores = jnp.where(allowed, scores, NEGATIVE)
    soft_low = low(jax.nn.softmax(scores, -1))
    attended = low_back(low(jnp.einsum('bhpj,jbhe->pbhe', soft_low, value_rows, precision=PRECISE)))
    attended = attended.reshape(positions, frames, features)
    branch = hidden + low_back(per_position(attended, out_weight))
    normed_two = low(rms_norm(branch, feed_gain))
    gate_act = low_back(per_position(normed_two, gate_weight))
    up_act = low_back(per_position(normed_two, up_weight))
    inner_act = low(jax.nn.silu(gate_act) * up_act)
    return branch + low_back(per_position(inner_act, down_weight))

def delayed_rows(source, delays):
    positions, frame_total, features = source.shape
    frame_index = jnp.arange(frame_total, dtype=jnp.int32)
    lag_table = jnp.repeat(delays, ITEM_FR, axis=0).T
    anchor = frame_index[None, :] - lag_table
    anchor_safe = jnp.maximum(anchor, 0).astype(jnp.int32)
    picked = jnp.take_along_axis(source, jnp.broadcast_to(anchor_safe[:, :, None], source.shape), axis=1)
    return jnp.where((anchor >= 0)[:, :, None], picked, 0.0)

def reference(inputs, delays, query_weight, key_weight, value_weight, out_weight, gate_weight, up_weight, down_weight, attention_gain, feed_gain, cotangent):
    params = tuple((tensor.astype(jnp.float32) for tensor in (query_weight, key_weight, value_weight, out_weight, gate_weight, up_weight, down_weight, attention_gain, feed_gain)))

    def forward(source, *weights):
        hidden = delayed_rows(source, delays)
        positions = hidden.shape[0]
        blocks = hidden.reshape(positions, N_FR, F_DEV, D).transpose(1, 0, 2, 3)

        def one_block(block_rows):
            return layer_block(block_rows, *weights)
        result = lax.map(jax.checkpoint(one_block), blocks)
        return result.transpose(1, 0, 2, 3).reshape(positions, N_FR * F_DEV, D)
    output, pullback = jax.vjp(forward, inputs.astype(jnp.float32), *params)
    gradients = pullback(cotangent.astype(jnp.float32))
    return (output.astype(jnp.bfloat16), gradients[0].astype(jnp.bfloat16), gradients[1], gradients[2], gradients[3], gradients[4], gradients[5], gradients[6], gradients[7], gradients[8], gradients[9])
```

```python
import functools

import jax
import jax.numpy as jnp
from jax import lax
from jax.experimental import pallas as pl
from jax.experimental.pallas import tpu as pltpu
from jax.sharding import PartitionSpec as P

HEAD = 64
LANES = 128
EPSILON = 1e-06
MESH = pl.DeviceIdType.MESH
F32 = jnp.float32
BF16 = jnp.bfloat16
ANY = pl.BlockSpec(memory_space=pl.ANY)
VMEM = pl.BlockSpec(memory_space=pltpu.VMEM)
DMA = pltpu.SemaphoreType.DMA
VMEM_BYTES = 64 * 1024 * 1024 - 65536


def greet(n_fr, n_pos):
    fr = lax.axis_index("fr")
    pos = lax.axis_index("pos")
    barrier = pltpu.get_barrier_semaphore()
    for k in range(1, n_fr):
        pl.semaphore_signal(
            barrier, inc=1, device_id={"fr": lax.rem(fr + k, n_fr)}, device_id_type=MESH
        )
    for k in range(1, n_pos):
        pl.semaphore_signal(
            barrier, inc=1, device_id={"pos": lax.rem(pos + k, n_pos)}, device_id_type=MESH
        )
    pl.semaphore_wait(barrier, n_fr + n_pos - 2)


def send(src, dst, send_sem, recv_sem, **device):
    return pltpu.make_async_remote_copy(
        src_ref=src,
        dst_ref=dst,
        send_sem=send_sem,
        recv_sem=recv_sem,
        device_id=device,
        device_id_type=MESH,
    )


def rows_of(index, rows):
    return pl.ds(pl.multiple_of(index * rows, rows), rows)


def head_sums(shape, feature_dim):
    features = lax.broadcasted_iota(jnp.int32, shape, feature_dim)
    heads = lax.broadcasted_iota(jnp.int32, shape, 1 - feature_dim)
    return (features // HEAD == heads).astype(BF16)


def sum_heads(product, sums):
    high = product.astype(BF16)
    low = (product - high.astype(F32)).astype(BF16)
    return jnp.dot(high, sums, preferred_element_type=F32) + jnp.dot(
        low, sums, preferred_element_type=F32
    )


def column_tile(columns):
    return 256 if columns % 256 == 0 else LANES


def multiply(rows_ref, weight_ref, out_ref):
    tile = column_tile(weight_ref.shape[1])

    def step(at, carry):
        columns = pl.ds(pl.multiple_of(at * tile, tile), tile)
        out_ref[:, columns] = jnp.dot(
            rows_ref[...], weight_ref[:, columns], preferred_element_type=F32
        ).astype(out_ref.dtype)
        return carry

    lax.fori_loop(0, weight_ref.shape[1] // tile, step, 0)


def peer_of(pos, k, n_pos):
    return lax.rem(pos + k, n_pos)


def forward_kernel(n_fr, n_pos, *refs):
    (
        own_rows,
        lags,
        gains,
        w0,
        w1,
        w2,
        w3,
        w4,
        w5,
        w6,
        o0,
        o1,
        o2,
        o3,
        o4,
        o5,
        o6,
        hidden_out,
        normed_out,
        attended_out,
        queries_out,
        keys_out,
        values_out,
        gains_out,
        f0,
        f1,
        f2,
        f3,
        f4,
        f5,
        f6,
        rim,
        gain_slots,
        hidden,
        normed,
        proj,
        turned,
        mixed,
        attended,
        score_slots,
        total,
        sums,
        spread,
        far_send,
        far_recv,
        near_send,
        near_recv,
        own_sem,
        out_sem,
        rim_sem,
        gain_send,
        gain_recv,
        turn_send,
        turn_recv,
        back_send,
        back_recv,
        act_sem,
    ) = refs
    shards = (w0, w1, w2, w3, w4, w5, w6)
    full_out = (o0, o1, o2, o3, o4, o5, o6)
    full = (f0, f1, f2, f3, f4, f5, f6)
    turned_out = (queries_out, keys_out, values_out)
    fr = lax.axis_index("fr")
    pos = lax.axis_index("pos")
    chips = n_fr // 2
    chip = fr // 2
    core = lax.rem(fr, 2)
    partner = chip * 2 + 1 - core
    frames, features = own_rows.shape
    part = frames // n_pos
    greet(n_fr, n_pos)

    edge = own_rows.shape[0] - rim.shape[0]
    rim_copy = send(
        own_rows.at[pl.ds(edge, rim.shape[0])],
        rim,
        rim_sem.at[0],
        rim_sem.at[1],
        fr=lax.rem(fr + 1, n_fr),
    )
    rim_copy.start()
    gain_copies = []
    for k in range(1, n_fr):
        copy = send(
            gains,
            gain_slots.at[fr],
            gain_send.at[k],
            gain_recv.at[k],
            fr=lax.rem(fr + k, n_fr),
        )
        copy.start()
        gain_copies.append(copy)
    far = {}
    near = {}
    own = {}
    for at, (shard, whole) in enumerate(zip(shards, full)):
        rows = shard.shape[0]
        for k in range(1, chips):
            there = lax.rem(chip + k, chips) * 2 + core
            far[at, k] = send(
                shard, whole.at[rows_of(fr, rows)], far_send.at[at, k], far_recv.at[at, k], fr=there
            )
            far[at, k].start()
        near[at, 0] = send(
            shard, whole.at[rows_of(fr, rows)], near_send.at[at, 0], near_recv.at[at, 0], fr=partner
        )
        near[at, 0].start()
        own[at] = pltpu.make_async_copy(shard, whole.at[rows_of(fr, rows)], own_sem.at[at])
        own[at].start()

    sums[...] = head_sums(sums.shape, 0)
    spread[...] = head_sums(spread.shape, 1)
    gain_slots[pl.ds(fr, 1)] = gains[...][None]
    for copy in gain_copies:
        copy.wait()
    gain_row = jnp.concatenate([gain_slots[at, 0:1, :] for at in range(n_fr)], 1)
    gains_out[...] = jnp.concatenate([gain_slots[at] for at in range(n_fr)], 1)
    rim_copy.wait()

    block = 64
    rim_rows = rim.shape[0]
    rim_all = jnp.where(fr == 0, 0.0, rim[...].astype(F32))[rim_rows - 8 :]

    def norm_block(at, carry):
        rows = pl.ds(pl.multiple_of(at * block, block), block)
        here = own_rows[rows, :].astype(F32)
        window = jnp.concatenate([carry, here], 0)
        once = pltpu.roll(window, 1, 0)[8:]
        twice = pltpu.roll(window, 2, 0)[8:]
        lag = lags[rows, :]
        values = jnp.where(lag == 0, here, jnp.where(lag == 1, once, twice))
        hidden[rows, :] = values.astype(BF16)
        scaling = lax.rsqrt(jnp.mean(values * values, -1, keepdims=True) + EPSILON)
        normed[rows, :] = (values * scaling * gain_row).astype(BF16)
        return here[block - 8 :]

    lax.fori_loop(0, frames // block, norm_block, rim_all)
    act_copies = [
        pltpu.make_async_copy(hidden, hidden_out, act_sem.at[0]),
        pltpu.make_async_copy(normed, normed_out, act_sem.at[1]),
    ]
    for copy in act_copies:
        copy.start()

    forwarded = {}
    outs = {}

    def pass_on(at):
        rows = shards[at].shape[0]
        for k in range(1, chips):
            far[at, k].wait_recv()
            origin = lax.rem(chip - k + chips, chips) * 2 + core
            near[at, k] = send(
                full[at].at[rows_of(origin, rows)],
                full[at].at[rows_of(origin, rows)],
                near_send.at[at, k],
                near_recv.at[at, k],
                fr=partner,
            )
            near[at, k].start()

    def complete(at):
        own[at].wait()
        for k in range(chips):
            near[at, k].wait_recv()
        outs[at] = pltpu.make_async_copy(full[at], full_out[at], out_sem.at[at])
        outs[at].start()

    def turn(which, k):
        peer = peer_of(pos, k, n_pos)
        return send(
            proj.at[which, rows_of(peer, part)],
            turned.at[which, pos],
            turn_send.at[which, k],
            turn_recv.at[which, k],
            pos=peer,
        )

    for which in range(3):
        pass_on(which)
        complete(which)
        multiply(normed, full[which], proj.at[which])

        def start_turn(k, carry):
            turn(which, k).start()
            return carry

        lax.fori_loop(1, n_pos, start_turn, 0)
        turned[which, pl.ds(pos, 1)] = proj[which, rows_of(pos, part), :][None]

    pass_on(3)
    pass_on(4)
    for which in range(3):

        def end_turn(k, carry):
            turn(which, k).wait()
            return carry

        lax.fori_loop(1, n_pos, end_turn, 0)
        copy = pltpu.make_async_copy(turned.at[which], turned_out[which], act_sem.at[2 + which])
        copy.start()
        act_copies.append(copy)

    def attend(at, carry):
        query = turned[0, at].astype(F32) * HEAD ** (-0.5)

        def score(j, highest):
            scores = sum_heads(query * turned[1, j].astype(F32), sums[...])
            score_slots[j] = scores
            return jnp.maximum(highest, scores)

        highest = lax.fori_loop(0, at + 1, score, jnp.full((part, LANES), -1e30, F32))

        def weigh(j, mass):
            return mass + jnp.exp(score_slots[j] - highest)

        mass = lax.fori_loop(0, at + 1, weigh, jnp.zeros((part, LANES), F32))
        logsum = highest + jnp.log(mass)
        total[...] = jnp.zeros_like(total)

        def mix(j, carry):
            soft_low = jnp.exp(score_slots[j] - logsum).astype(BF16)
            total[...] += jnp.dot(soft_low, spread[...], preferred_element_type=F32) * turned[
                2, j
            ].astype(F32)
            return carry

        lax.fori_loop(0, at + 1, mix, 0)
        mixed[at] = total[...].astype(BF16)

        @pl.when(at != pos)
        def _():
            send(
                mixed.at[at],
                attended.at[rows_of(pos, part)],
                back_send.at[at],
                back_recv.at[pos],
                pos=at,
            ).start()

        return carry

    lax.fori_loop(0, n_pos, attend, 0)
    attended[rows_of(pos, part), :] = mixed[pos]

    complete(3)
    complete(4)
    for at in (5, 6):
        pass_on(at)
        complete(at)

    def end_back(k, carry):
        peer = peer_of(pos, k, n_pos)
        send(
            mixed.at[peer],
            attended.at[rows_of(peer, part)],
            back_send.at[peer],
            back_recv.at[peer],
            pos=peer,
        ).wait()
        return carry

    lax.fori_loop(1, n_pos, end_back, 0)
    copy = pltpu.make_async_copy(attended, attended_out, act_sem.at[5])
    copy.start()
    act_copies.append(copy)
    for copy in far.values():
        copy.wait_send()
    for copy in near.values():
        copy.wait_send()
    for copy in outs.values():
        copy.wait()
    for copy in act_copies:
        copy.wait()


def forward_call(n_fr, n_pos, own_rows, lags, gains, shards):
    frames, features = own_rows.shape
    part = frames // n_pos
    count = len(shards)
    chips = n_fr // 2
    full = [(n_fr * shard.shape[0], shard.shape[1]) for shard in shards]
    act = jax.ShapeDtypeStruct((frames, features), BF16)
    turned = jax.ShapeDtypeStruct((n_pos, part, features), BF16)
    return pl.pallas_call(
        functools.partial(forward_kernel, n_fr, n_pos),
        name="forward",
        out_shape=[jax.ShapeDtypeStruct(shape, BF16) for shape in full]
        + [act, act, act, turned, turned, turned, jax.ShapeDtypeStruct((8, features), F32)],
        in_specs=[VMEM, VMEM, VMEM] + [ANY] * count,
        out_specs=[ANY] * (count + 6) + [VMEM],
        scratch_shapes=[pltpu.VMEM(shape, BF16) for shape in full]
        + [
            pltpu.VMEM((16, features), BF16),
            pltpu.VMEM((n_fr, *gains.shape), F32),
            pltpu.VMEM((frames, features), BF16),
            pltpu.VMEM((frames, features), BF16),
            pltpu.VMEM((3, frames, features), BF16),
            pltpu.VMEM((3, n_pos, part, features), BF16),
            pltpu.VMEM((n_pos, part, features), BF16),
            pltpu.VMEM((frames, features), BF16),
            pltpu.VMEM((n_pos, part, LANES), F32),
            pltpu.VMEM((part, features), F32),
            pltpu.VMEM((features, LANES), BF16),
            pltpu.VMEM((LANES, features), BF16),
            DMA((count, chips)),
            DMA((count, chips)),
            DMA((count, chips)),
            DMA((count, chips)),
            DMA((count,)),
            DMA((count,)),
            DMA((2,)),
            DMA((n_fr,)),
            DMA((n_fr,)),
            DMA((3, n_pos)),
            DMA((3, n_pos)),
            DMA((n_pos,)),
            DMA((n_pos,)),
            DMA((6,)),
        ],
        compiler_params=pltpu.CompilerParams(
            collective_id=0, has_side_effects=True, vmem_limit_bytes=VMEM_BYTES
        ),
    )(own_rows, lags, gains, *shards)


def rms_scaling(values):
    return lax.rsqrt(jnp.mean(values * values, -1, keepdims=True) + EPSILON)


def product(operand, weight):
    return jnp.dot(operand, weight, preferred_element_type=F32)


def outer_sum(operand, second):
    return lax.dot_general(operand, second, (((0,), (0,)), ((), ())), preferred_element_type=F32)


def back_product(grad_rows, weight):
    return lax.dot_general(grad_rows, weight, (((1,), (1,)), ((), ())), preferred_element_type=F32)


def norm_back(values, scaling, gain_row, grad_normed):
    weighted = gain_row * grad_normed
    return scaling * weighted - values * scaling**3 * jnp.mean(weighted * values, -1, keepdims=True)


def scatter_sum(grad):
    return lax.psum_scatter(
        grad[None].astype(BF16), "fr", scatter_dimension=1, tiled=True
    ).astype(F32)


def on_device(
    inputs,
    delays,
    query_weight,
    key_weight,
    value_weight,
    out_weight,
    gate_weight,
    up_weight,
    down_weight,
    attention_gain,
    feed_gain,
    cotangent,
):
    n_fr = lax.axis_size("fr")
    n_pos = lax.axis_size("pos")
    own_rows = inputs[0]
    frames, features = own_rows.shape
    part = frames // n_pos
    lags = jnp.repeat(delays[:, 0], frames // delays.shape[0])[:, None]
    gains = jnp.pad(jnp.concatenate([attention_gain, feed_gain], 0).astype(F32), ((0, 6), (0, 0)))
    shards = [
        weight[0]
        for weight in (
            query_weight,
            key_weight,
            value_weight,
            out_weight,
            gate_weight,
            up_weight,
            down_weight,
        )
    ]
    (
        query_full,
        key_full,
        value_full,
        out_full,
        gate_full,
        up_full,
        down_full,
        hidden,
        normed,
        attended,
        queries,
        keys,
        values,
        gain_rows,
    ) = forward_call(n_fr, n_pos, own_rows, lags, gains, shards)
    gain_one, gain_two = gain_rows[0:1], gain_rows[1:2]
    hidden = hidden.astype(F32)
    scaling = rms_scaling(hidden)
    branch = hidden + product(attended, out_full)
    scaling_two = rms_scaling(branch)
    normed_two = (branch * scaling_two * gain_two).astype(BF16)
    gate_act = product(normed_two, gate_full)
    up_act = product(normed_two, up_full)
    inner_act = (jax.nn.silu(gate_act) * up_act).astype(BF16)
    output = (branch + product(inner_act, down_full)).astype(BF16)
    grad_out = cotangent[0]
    grad_inner = back_product(grad_out, down_full)
    sigmoid_gate = jax.nn.sigmoid(gate_act)
    grad_gate = (
        grad_inner * up_act * sigmoid_gate * (1.0 + gate_act * (1.0 - sigmoid_gate))
    ).astype(BF16)
    grad_up = (grad_inner * jax.nn.silu(gate_act)).astype(BF16)
    down_grad = outer_sum(inner_act, grad_out)
    gate_grad = outer_sum(normed_two, grad_gate)
    up_grad = outer_sum(normed_two, grad_up)
    grad_normed_two = back_product(grad_gate, gate_full) + back_product(grad_up, up_full)
    feed_gain_grad = jnp.sum(grad_normed_two * branch * scaling_two, 0)
    grad_branch = grad_out.astype(F32) + norm_back(branch, scaling_two, gain_two, grad_normed_two)
    grad_branch_low = grad_branch.astype(BF16)
    out_grad = outer_sum(attended, grad_branch_low)
    grad_attended = back_product(grad_branch_low, out_full).astype(BF16)

    def turn(rows):
        return lax.all_to_all(rows.reshape(n_pos, part, features), "pos", 0, 0, tiled=True)

    heads = features // HEAD
    split = (n_pos, part, heads, HEAD)
    query_heads = queries.reshape(split)
    key_heads = keys.reshape(split)
    value_heads = values.reshape(split)
    grad_heads = turn(grad_attended).reshape(split)
    scores = jnp.einsum("pfhe,jfhe->pfhj", query_heads, key_heads, preferred_element_type=F32)
    scores = scores * HEAD ** (-0.5)
    index = jnp.arange(n_pos)
    allowed = (index[None, :] <= index[:, None])[:, None, None, :]
    soft = jax.nn.softmax(jnp.where(allowed, scores, -1e30), -1)
    soft_low = soft.astype(BF16)
    grad_soft = jnp.einsum("pfhe,jfhe->pfhj", grad_heads, value_heads, preferred_element_type=F32)
    centre = jnp.sum(grad_soft * soft, -1, keepdims=True)
    grad_scores = (soft * (grad_soft - centre)).astype(BF16)
    grad_queries = (
        jnp.einsum("pfhj,jfhe->pfhe", grad_scores, key_heads, preferred_element_type=F32)
        * HEAD ** (-0.5)
    )
    grad_keys = (
        jnp.einsum("pfhj,pfhe->jfhe", grad_scores, query_heads, preferred_element_type=F32)
        * HEAD ** (-0.5)
    )
    grad_values = jnp.einsum(
        "pfhj,pfhe->jfhe", soft_low, grad_heads, preferred_element_type=F32
    )
    grad_queries, grad_keys, grad_values = (
        turn(grad.astype(BF16).reshape(n_pos, part, features)).reshape(frames, features)
        for grad in (grad_queries, grad_keys, grad_values)
    )
    query_grad = outer_sum(normed, grad_queries)
    key_grad = outer_sum(normed, grad_keys)
    value_grad = outer_sum(normed, grad_values)
    grad_normed = (
        back_product(grad_queries, query_full)
        + back_product(grad_keys, key_full)
        + back_product(grad_values, value_full)
    )
    attention_gain_grad = jnp.sum(grad_normed * hidden * scaling, 0)
    grad_hidden = grad_branch + norm_back(hidden, scaling, gain_one, grad_normed)
    grad_extended = jnp.pad(jnp.where(lags == 0, grad_hidden, 0.0), ((2, 0), (0, 0)))
    grad_extended = grad_extended + jnp.pad(jnp.where(lags == 1, grad_hidden, 0.0), ((1, 1), (0, 0)))
    grad_extended = grad_extended + jnp.pad(jnp.where(lags == 2, grad_hidden, 0.0), ((0, 2), (0, 0)))
    rim_back = lax.ppermute(grad_extended[:2], "fr", [(i + 1, i) for i in range(n_fr - 1)])
    input_grad = (grad_extended[2:] + jnp.pad(rim_back, ((frames - 2, 0), (0, 0)))).astype(BF16)
    return (
        output[None],
        input_grad[None],
        scatter_sum(query_grad),
        scatter_sum(key_grad),
        scatter_sum(value_grad),
        scatter_sum(out_grad),
        scatter_sum(gate_grad),
        scatter_sum(up_grad),
        scatter_sum(down_grad),
        scatter_sum(attention_gain_grad),
        scatter_sum(feed_gain_grad),
    )


def solution(mesh):
    matrix = P("pos", "fr", None)
    vector = P("pos", "fr")
    return jax.shard_map(
        on_device,
        mesh=mesh,
        in_specs=(matrix, P("fr", "pos")) + (matrix,) * 7 + (vector, vector, matrix),
        out_specs=(matrix,) * 9 + (vector, vector),
        check_vma=False,
    )
```

```python
import functools

import jax
import jax.numpy as jnp
from jax import lax
from jax.experimental import pallas as pl
from jax.experimental.pallas import tpu as pltpu
from jax.sharding import PartitionSpec as P

HEAD = 64
LANES = 128
EPSILON = 1e-06
MESH = pl.DeviceIdType.MESH
F32 = jnp.float32
BF16 = jnp.bfloat16
ANY = pl.BlockSpec(memory_space=pl.ANY)
VMEM = pl.BlockSpec(memory_space=pltpu.VMEM)
DMA = pltpu.SemaphoreType.DMA
VMEM_BYTES = 64 * 1024 * 1024 - 65536


def greet(n_fr, n_pos):
    fr = lax.axis_index("fr")
    pos = lax.axis_index("pos")
    barrier = pltpu.get_barrier_semaphore()
    for k in range(1, n_fr):
        pl.semaphore_signal(
            barrier, inc=1, device_id={"fr": lax.rem(fr + k, n_fr)}, device_id_type=MESH
        )
    for k in range(1, n_pos):
        pl.semaphore_signal(
            barrier, inc=1, device_id={"pos": lax.rem(pos + k, n_pos)}, device_id_type=MESH
        )
    pl.semaphore_wait(barrier, n_fr + n_pos - 2)


def send(src, dst, send_sem, recv_sem, **device):
    return pltpu.make_async_remote_copy(
        src_ref=src,
        dst_ref=dst,
        send_sem=send_sem,
        recv_sem=recv_sem,
        device_id=device,
        device_id_type=MESH,
    )


def rows_of(index, rows):
    return pl.ds(pl.multiple_of(index * rows, rows), rows)


def head_sums(shape, feature_dim):
    features = lax.broadcasted_iota(jnp.int32, shape, feature_dim)
    heads = lax.broadcasted_iota(jnp.int32, shape, 1 - feature_dim)
    return (features // HEAD == heads).astype(BF16)


def sum_heads(product, sums):
    high = product.astype(BF16)
    low = (product - high.astype(F32)).astype(BF16)
    return jnp.dot(high, sums, preferred_element_type=F32) + jnp.dot(
        low, sums, preferred_element_type=F32
    )


def column_tile(columns):
    return 256 if columns % 256 == 0 else LANES


def multiply(rows_ref, weight_ref, out_ref):
    tile = column_tile(weight_ref.shape[1])

    def step(at, carry):
        columns = pl.ds(pl.multiple_of(at * tile, tile), tile)
        out_ref[:, columns] = jnp.dot(
            rows_ref[...], weight_ref[:, columns], preferred_element_type=F32
        ).astype(out_ref.dtype)
        return carry

    lax.fori_loop(0, weight_ref.shape[1] // tile, step, 0)


def peer_of(pos, k, n_pos):
    return lax.rem(pos + k, n_pos)


def forward_kernel(n_fr, n_pos, *refs):
    (
        own_rows,
        lags,
        gains,
        w0,
        w1,
        w2,
        w3,
        w4,
        w5,
        w6,
        o0,
        o1,
        o2,
        o3,
        o4,
        o5,
        o6,
        hidden_out,
        normed_out,
        attended_out,
        queries_out,
        keys_out,
        values_out,
        soft_out,
        gains_out,
        f0,
        f1,
        f2,
        f3,
        f4,
        f5,
        f6,
        rim,
        gain_slots,
        hidden,
        normed,
        proj,
        turned,
        mixed,
        attended,
        score_slots,
        soft_slots,
        total,
        sums,
        spread,
        far_send,
        far_recv,
        near_send,
        near_recv,
        own_sem,
        out_sem,
        rim_sem,
        gain_send,
        gain_recv,
        turn_send,
        turn_recv,
        back_send,
        back_recv,
        act_sem,
    ) = refs
    shards = (w0, w1, w2, w3, w4, w5, w6)
    full_out = (o0, o1, o2, o3, o4, o5, o6)
    full = (f0, f1, f2, f3, f4, f5, f6)
    turned_out = (queries_out, keys_out, values_out)
    fr = lax.axis_index("fr")
    pos = lax.axis_index("pos")
    chips = n_fr // 2
    chip = fr // 2
    core = lax.rem(fr, 2)
    partner = chip * 2 + 1 - core
    frames, features = own_rows.shape
    part = frames // n_pos
    greet(n_fr, n_pos)

    edge = own_rows.shape[0] - rim.shape[0]
    rim_copy = send(
        own_rows.at[pl.ds(edge, rim.shape[0])],
        rim,
        rim_sem.at[0],
        rim_sem.at[1],
        fr=lax.rem(fr + 1, n_fr),
    )
    rim_copy.start()
    gain_copies = []
    for k in range(1, n_fr):
        copy = send(
            gains,
            gain_slots.at[fr],
            gain_send.at[k],
            gain_recv.at[k],
            fr=lax.rem(fr + k, n_fr),
        )
        copy.start()
        gain_copies.append(copy)
    far = {}
    near = {}
    own = {}
    for at, (shard, whole) in enumerate(zip(shards, full)):
        rows = shard.shape[0]
        for k in range(1, chips):
            there = lax.rem(chip + k, chips) * 2 + core
            far[at, k] = send(
                shard, whole.at[rows_of(fr, rows)], far_send.at[at, k], far_recv.at[at, k], fr=there
            )
            far[at, k].start()
        near[at, 0] = send(
            shard, whole.at[rows_of(fr, rows)], near_send.at[at, 0], near_recv.at[at, 0], fr=partner
        )
        near[at, 0].start()
        own[at] = pltpu.make_async_copy(shard, whole.at[rows_of(fr, rows)], own_sem.at[at])
        own[at].start()

    sums[...] = head_sums(sums.shape, 0)
    spread[...] = head_sums(spread.shape, 1)
    gain_slots[pl.ds(fr, 1)] = gains[...][None]
    for copy in gain_copies:
        copy.wait()
    gain_row = jnp.concatenate([gain_slots[at, 0:1, :] for at in range(n_fr)], 1)
    gains_out[...] = jnp.concatenate([gain_slots[at] for at in range(n_fr)], 1)
    rim_copy.wait()

    block = 64
    rim_rows = rim.shape[0]
    rim_all = jnp.where(fr == 0, 0.0, rim[...].astype(F32))[rim_rows - 8 :]

    def norm_block(at, carry):
        rows = pl.ds(pl.multiple_of(at * block, block), block)
        here = own_rows[rows, :].astype(F32)
        window = jnp.concatenate([carry, here], 0)
        once = pltpu.roll(window, 1, 0)[8:]
        twice = pltpu.roll(window, 2, 0)[8:]
        lag = lags[rows, :]
        values = jnp.where(lag == 0, here, jnp.where(lag == 1, once, twice))
        hidden[rows, :] = values.astype(BF16)
        scaling = lax.rsqrt(jnp.mean(values * values, -1, keepdims=True) + EPSILON)
        normed[rows, :] = (values * scaling * gain_row).astype(BF16)
        return here[block - 8 :]

    lax.fori_loop(0, frames // block, norm_block, rim_all)
    act_copies = [
        pltpu.make_async_copy(hidden, hidden_out, act_sem.at[0]),
        pltpu.make_async_copy(normed, normed_out, act_sem.at[1]),
    ]
    for copy in act_copies:
        copy.start()

    forwarded = {}
    outs = {}

    def pass_on(at):
        rows = shards[at].shape[0]
        for k in range(1, chips):
            far[at, k].wait_recv()
            origin = lax.rem(chip - k + chips, chips) * 2 + core
            near[at, k] = send(
                full[at].at[rows_of(origin, rows)],
                full[at].at[rows_of(origin, rows)],
                near_send.at[at, k],
                near_recv.at[at, k],
                fr=partner,
            )
            near[at, k].start()

    def complete(at):
        own[at].wait()
        for k in range(chips):
            near[at, k].wait_recv()
        outs[at] = pltpu.make_async_copy(full[at], full_out[at], out_sem.at[at])
        outs[at].start()

    def turn(which, k):
        peer = peer_of(pos, k, n_pos)
        return send(
            proj.at[which, rows_of(peer, part)],
            turned.at[which, pos],
            turn_send.at[which, k],
            turn_recv.at[which, k],
            pos=peer,
        )

    for which in range(3):
        pass_on(which)
        complete(which)
        multiply(normed, full[which], proj.at[which])

        def start_turn(k, carry):
            turn(which, k).start()
            return carry

        lax.fori_loop(1, n_pos, start_turn, 0)
        turned[which, pl.ds(pos, 1)] = proj[which, rows_of(pos, part), :][None]

    pass_on(3)
    pass_on(4)
    for which in range(3):

        def end_turn(k, carry):
            turn(which, k).wait()
            return carry

        lax.fori_loop(1, n_pos, end_turn, 0)
        copy = pltpu.make_async_copy(turned.at[which], turned_out[which], act_sem.at[2 + which])
        copy.start()
        act_copies.append(copy)

    def attend(at, carry):
        query = turned[0, at].astype(F32) * HEAD ** (-0.5)

        def score(j, highest):
            scores = sum_heads(query * turned[1, j].astype(F32), sums[...])
            score_slots[j] = scores
            return jnp.maximum(highest, scores)

        highest = lax.fori_loop(0, at + 1, score, jnp.full((part, LANES), -1e30, F32))

        def weigh(j, mass):
            return mass + jnp.exp(score_slots[j] - highest)

        mass = lax.fori_loop(0, at + 1, weigh, jnp.zeros((part, LANES), F32))
        logsum = highest + jnp.log(mass)
        total[...] = jnp.zeros_like(total)

        def mix(j, carry):
            soft = jnp.exp(score_slots[j] - logsum)
            soft_slots[at, j] = soft
            soft_low = soft.astype(BF16)
            total[...] += jnp.dot(soft_low, spread[...], preferred_element_type=F32) * turned[
                2, j
            ].astype(F32)
            return carry

        lax.fori_loop(0, at + 1, mix, 0)
        mixed[at] = total[...].astype(BF16)

        @pl.when(at != pos)
        def _():
            send(
                mixed.at[at],
                attended.at[rows_of(pos, part)],
                back_send.at[at],
                back_recv.at[pos],
                pos=at,
            ).start()

        return carry

    lax.fori_loop(0, n_pos, attend, 0)
    copy = pltpu.make_async_copy(soft_slots, soft_out, act_sem.at[6])
    copy.start()
    act_copies.append(copy)
    attended[rows_of(pos, part), :] = mixed[pos]

    complete(3)
    complete(4)
    for at in (5, 6):
        pass_on(at)
        complete(at)

    def end_back(k, carry):
        peer = peer_of(pos, k, n_pos)
        send(
            mixed.at[peer],
            attended.at[rows_of(peer, part)],
            back_send.at[peer],
            back_recv.at[peer],
            pos=peer,
        ).wait()
        return carry

    lax.fori_loop(1, n_pos, end_back, 0)
    copy = pltpu.make_async_copy(attended, attended_out, act_sem.at[5])
    copy.start()
    act_copies.append(copy)
    for copy in far.values():
        copy.wait_send()
    for copy in near.values():
        copy.wait_send()
    for copy in outs.values():
        copy.wait()
    for copy in act_copies:
        copy.wait()


def forward_call(n_fr, n_pos, own_rows, lags, gains, shards):
    frames, features = own_rows.shape
    part = frames // n_pos
    count = len(shards)
    chips = n_fr // 2
    full = [(n_fr * shard.shape[0], shard.shape[1]) for shard in shards]
    act = jax.ShapeDtypeStruct((frames, features), BF16)
    turned = jax.ShapeDtypeStruct((n_pos, part, features), BF16)
    return pl.pallas_call(
        functools.partial(forward_kernel, n_fr, n_pos),
        name="forward",
        out_shape=[jax.ShapeDtypeStruct(shape, BF16) for shape in full]
        + [act, act, act, turned, turned, turned]
        + [
            jax.ShapeDtypeStruct((n_pos, n_pos, part, LANES), F32),
            jax.ShapeDtypeStruct((8, features), F32),
        ],
        in_specs=[VMEM, VMEM, VMEM] + [ANY] * count,
        out_specs=[ANY] * (count + 7) + [VMEM],
        scratch_shapes=[pltpu.VMEM(shape, BF16) for shape in full]
        + [
            pltpu.VMEM((16, features), BF16),
            pltpu.VMEM((n_fr, *gains.shape), F32),
            pltpu.VMEM((frames, features), BF16),
            pltpu.VMEM((frames, features), BF16),
            pltpu.VMEM((3, frames, features), BF16),
            pltpu.VMEM((3, n_pos, part, features), BF16),
            pltpu.VMEM((n_pos, part, features), BF16),
            pltpu.VMEM((frames, features), BF16),
            pltpu.VMEM((n_pos, part, LANES), F32),
            pltpu.VMEM((n_pos, n_pos, part, LANES), F32),
            pltpu.VMEM((part, features), F32),
            pltpu.VMEM((features, LANES), BF16),
            pltpu.VMEM((LANES, features), BF16),
            DMA((count, chips)),
            DMA((count, chips)),
            DMA((count, chips)),
            DMA((count, chips)),
            DMA((count,)),
            DMA((count,)),
            DMA((2,)),
            DMA((n_fr,)),
            DMA((n_fr,)),
            DMA((3, n_pos)),
            DMA((3, n_pos)),
            DMA((n_pos,)),
            DMA((n_pos,)),
            DMA((7,)),
        ],
        compiler_params=pltpu.CompilerParams(
            collective_id=0, has_side_effects=True, vmem_limit_bytes=VMEM_BYTES
        ),
    )(own_rows, lags, gains, *shards)


def rms_scaling(values):
    return lax.rsqrt(jnp.mean(values * values, -1, keepdims=True) + EPSILON)


def product(operand, weight):
    return jnp.dot(operand, weight, preferred_element_type=F32)


def back_product(grad_rows, weight):
    return lax.dot_general(grad_rows, weight, (((1,), (1,)), ((), ())), preferred_element_type=F32)


def sublane_sums(values):
    rows, features = values.shape
    return jnp.sum(values.reshape(rows // 8, 8, features), 0)


def backward_kernel(n_fr, n_pos, shard_rows, *refs):
    (
        lags,
        gain_rows,
        inner_t,
        cot,
        gate_low,
        up_low,
        normed_two_t,
        attended_t,
        normed_t,
        branch_in,
        hidden_in,
        queries,
        keys,
        values,
        soft_in,
        *weights,
    ) = refs[:22]
    kept_out = refs[22:29]
    come_out = refs[29:36]
    input_grad, gains_out = refs[36:38]
    held = refs[38:45]
    (
        made,
        down_slots,
        gate_slots,
        up_slots,
        small,
        inner_v,
        cot_v,
        gate_v,
        up_v,
        normed_two_v,
        attended_v,
        normed_v,
        branch,
        hidden,
        total,
        low_rows,
        grad_rows,
        turned,
        soft,
        soft_grads,
        score_slots,
        sum_rows,
        leaving,
        arrived,
        sums,
        spread,
        gain_split,
        gain_in,
        rim_out,
        rim_in,
        load_sem,
        stream_sem,
        give_send,
        take_recv,
        far_send,
        far_recv,
        kept_sem,
        turn_send,
        turn_recv,
        back_send,
        back_recv,
        gain_send,
        gain_recv,
        rim_sem,
        out_sem,
    ) = refs[45:]
    query_w, key_w, value_w, out_w, gate_w, up_w, down_w = weights
    fr = lax.axis_index("fr")
    pos = lax.axis_index("pos")
    chips = n_fr // 2
    chip = fr // 2
    core = lax.rem(fr, 2)
    partner = chip * 2 + 1 - core
    frames, features = cot.shape
    part = frames // n_pos
    tile = made.shape[-1]
    greet(n_fr, n_pos)

    loads = {}

    def load(name, src, dst):
        loads[name] = pltpu.make_async_copy(src, dst, load_sem.at[len(loads)])
        loads[name].start()

    def columns_of(t):
        return pl.ds(pl.multiple_of(t * tile, tile), tile)

    def feed_copies(t):
        slot = lax.rem(t, 2)
        return (
            pltpu.make_async_copy(
                down_w.at[columns_of(t)], down_slots.at[slot], stream_sem.at[slot, 0]
            ),
            pltpu.make_async_copy(
                gate_w.at[:, columns_of(t)], gate_slots.at[slot], stream_sem.at[slot, 1]
            ),
            pltpu.make_async_copy(
                up_w.at[:, columns_of(t)], up_slots.at[slot], stream_sem.at[slot, 2]
            ),
        )

    load("inner", inner_t, inner_v)
    load("cot", cot, cot_v)
    for copy in feed_copies(0):
        copy.start()
    load("gate", gate_low, gate_v)
    load("up", up_low, up_v)
    load("branch", branch_in, branch)
    load("out", out_w, small.at[0])
    load("normed_two", normed_two_t, normed_two_v)
    load("attended", attended_t, attended_v)
    load("queries", queries, turned.at[0])
    load("keys", keys, turned.at[1])
    load("values", values, turned.at[2])
    load("soft", soft_in, soft)
    load("normed", normed_t, normed_v)
    load("hidden", hidden_in, hidden)
    load("value_w", value_w, small.at[1])
    load("key_w", key_w, small.at[2])
    sums[...] = head_sums(sums.shape, 0)
    spread[...] = head_sums(spread.shape, 1)

    pending = []
    done = [0]

    def settle():
        while pending:
            pending.pop(0)()

    def reduce_weight(at, left_t, right):
        rows = shard_rows[at]
        tiles = right.shape[1] // tile
        base = done[0]
        done[0] += tiles
        group = max(1, 1024 // rows)

        def outgoing(t):
            slot = lax.rem(t + base, 2)
            return send(
                made.at[slot, 1 - core, :, pl.ds(0, rows)],
                held[at].at[t],
                give_send.at[slot],
                take_recv.at[at, t],
                fr=partner,
            )

        def consume(t):
            slot = lax.rem(t + base, 2)
            outgoing(t).wait_recv()
            for there in range(chips):
                held[at][t, there] = (
                    held[at][t, there].astype(F32) + made[slot, core, there, 0:rows].astype(F32)
                ).astype(BF16)
            pltpu.make_async_copy(
                held[at].at[t, chip], kept_out[at].at[:, columns_of(t)], kept_sem.at[at]
            ).start()
            for k in range(1, chips):
                there = lax.rem(chip + k, chips)
                send(
                    held[at].at[t, there],
                    come_out[at].at[k - 1, :, columns_of(t)],
                    far_send.at[at, k],
                    far_recv.at[at, k],
                    fr=there * 2 + core,
                ).start()

        def step(t, carry):
            slot = lax.rem(t + base, 2)

            @pl.when(t >= 2)
            def _():
                outgoing(t - 2).wait_send()

            for first in range(0, n_fr, group):
                last = min(first + group, n_fr)
                grads = product(left_t[first * rows : last * rows], right[:, columns_of(t)])
                for b in range(first, last):
                    made[slot, b % 2, b // 2, 0:rows] = grads[
                        (b - first) * rows : (b - first + 1) * rows
                    ].astype(BF16)
            outgoing(t).start()

            @pl.when(t >= 1)
            def _():
                consume(t - 1)

            return carry

        settle()
        lax.fori_loop(0, tiles, step, 0)

        def finish():
            consume(tiles - 1)
            outgoing(tiles - 2).wait_send()
            outgoing(tiles - 1).wait_send()

        pending.append(finish)

    loads["inner"].wait()
    loads["cot"].wait()
    reduce_weight(6, inner_v, cot_v)

    loads["gate"].wait()
    loads["up"].wait()
    feed_tiles = gate_v.shape[1] // tile
    total[...] = jnp.zeros_like(total)

    def feed(t, carry):
        slot = lax.rem(t, 2)

        @pl.when(t + 1 < feed_tiles)
        def _():
            for copy in feed_copies(t + 1):
                copy.start()

        for copy in feed_copies(t):
            copy.wait()
        columns = columns_of(t)
        grad_inner = back_product(cot_v[...], down_slots[slot])
        gate = gate_v[:, columns].astype(F32)
        sigmoid = jax.nn.sigmoid(gate)
        scaled = grad_inner * sigmoid
        gate_v[:, columns] = (
            scaled * up_v[:, columns].astype(F32) * (1.0 + gate * (1.0 - sigmoid))
        ).astype(BF16)
        up_v[:, columns] = (scaled * gate).astype(BF16)
        for at in range(features // tile):
            rows = slice(at * tile, (at + 1) * tile)
            total[:, rows] += back_product(
                gate_v[:, columns], gate_slots[slot, rows, :]
            ) + back_product(up_v[:, columns], up_slots[slot, rows, :])
        return carry

    lax.fori_loop(0, feed_tiles, feed, 0)
    settle()

    block = 64
    blocks = frames // block
    loads["branch"].wait()

    def block_rows(at):
        return pl.ds(pl.multiple_of(at * block, block), block)

    def feed_norm(at, carry):
        rows = block_rows(at)
        here = branch[rows, :]
        grads = total[rows, :]
        scaling = rms_scaling(here)
        weighted = gain_rows[1:2, :] * grads
        back = scaling * weighted - here * scaling**3 * jnp.mean(weighted * here, -1, keepdims=True)
        back = cot_v[rows, :].astype(F32) + back
        branch[rows, :] = back
        low_rows[rows, :] = back.astype(BF16)
        return carry + sublane_sums(grads * here * scaling)

    feed_gain = lax.fori_loop(0, blocks, feed_norm, jnp.zeros((8, features), F32))
    feed_gain = jnp.sum(feed_gain, 0, keepdims=True)

    loads["out"].wait()

    def turn_back(t, carry):
        columns = columns_of(t)
        grad_rows[:, columns] = back_product(low_rows[...], small[0, columns, :]).astype(BF16)
        return carry

    lax.fori_loop(0, features // tile, turn_back, 0)

    def turn(k):
        peer = peer_of(pos, k, n_pos)
        return send(
            grad_rows.at[rows_of(peer, part)],
            turned.at[3, pos],
            turn_send.at[k],
            turn_recv.at[k],
            pos=peer,
        )

    def start_turn(k, carry):
        turn(k).start()
        return carry

    lax.fori_loop(1, n_pos, start_turn, 0)
    turned[3, pl.ds(pos, 1)] = grad_rows[rows_of(pos, part), :][None]
    load("query_w", query_w, small.at[0])

    loads["normed_two"].wait()
    reduce_weight(4, normed_two_v, gate_v)
    reduce_weight(5, normed_two_v, up_v)
    loads["attended"].wait()
    reduce_weight(3, attended_v, low_rows)

    for name in ("queries", "keys", "values", "soft"):
        loads[name].wait()

    def end_turn(k, carry):
        turn(k).wait()
        return carry

    lax.fori_loop(1, n_pos, end_turn, 0)
    settle()

    def give_back(which, j):
        return send(
            leaving.at[which, j],
            arrived.at[which, rows_of(pos, part)],
            back_send.at[which, j],
            back_recv.at[which, pos],
            pos=j,
        )

    def part_sum(which, j, low, high, weight_of, other, scale):
        sum_rows[...] = jnp.zeros_like(sum_rows)

        def add(at, carry):
            sum_rows[...] += product(weight_of(at), spread[...]) * turned[other, at].astype(F32)
            return carry

        lax.fori_loop(low, high, add, 0)
        leaving[which, j] = (sum_rows[...] * scale).astype(BF16)

        @pl.when(j != pos)
        def _():
            give_back(which, j).start()

        @pl.when(j == pos)
        def _():
            arrived[which, rows_of(pos, part), :] = leaving[which, j]

    def value_part(k, carry):
        j = peer_of(pos, k, n_pos)
        part_sum(2, j, j, n_pos, lambda p: soft[p, j].astype(BF16), 3, 1.0)
        return carry

    lax.fori_loop(1, n_pos + 1, value_part, 0)

    def score_part(p, carry):
        grads = turned[3, p].astype(F32)

        def score(j, centre):
            scores = sum_heads(grads * turned[2, j].astype(F32), sums[...])
            score_slots[j] = scores
            return centre + scores * soft[p, j]

        centre = lax.fori_loop(0, p + 1, score, jnp.zeros((part, LANES), F32))

        def level(j, carry):
            soft_grads[p, j] = (soft[p, j] * (score_slots[j] - centre)).astype(BF16)
            return carry

        return lax.fori_loop(0, p + 1, level, carry)

    lax.fori_loop(0, n_pos, score_part, 0)

    def key_part(k, carry):
        j = peer_of(pos, k, n_pos)
        part_sum(1, j, j, n_pos, lambda p: soft_grads[p, j], 0, HEAD ** (-0.5))
        return carry

    lax.fori_loop(1, n_pos + 1, key_part, 0)

    def query_part(k, carry):
        p = peer_of(pos, k, n_pos)
        part_sum(0, p, 0, p + 1, lambda j: soft_grads[p, j], 1, HEAD ** (-0.5))
        return carry

    lax.fori_loop(1, n_pos + 1, query_part, 0)

    loads["normed"].wait()
    for which, slot, name in ((2, 1, "value_w"), (1, 2, "key_w"), (0, 0, "query_w")):

        def end_back(k, carry):
            peer = peer_of(pos, k, n_pos)
            send(
                leaving.at[which, peer],
                arrived.at[which, rows_of(peer, part)],
                back_send.at[which, peer],
                back_recv.at[which, peer],
                pos=peer,
            ).wait()
            return carry

        lax.fori_loop(1, n_pos, end_back, 0)
        reduce_weight(which, normed_v, arrived.at[which])
        loads[name].wait()

        def add_normed(t, carry):
            columns = columns_of(t)
            grads = back_product(arrived[which], small[slot, columns, :])
            total[:, columns] = grads if which == 2 else total[:, columns] + grads
            return carry

        lax.fori_loop(0, features // tile, add_normed, 0)

    loads["hidden"].wait()

    def attention_norm(at, carry):
        rows = block_rows(at)
        here = hidden[rows, :].astype(F32)
        grads = total[rows, :]
        scaling = rms_scaling(here)
        weighted = gain_rows[0:1, :] * grads
        back = scaling * weighted - here * scaling**3 * jnp.mean(weighted * here, -1, keepdims=True)
        branch[rows, :] = branch[rows, :] + back
        return carry + sublane_sums(grads * here * scaling)

    gain = lax.fori_loop(0, blocks, attention_norm, jnp.zeros((8, features), F32))
    gain = jnp.sum(gain, 0, keepdims=True)

    first_lags = lags[0:8, :]
    once = jnp.where(first_lags == 1, branch[0:8, :], 0.0)
    once = jnp.where(
        lax.broadcasted_iota(jnp.int32, once.shape, 0) == 0, 0.0, pltpu.roll(once, 1, 0)
    )
    rim_out[...] = once + jnp.where(first_lags == 2, branch[0:8, :], 0.0)
    rim_copy = send(
        rim_out, rim_in, rim_sem.at[0], rim_sem.at[1], fr=lax.rem(fr + n_fr - 1, n_fr)
    )
    rim_copy.start()
    gain_pair = jnp.concatenate([gain, feed_gain, jnp.zeros((6, features), F32)], 0)
    width = features // n_fr
    for b in range(n_fr):
        gain_split[b] = gain_pair[:, b * width : (b + 1) * width]
    gain_copies = []
    for k in range(1, n_fr):
        there = lax.rem(fr + k, n_fr)
        copy = send(
            gain_split.at[there], gain_in.at[fr], gain_send.at[k], gain_recv.at[k], fr=there
        )
        copy.start()
        gain_copies.append(copy)
    gain_in[pl.ds(fr, 1)] = gain_split[pl.ds(fr, 1)]
    settle()

    rim_copy.wait()
    rim = jnp.where(fr == n_fr - 1, 0.0, rim_in[...])

    def shift(at, carry):
        after_one, after_two = carry
        rows = block_rows(blocks - 1 - at)
        grads = branch[rows, :]
        lag = lags[rows, :]
        one = jnp.where(lag == 1, grads, 0.0)
        two = jnp.where(lag == 2, grads, 0.0)
        moved = pltpu.roll(jnp.concatenate([one, after_one], 0), block + 7, 0)[:block]
        moved = moved + pltpu.roll(jnp.concatenate([two, after_two], 0), block + 6, 0)[:block]
        low_rows[rows, :] = (jnp.where(lag == 0, grads, 0.0) + moved).astype(BF16)
        return one[:8], two[:8]

    lax.fori_loop(0, blocks, shift, (jnp.zeros_like(rim), rim))
    out_copy = pltpu.make_async_copy(low_rows, input_grad, out_sem.at[0])
    out_copy.start()
    for copy in gain_copies:
        copy.wait()
    gain_sum = gain_in[0]
    for b in range(1, n_fr):
        gain_sum = gain_sum + gain_in[b]
    gains_out[...] = gain_sum

    for at in range(7):
        pltpu.make_async_copy(kept_out[at], kept_out[at], kept_sem.at[at]).wait()
        for k in range(1, chips):
            there = lax.rem(chip + k, chips)
            send(
                come_out[at].at[k - 1],
                come_out[at].at[k - 1],
                far_send.at[at, k],
                far_recv.at[at, k],
                fr=there * 2 + core,
            ).wait()
    out_copy.wait()


def backward_call(n_fr, n_pos, shard_shapes, *operands):
    cot = operands[3]
    frames, features = cot.shape
    part = frames // n_pos
    chips = n_fr // 2
    tile = column_tile(features)
    count = len(shard_shapes)
    shard_rows = [rows for rows, _ in shard_shapes]
    hidden_units = operands[4].shape[1]
    most = max(shard_rows)
    return pl.pallas_call(
        functools.partial(backward_kernel, n_fr, n_pos, shard_rows),
        name="backward",
        out_shape=[jax.ShapeDtypeStruct(shape, BF16) for shape in shard_shapes]
        + [jax.ShapeDtypeStruct((chips - 1, *shape), BF16) for shape in shard_shapes]
        + [
            jax.ShapeDtypeStruct((frames, features), BF16),
            jax.ShapeDtypeStruct((8, features // n_fr), F32),
        ],
        in_specs=[VMEM, VMEM] + [ANY] * (len(operands) - 2),
        out_specs=[ANY] * (2 * count + 1) + [VMEM],
        scratch_shapes=[
            pltpu.VMEM((columns // tile, chips, rows, tile), BF16) for rows, columns in shard_shapes
        ]
        + [
            pltpu.VMEM((2, 2, chips, most, tile), BF16),
            pltpu.VMEM((2, tile, features), BF16),
            pltpu.VMEM((2, features, tile), BF16),
            pltpu.VMEM((2, features, tile), BF16),
            pltpu.VMEM((3, features, features), BF16),
            pltpu.VMEM((hidden_units, frames), BF16),
            pltpu.VMEM((frames, features), BF16),
            pltpu.VMEM((frames, hidden_units), BF16),
            pltpu.VMEM((frames, hidden_units), BF16),
            pltpu.VMEM((features, frames), BF16),
            pltpu.VMEM((features, frames), BF16),
            pltpu.VMEM((features, frames), BF16),
            pltpu.VMEM((frames, features), F32),
            pltpu.VMEM((frames, features), BF16),
            pltpu.VMEM((frames, features), F32),
            pltpu.VMEM((frames, features), BF16),
            pltpu.VMEM((frames, features), BF16),
            pltpu.VMEM((4, n_pos, part, features), BF16),
            pltpu.VMEM((n_pos, n_pos, part, LANES), F32),
            pltpu.VMEM((n_pos, n_pos, part, LANES), BF16),
            pltpu.VMEM((n_pos, part, LANES), F32),
            pltpu.VMEM((part, features), F32),
            pltpu.VMEM((3, n_pos, part, features), BF16),
            pltpu.VMEM((3, frames, features), BF16),
            pltpu.VMEM((features, LANES), BF16),
            pltpu.VMEM((LANES, features), BF16),
            pltpu.VMEM((n_fr, 8, features // n_fr), F32),
            pltpu.VMEM((n_fr, 8, features // n_fr), F32),
            pltpu.VMEM((8, features), F32),
            pltpu.VMEM((8, features), F32),
            DMA((17,)),
            DMA((2, 3)),
            DMA((2,)),
            DMA((count, max(columns for _, columns in shard_shapes) // tile)),
            DMA((count, chips)),
            DMA((count, chips)),
            DMA((count,)),
            DMA((n_pos,)),
            DMA((n_pos,)),
            DMA((3, n_pos)),
            DMA((3, n_pos)),
            DMA((n_fr,)),
            DMA((n_fr,)),
            DMA((2,)),
            DMA((1,)),
        ],
        compiler_params=pltpu.CompilerParams(
            collective_id=1, has_side_effects=True, vmem_limit_bytes=VMEM_BYTES
        ),
    )(*operands)


def on_device(
    inputs,
    delays,
    query_weight,
    key_weight,
    value_weight,
    out_weight,
    gate_weight,
    up_weight,
    down_weight,
    attention_gain,
    feed_gain,
    cotangent,
):
    n_fr = lax.axis_size("fr")
    n_pos = lax.axis_size("pos")
    own_rows = inputs[0]
    frames, features = own_rows.shape
    lags = jnp.repeat(delays[:, 0], frames // delays.shape[0])[:, None]
    gains = jnp.pad(jnp.concatenate([attention_gain, feed_gain], 0).astype(F32), ((0, 6), (0, 0)))
    shards = [
        weight[0]
        for weight in (
            query_weight,
            key_weight,
            value_weight,
            out_weight,
            gate_weight,
            up_weight,
            down_weight,
        )
    ]
    *full, hidden, normed, attended, queries, keys, values, soft, gain_rows = forward_call(
        n_fr, n_pos, own_rows, lags, gains, shards
    )
    out_full, gate_full, up_full, down_full = full[3:]
    branch = hidden.astype(F32) + product(attended, out_full)
    normed_two = (branch * rms_scaling(branch) * gain_rows[1:2]).astype(BF16)
    gate_act = product(normed_two, gate_full)
    up_act = product(normed_two, up_full)
    inner_act = (jax.nn.silu(gate_act) * up_act).astype(BF16)
    output = (branch + product(inner_act, down_full)).astype(BF16)
    grads = backward_call(
        n_fr,
        n_pos,
        [shard.shape for shard in shards],
        lags,
        gain_rows,
        inner_act.T,
        cotangent[0],
        gate_act.astype(BF16),
        up_act.astype(BF16),
        normed_two.T,
        attended.T,
        normed.T,
        branch,
        hidden,
        queries,
        keys,
        values,
        soft,
        *full,
    )
    kept, come, (input_grad, gain_grads) = grads[:7], grads[7:14], grads[14:]
    return (
        output[None],
        input_grad[None],
        *(
            (own.astype(F32) + jnp.sum(others.astype(F32), 0))[None]
            for own, others in zip(kept, come)
        ),
        gain_grads[0:1],
        gain_grads[1:2],
    )


def solution(mesh):
    matrix = P("pos", "fr", None)
    vector = P("pos", "fr")
    return jax.shard_map(
        on_device,
        mesh=mesh,
        in_specs=(matrix, P("fr", "pos")) + (matrix,) * 7 + (vector, vector, matrix),
        out_specs=(matrix,) * 9 + (vector, vector),
        check_vma=False,
    )
```

```python
import functools

import jax
import jax.numpy as jnp
from jax import lax
from jax.experimental import pallas as pl
from jax.experimental.pallas import tpu as pltpu
from jax.sharding import PartitionSpec as P

HEAD = 64
LANES = 128
EPSILON = 1e-06
MESH = pl.DeviceIdType.MESH
F32 = jnp.float32
BF16 = jnp.bfloat16
ANY = pl.BlockSpec(memory_space=pl.ANY)
VMEM = pl.BlockSpec(memory_space=pltpu.VMEM)
DMA = pltpu.SemaphoreType.DMA
VMEM_BYTES = 64 * 1024 * 1024 - 65536


def greet(n_fr, n_pos):
    fr = lax.axis_index("fr")
    pos = lax.axis_index("pos")
    barrier = pltpu.get_barrier_semaphore()
    for k in range(1, n_fr):
        pl.semaphore_signal(
            barrier, inc=1, device_id={"fr": lax.rem(fr + k, n_fr)}, device_id_type=MESH
        )
    for k in range(1, n_pos):
        pl.semaphore_signal(
            barrier, inc=1, device_id={"pos": lax.rem(pos + k, n_pos)}, device_id_type=MESH
        )
    pl.semaphore_wait(barrier, n_fr + n_pos - 2)


def send(src, dst, send_sem, recv_sem, **device):
    return pltpu.make_async_remote_copy(
        src_ref=src,
        dst_ref=dst,
        send_sem=send_sem,
        recv_sem=recv_sem,
        device_id=device,
        device_id_type=MESH,
    )


def rows_of(index, rows):
    return pl.ds(pl.multiple_of(index * rows, rows), rows)


def head_sums(shape, feature_dim):
    features = lax.broadcasted_iota(jnp.int32, shape, feature_dim)
    heads = lax.broadcasted_iota(jnp.int32, shape, 1 - feature_dim)
    return (features // HEAD == heads).astype(BF16)


def sum_heads(product, sums):
    high = product.astype(BF16)
    low = (product - high.astype(F32)).astype(BF16)
    return jnp.dot(high, sums, preferred_element_type=F32) + jnp.dot(
        low, sums, preferred_element_type=F32
    )


def rms_scaling(values):
    return lax.rsqrt(jnp.mean(values * values, -1, keepdims=True) + EPSILON)


def product(operand, weight):
    return jnp.dot(operand, weight, preferred_element_type=F32)


def column_tile(columns):
    return 256 if columns % 256 == 0 else LANES


def multiply(rows_ref, weight_ref, out_ref):
    tile = column_tile(weight_ref.shape[1])

    def step(at, carry):
        columns = pl.ds(pl.multiple_of(at * tile, tile), tile)
        out_ref[:, columns] = jnp.dot(
            rows_ref[...], weight_ref[:, columns], preferred_element_type=F32
        ).astype(out_ref.dtype)
        return carry

    lax.fori_loop(0, weight_ref.shape[1] // tile, step, 0)


def peer_of(pos, k, n_pos):
    return lax.rem(pos + k, n_pos)


def forward_kernel(n_fr, n_pos, *refs):
    (
        own_rows,
        lags,
        gains,
        w0,
        w1,
        w2,
        w3,
        w4,
        w5,
        w6,
        o0,
        o1,
        o2,
        o3,
        o4,
        o5,
        o6,
        output_out,
        inner_out,
        gate_out,
        up_out,
        normed_two_out,
        attended_out,
        normed_out,
        branch_out,
        hidden_out,
        queries_out,
        keys_out,
        values_out,
        soft_out,
        gains_out,
        f0,
        f1,
        f2,
        f3,
        f4,
        f5,
        f6,
        rim,
        gain_slots,
        hidden,
        normed,
        proj,
        turned,
        mixed,
        attended,
        normed_t,
        attended_t,
        normed_two_t,
        normed_two,
        inner,
        inner_t,
        gate_low,
        up_low,
        branch,
        output,
        score_slots,
        soft_slots,
        total,
        sums,
        spread,
        far_send,
        far_recv,
        near_send,
        near_recv,
        own_sem,
        out_sem,
        rim_sem,
        gain_send,
        gain_recv,
        turn_send,
        turn_recv,
        back_send,
        back_recv,
        act_sem,
    ) = refs
    shards = (w0, w1, w2, w3, w4, w5, w6)
    full_out = (o0, o1, o2, o3, o4, o5, o6)
    full = (f0, f1, f2, f3, f4, f5, f6)
    turned_out = (queries_out, keys_out, values_out)
    fr = lax.axis_index("fr")
    pos = lax.axis_index("pos")
    chips = n_fr // 2
    chip = fr // 2
    core = lax.rem(fr, 2)
    partner = chip * 2 + 1 - core
    frames, features = own_rows.shape
    part = frames // n_pos
    greet(n_fr, n_pos)

    edge = own_rows.shape[0] - rim.shape[0]
    rim_copy = send(
        own_rows.at[pl.ds(edge, rim.shape[0])],
        rim,
        rim_sem.at[0],
        rim_sem.at[1],
        fr=lax.rem(fr + 1, n_fr),
    )
    rim_copy.start()
    gain_copies = []
    for k in range(1, n_fr):
        copy = send(
            gains,
            gain_slots.at[fr],
            gain_send.at[k],
            gain_recv.at[k],
            fr=lax.rem(fr + k, n_fr),
        )
        copy.start()
        gain_copies.append(copy)
    far = {}
    near = {}
    own = {}
    for at, (shard, whole) in enumerate(zip(shards, full)):
        rows = shard.shape[0]
        for k in range(1, chips):
            there = lax.rem(chip + k, chips) * 2 + core
            far[at, k] = send(
                shard, whole.at[rows_of(fr, rows)], far_send.at[at, k], far_recv.at[at, k], fr=there
            )
            far[at, k].start()
        near[at, 0] = send(
            shard, whole.at[rows_of(fr, rows)], near_send.at[at, 0], near_recv.at[at, 0], fr=partner
        )
        near[at, 0].start()
        own[at] = pltpu.make_async_copy(shard, whole.at[rows_of(fr, rows)], own_sem.at[at])
        own[at].start()

    sums[...] = head_sums(sums.shape, 0)
    spread[...] = head_sums(spread.shape, 1)
    gain_slots[pl.ds(fr, 1)] = gains[...][None]
    for copy in gain_copies:
        copy.wait()
    gain_row = jnp.concatenate([gain_slots[at, 0:1, :] for at in range(n_fr)], 1)
    gains_out[...] = jnp.concatenate([gain_slots[at] for at in range(n_fr)], 1)
    rim_copy.wait()

    block = 64
    rim_rows = rim.shape[0]
    rim_all = jnp.where(fr == 0, 0.0, rim[...].astype(F32))[rim_rows - 8 :]

    def norm_block(at, carry):
        rows = pl.ds(pl.multiple_of(at * block, block), block)
        here = own_rows[rows, :].astype(F32)
        window = jnp.concatenate([carry, here], 0)
        once = pltpu.roll(window, 1, 0)[8:]
        twice = pltpu.roll(window, 2, 0)[8:]
        lag = lags[rows, :]
        values = jnp.where(lag == 0, here, jnp.where(lag == 1, once, twice))
        hidden[rows, :] = values.astype(BF16)
        scaling = lax.rsqrt(jnp.mean(values * values, -1, keepdims=True) + EPSILON)
        normed[rows, :] = (values * scaling * gain_row).astype(BF16)
        return here[block - 8 :]

    lax.fori_loop(0, frames // block, norm_block, rim_all)
    act_copies = []

    def put(src, dst):
        act_copies.append(pltpu.make_async_copy(src, dst, act_sem.at[len(act_copies)]))
        act_copies[-1].start()

    put(hidden, hidden_out)

    outs = {}

    def pass_on(at):
        rows = shards[at].shape[0]
        for k in range(1, chips):
            far[at, k].wait_recv()
            origin = lax.rem(chip - k + chips, chips) * 2 + core
            near[at, k] = send(
                full[at].at[rows_of(origin, rows)],
                full[at].at[rows_of(origin, rows)],
                near_send.at[at, k],
                near_recv.at[at, k],
                fr=partner,
            )
            near[at, k].start()

    def complete(at):
        own[at].wait()
        for k in range(chips):
            near[at, k].wait_recv()
        outs[at] = pltpu.make_async_copy(full[at], full_out[at], out_sem.at[at])
        outs[at].start()

    def turn(which, k):
        peer = peer_of(pos, k, n_pos)
        return send(
            proj.at[which, rows_of(peer, part)],
            turned.at[which, pos],
            turn_send.at[which, k],
            turn_recv.at[which, k],
            pos=peer,
        )

    for which in range(3):
        pass_on(which)
        complete(which)
        multiply(normed, full[which], proj.at[which])

        def start_turn(k, carry):
            turn(which, k).start()
            return carry

        lax.fori_loop(1, n_pos, start_turn, 0)
        turned[which, pl.ds(pos, 1)] = proj[which, rows_of(pos, part), :][None]

    def transpose(src, dst):
        tile = column_tile(src.shape[1])

        def step(t, carry):
            at = pl.ds(pl.multiple_of(t * tile, tile), tile)
            dst[at, :] = src[:, at].T
            return carry

        lax.fori_loop(0, src.shape[1] // tile, step, 0)

    transpose(normed, normed_t)
    put(normed_t, normed_out)
    pass_on(3)

    def end_turns(which):
        def end_turn(k, carry):
            turn(which, k).wait()
            return carry

        lax.fori_loop(1, n_pos, end_turn, 0)
        put(turned.at[which], turned_out[which])

    end_turns(0)
    end_turns(1)

    def score_rows(p, carry):
        query = turned[0, p].astype(F32) * HEAD ** (-0.5)

        def score(j, highest):
            scores = sum_heads(query * turned[1, j].astype(F32), sums[...])
            score_slots[j] = scores
            return jnp.maximum(highest, scores)

        highest = lax.fori_loop(0, p + 1, score, jnp.full((part, LANES), -1e30, F32))

        def weigh(j, mass):
            return mass + jnp.exp(score_slots[j] - highest)

        mass = lax.fori_loop(0, p + 1, weigh, jnp.zeros((part, LANES), F32))
        logsum = highest + jnp.log(mass)

        def level(j, carry):
            soft_slots[p, j] = jnp.exp(score_slots[j] - logsum)
            return carry

        return lax.fori_loop(0, p + 1, level, carry)

    lax.fori_loop(0, n_pos, score_rows, 0)
    put(soft_slots, soft_out)
    pass_on(4)
    end_turns(2)

    def back(p):
        return send(
            mixed.at[p],
            attended.at[rows_of(pos, part)],
            back_send.at[p],
            back_recv.at[pos],
            pos=p,
        )

    def mix_rows(k, carry):
        p = peer_of(pos, k, n_pos)
        total[...] = jnp.zeros_like(total)

        def mix(j, carry):
            total[...] += product(soft_slots[p, j].astype(BF16), spread[...]) * turned[
                2, j
            ].astype(F32)
            return carry

        lax.fori_loop(0, p + 1, mix, 0)
        mixed[p] = total[...].astype(BF16)

        @pl.when(p != pos)
        def _():
            back(p).start()

        @pl.when(p == pos)
        def _():
            attended[rows_of(pos, part), :] = mixed[p]

        return carry

    lax.fori_loop(1, n_pos + 1, mix_rows, 0)
    complete(3)
    complete(4)
    pass_on(5)

    def end_back(k, carry):
        peer = peer_of(pos, k, n_pos)
        send(
            mixed.at[peer],
            attended.at[rows_of(peer, part)],
            back_send.at[peer],
            back_recv.at[peer],
            pos=peer,
        ).wait()
        return carry

    lax.fori_loop(1, n_pos, end_back, 0)
    complete(5)
    tile = column_tile(features)

    def columns_of(t):
        return pl.ds(pl.multiple_of(t * tile, tile), tile)

    def leave(t, carry):
        columns = columns_of(t)
        branch[:, columns] = hidden[:, columns].astype(F32) + product(
            attended[...], full[3][:, columns]
        )
        return carry

    lax.fori_loop(0, features // tile, leave, 0)
    put(branch, branch_out)
    gain_two = gains_out[1:2, :]

    def norm_two(at, carry):
        rows = pl.ds(pl.multiple_of(at * block, block), block)
        here = branch[rows, :]
        normed_two[rows, :] = (here * rms_scaling(here) * gain_two).astype(BF16)
        return carry

    lax.fori_loop(0, frames // block, norm_two, 0)

    def feed(t, carry):
        columns = columns_of(t)
        gate = product(normed_two[...], full[4][:, columns])
        up = product(normed_two[...], full[5][:, columns])
        gate_low[:, columns] = gate.astype(BF16)
        up_low[:, columns] = up.astype(BF16)
        low = (gate * jax.nn.sigmoid(gate) * up).astype(BF16)
        inner[:, columns] = low
        inner_t[columns, :] = low.T
        return carry

    lax.fori_loop(0, inner.shape[1] // tile, feed, 0)
    put(gate_low, gate_out)
    put(up_low, up_out)
    put(inner_t, inner_out)
    transpose(attended, attended_t)
    put(attended_t, attended_out)
    transpose(normed_two, normed_two_t)
    put(normed_two_t, normed_two_out)
    pass_on(6)
    complete(6)

    def close(t, carry):
        columns = columns_of(t)
        output[:, columns] = (
            branch[:, columns] + product(inner[...], full[6][:, columns])
        ).astype(BF16)
        return carry

    lax.fori_loop(0, features // tile, close, 0)
    put(output, output_out)
    for copy in far.values():
        copy.wait_send()
    for copy in near.values():
        copy.wait_send()
    for copy in outs.values():
        copy.wait()
    for copy in act_copies:
        copy.wait()


def forward_call(n_fr, n_pos, own_rows, lags, gains, shards):
    frames, features = own_rows.shape
    part = frames // n_pos
    count = len(shards)
    chips = n_fr // 2
    full = [(n_fr * shard.shape[0], shard.shape[1]) for shard in shards]
    hidden_units = shards[4].shape[1]
    act = jax.ShapeDtypeStruct((frames, features), BF16)
    act_t = jax.ShapeDtypeStruct((features, frames), BF16)
    wide = jax.ShapeDtypeStruct((frames, hidden_units), BF16)
    wide_t = jax.ShapeDtypeStruct((hidden_units, frames), BF16)
    turned = jax.ShapeDtypeStruct((n_pos, part, features), BF16)
    return pl.pallas_call(
        functools.partial(forward_kernel, n_fr, n_pos),
        name="forward",
        out_shape=[jax.ShapeDtypeStruct(shape, BF16) for shape in full]
        + [act, wide_t, wide, wide, act_t, act_t, act_t]
        + [jax.ShapeDtypeStruct((frames, features), F32), act, turned, turned, turned]
        + [
            jax.ShapeDtypeStruct((n_pos, n_pos, part, LANES), F32),
            jax.ShapeDtypeStruct((8, features), F32),
        ],
        in_specs=[VMEM, VMEM, VMEM] + [ANY] * count,
        out_specs=[ANY] * (count + 13) + [VMEM],
        scratch_shapes=[pltpu.VMEM(shape, BF16) for shape in full]
        + [
            pltpu.VMEM((16, features), BF16),
            pltpu.VMEM((n_fr, *gains.shape), F32),
            pltpu.VMEM((frames, features), BF16),
            pltpu.VMEM((frames, features), BF16),
            pltpu.VMEM((3, frames, features), BF16),
            pltpu.VMEM((3, n_pos, part, features), BF16),
            pltpu.VMEM((n_pos, part, features), BF16),
            pltpu.VMEM((frames, features), BF16),
            pltpu.VMEM((features, frames), BF16),
            pltpu.VMEM((features, frames), BF16),
            pltpu.VMEM((features, frames), BF16),
            pltpu.VMEM((frames, features), BF16),
            pltpu.VMEM((frames, hidden_units), BF16),
            pltpu.VMEM((hidden_units, frames), BF16),
            pltpu.VMEM((frames, hidden_units), BF16),
            pltpu.VMEM((frames, hidden_units), BF16),
            pltpu.VMEM((frames, features), F32),
            pltpu.VMEM((frames, features), BF16),
            pltpu.VMEM((n_pos, part, LANES), F32),
            pltpu.VMEM((n_pos, n_pos, part, LANES), F32),
            pltpu.VMEM((part, features), F32),
            pltpu.VMEM((features, LANES), BF16),
            pltpu.VMEM((LANES, features), BF16),
            DMA((count, chips)),
            DMA((count, chips)),
            DMA((count, chips)),
            DMA((count, chips)),
            DMA((count,)),
            DMA((count,)),
            DMA((2,)),
            DMA((n_fr,)),
            DMA((n_fr,)),
            DMA((3, n_pos)),
            DMA((3, n_pos)),
            DMA((n_pos,)),
            DMA((n_pos,)),
            DMA((14,)),
        ],
        compiler_params=pltpu.CompilerParams(
            collective_id=0, has_side_effects=True, vmem_limit_bytes=VMEM_BYTES
        ),
    )(own_rows, lags, gains, *shards)


def back_product(grad_rows, weight):
    return lax.dot_general(grad_rows, weight, (((1,), (1,)), ((), ())), preferred_element_type=F32)


def sublane_sums(values):
    rows, features = values.shape
    return jnp.sum(values.reshape(rows // 8, 8, features), 0)


def backward_kernel(n_fr, n_pos, shard_rows, *refs):
    (
        lags,
        gain_rows,
        inner_t,
        cot,
        gate_low,
        up_low,
        normed_two_t,
        attended_t,
        normed_t,
        branch_in,
        hidden_in,
        queries,
        keys,
        values,
        soft_in,
        *weights,
    ) = refs[:22]
    kept_out = refs[22:29]
    come_out = refs[29:36]
    input_grad, gains_out = refs[36:38]
    held = refs[38:45]
    (
        made,
        down_slots,
        gate_slots,
        up_slots,
        small,
        inner_v,
        cot_v,
        gate_v,
        up_v,
        normed_two_v,
        attended_v,
        normed_v,
        branch,
        hidden,
        total,
        low_rows,
        grad_rows,
        turned,
        soft,
        soft_grads,
        score_slots,
        sum_rows,
        leaving,
        arrived,
        sums,
        spread,
        gain_split,
        gain_in,
        rim_out,
        rim_in,
        load_sem,
        stream_sem,
        give_send,
        take_recv,
        far_send,
        far_recv,
        kept_sem,
        turn_send,
        turn_recv,
        back_send,
        back_recv,
        gain_send,
        gain_recv,
        rim_sem,
        out_sem,
    ) = refs[45:]
    query_w, key_w, value_w, out_w, gate_w, up_w, down_w = weights
    fr = lax.axis_index("fr")
    pos = lax.axis_index("pos")
    chips = n_fr // 2
    chip = fr // 2
    core = lax.rem(fr, 2)
    partner = chip * 2 + 1 - core
    frames, features = cot.shape
    part = frames // n_pos
    tile = made.shape[-1]
    greet(n_fr, n_pos)

    loads = {}

    def load(name, src, dst):
        loads[name] = pltpu.make_async_copy(src, dst, load_sem.at[len(loads)])
        loads[name].start()

    def columns_of(t):
        return pl.ds(pl.multiple_of(t * tile, tile), tile)

    def feed_copies(t):
        slot = lax.rem(t, 2)
        return (
            pltpu.make_async_copy(
                down_w.at[columns_of(t)], down_slots.at[slot], stream_sem.at[slot, 0]
            ),
            pltpu.make_async_copy(
                gate_w.at[:, columns_of(t)], gate_slots.at[slot], stream_sem.at[slot, 1]
            ),
            pltpu.make_async_copy(
                up_w.at[:, columns_of(t)], up_slots.at[slot], stream_sem.at[slot, 2]
            ),
        )

    load("inner", inner_t, inner_v)
    load("cot", cot, cot_v)
    for copy in feed_copies(0):
        copy.start()
    load("gate", gate_low, gate_v)
    load("up", up_low, up_v)
    load("branch", branch_in, branch)
    load("out", out_w, small.at[0])
    load("normed_two", normed_two_t, normed_two_v)
    load("attended", attended_t, attended_v)
    load("queries", queries, turned.at[0])
    load("keys", keys, turned.at[1])
    load("values", values, turned.at[2])
    load("soft", soft_in, soft)
    load("normed", normed_t, normed_v)
    load("hidden", hidden_in, hidden)
    load("value_w", value_w, small.at[1])
    load("key_w", key_w, small.at[2])
    sums[...] = head_sums(sums.shape, 0)
    spread[...] = head_sums(spread.shape, 1)

    pending = []
    done = [0]

    def settle():
        while pending:
            pending.pop(0)()

    def reduce_weight(at, left_t, right):
        rows = shard_rows[at]
        tiles = right.shape[1] // tile
        base = done[0]
        done[0] += tiles
        group = max(1, 1024 // rows)

        def outgoing(t):
            slot = lax.rem(t + base, 2)
            return send(
                made.at[slot, 1 - core, :, pl.ds(0, rows)],
                held[at].at[t],
                give_send.at[slot],
                take_recv.at[at, t],
                fr=partner,
            )

        def consume(t):
            slot = lax.rem(t + base, 2)
            outgoing(t).wait_recv()
            for there in range(chips):
                held[at][t, there] = (
                    held[at][t, there].astype(F32) + made[slot, core, there, 0:rows].astype(F32)
                ).astype(BF16)
            pltpu.make_async_copy(
                held[at].at[t, chip], kept_out[at].at[:, columns_of(t)], kept_sem.at[at]
            ).start()
            for k in range(1, chips):
                there = lax.rem(chip + k, chips)
                send(
                    held[at].at[t, there],
                    come_out[at].at[k - 1, :, columns_of(t)],
                    far_send.at[at, k],
                    far_recv.at[at, k],
                    fr=there * 2 + core,
                ).start()

        def step(t, carry):
            slot = lax.rem(t + base, 2)

            @pl.when(t >= 2)
            def _():
                outgoing(t - 2).wait_send()

            for first in range(0, n_fr, group):
                last = min(first + group, n_fr)
                grads = product(left_t[first * rows : last * rows], right[:, columns_of(t)])
                for b in range(first, last):
                    made[slot, b % 2, b // 2, 0:rows] = grads[
                        (b - first) * rows : (b - first + 1) * rows
                    ].astype(BF16)
            outgoing(t).start()

            @pl.when(t >= 1)
            def _():
                consume(t - 1)

            return carry

        settle()
        lax.fori_loop(0, tiles, step, 0)

        def finish():
            consume(tiles - 1)
            outgoing(tiles - 2).wait_send()
            outgoing(tiles - 1).wait_send()

        pending.append(finish)

    loads["inner"].wait()
    loads["cot"].wait()
    reduce_weight(6, inner_v, cot_v)

    loads["gate"].wait()
    loads["up"].wait()
    feed_tiles = gate_v.shape[1] // tile
    total[...] = jnp.zeros_like(total)

    def feed(t, carry):
        slot = lax.rem(t, 2)

        @pl.when(t + 1 < feed_tiles)
        def _():
            for copy in feed_copies(t + 1):
                copy.start()

        for copy in feed_copies(t):
            copy.wait()
        columns = columns_of(t)
        grad_inner = back_product(cot_v[...], down_slots[slot])
        gate = gate_v[:, columns].astype(F32)
        sigmoid = jax.nn.sigmoid(gate)
        scaled = grad_inner * sigmoid
        gate_v[:, columns] = (
            scaled * up_v[:, columns].astype(F32) * (1.0 + gate * (1.0 - sigmoid))
        ).astype(BF16)
        up_v[:, columns] = (scaled * gate).astype(BF16)
        for at in range(features // tile):
            rows = slice(at * tile, (at + 1) * tile)
            total[:, rows] += back_product(
                gate_v[:, columns], gate_slots[slot, rows, :]
            ) + back_product(up_v[:, columns], up_slots[slot, rows, :])
        return carry

    lax.fori_loop(0, feed_tiles, feed, 0)
    settle()

    block = 64
    blocks = frames // block
    loads["branch"].wait()

    def block_rows(at):
        return pl.ds(pl.multiple_of(at * block, block), block)

    def feed_norm(at, carry):
        rows = block_rows(at)
        here = branch[rows, :]
        grads = total[rows, :]
        scaling = rms_scaling(here)
        weighted = gain_rows[1:2, :] * grads
        back = scaling * weighted - here * scaling**3 * jnp.mean(weighted * here, -1, keepdims=True)
        back = cot_v[rows, :].astype(F32) + back
        branch[rows, :] = back
        low_rows[rows, :] = back.astype(BF16)
        return carry + sublane_sums(grads * here * scaling)

    feed_gain = lax.fori_loop(0, blocks, feed_norm, jnp.zeros((8, features), F32))
    feed_gain = jnp.sum(feed_gain, 0, keepdims=True)

    loads["out"].wait()

    def turn_back(t, carry):
        columns = columns_of(t)
        grad_rows[:, columns] = back_product(low_rows[...], small[0, columns, :]).astype(BF16)
        return carry

    lax.fori_loop(0, features // tile, turn_back, 0)

    def turn(k):
        peer = peer_of(pos, k, n_pos)
        return send(
            grad_rows.at[rows_of(peer, part)],
            turned.at[3, pos],
            turn_send.at[k],
            turn_recv.at[k],
            pos=peer,
        )

    def start_turn(k, carry):
        turn(k).start()
        return carry

    lax.fori_loop(1, n_pos, start_turn, 0)
    turned[3, pl.ds(pos, 1)] = grad_rows[rows_of(pos, part), :][None]
    load("query_w", query_w, small.at[0])

    loads["normed_two"].wait()
    reduce_weight(4, normed_two_v, gate_v)
    reduce_weight(5, normed_two_v, up_v)
    loads["attended"].wait()
    reduce_weight(3, attended_v, low_rows)

    for name in ("queries", "keys", "values", "soft"):
        loads[name].wait()

    def end_turn(k, carry):
        turn(k).wait()
        return carry

    lax.fori_loop(1, n_pos, end_turn, 0)
    settle()

    def give_back(which, j):
        return send(
            leaving.at[which, j],
            arrived.at[which, rows_of(pos, part)],
            back_send.at[which, j],
            back_recv.at[which, pos],
            pos=j,
        )

    def part_sum(which, j, low, high, weight_of, other, scale):
        sum_rows[...] = jnp.zeros_like(sum_rows)

        def add(at, carry):
            sum_rows[...] += product(weight_of(at), spread[...]) * turned[other, at].astype(F32)
            return carry

        lax.fori_loop(low, high, add, 0)
        leaving[which, j] = (sum_rows[...] * scale).astype(BF16)

        @pl.when(j != pos)
        def _():
            give_back(which, j).start()

        @pl.when(j == pos)
        def _():
            arrived[which, rows_of(pos, part), :] = leaving[which, j]

    def value_part(k, carry):
        j = peer_of(pos, k, n_pos)
        part_sum(2, j, j, n_pos, lambda p: soft[p, j].astype(BF16), 3, 1.0)
        return carry

    lax.fori_loop(1, n_pos + 1, value_part, 0)

    def score_part(p, carry):
        grads = turned[3, p].astype(F32)

        def score(j, centre):
            scores = sum_heads(grads * turned[2, j].astype(F32), sums[...])
            score_slots[j] = scores
            return centre + scores * soft[p, j]

        centre = lax.fori_loop(0, p + 1, score, jnp.zeros((part, LANES), F32))

        def level(j, carry):
            soft_grads[p, j] = (soft[p, j] * (score_slots[j] - centre)).astype(BF16)
            return carry

        return lax.fori_loop(0, p + 1, level, carry)

    lax.fori_loop(0, n_pos, score_part, 0)

    def key_part(k, carry):
        j = peer_of(pos, k, n_pos)
        part_sum(1, j, j, n_pos, lambda p: soft_grads[p, j], 0, HEAD ** (-0.5))
        return carry

    lax.fori_loop(1, n_pos + 1, key_part, 0)

    def query_part(k, carry):
        p = peer_of(pos, k, n_pos)
        part_sum(0, p, 0, p + 1, lambda j: soft_grads[p, j], 1, HEAD ** (-0.5))
        return carry

    lax.fori_loop(1, n_pos + 1, query_part, 0)

    loads["normed"].wait()
    for which, slot, name in ((2, 1, "value_w"), (1, 2, "key_w"), (0, 0, "query_w")):

        def end_back(k, carry):
            peer = peer_of(pos, k, n_pos)
            send(
                leaving.at[which, peer],
                arrived.at[which, rows_of(peer, part)],
                back_send.at[which, peer],
                back_recv.at[which, peer],
                pos=peer,
            ).wait()
            return carry

        lax.fori_loop(1, n_pos, end_back, 0)
        reduce_weight(which, normed_v, arrived.at[which])
        loads[name].wait()

        def add_normed(t, carry):
            columns = columns_of(t)
            grads = back_product(arrived[which], small[slot, columns, :])
            total[:, columns] = grads if which == 2 else total[:, columns] + grads
            return carry

        lax.fori_loop(0, features // tile, add_normed, 0)

    loads["hidden"].wait()

    def attention_norm(at, carry):
        rows = block_rows(at)
        here = hidden[rows, :].astype(F32)
        grads = total[rows, :]
        scaling = rms_scaling(here)
        weighted = gain_rows[0:1, :] * grads
        back = scaling * weighted - here * scaling**3 * jnp.mean(weighted * here, -1, keepdims=True)
        branch[rows, :] = branch[rows, :] + back
        return carry + sublane_sums(grads * here * scaling)

    gain = lax.fori_loop(0, blocks, attention_norm, jnp.zeros((8, features), F32))
    gain = jnp.sum(gain, 0, keepdims=True)

    first_lags = lags[0:8, :]
    once = jnp.where(first_lags == 1, branch[0:8, :], 0.0)
    once = jnp.where(
        lax.broadcasted_iota(jnp.int32, once.shape, 0) == 0, 0.0, pltpu.roll(once, 1, 0)
    )
    rim_out[...] = once + jnp.where(first_lags == 2, branch[0:8, :], 0.0)
    rim_copy = send(
        rim_out, rim_in, rim_sem.at[0], rim_sem.at[1], fr=lax.rem(fr + n_fr - 1, n_fr)
    )
    rim_copy.start()
    gain_pair = jnp.concatenate([gain, feed_gain, jnp.zeros((6, features), F32)], 0)
    width = features // n_fr
    for b in range(n_fr):
        gain_split[b] = gain_pair[:, b * width : (b + 1) * width]
    gain_copies = []
    for k in range(1, n_fr):
        there = lax.rem(fr + k, n_fr)
        copy = send(
            gain_split.at[there], gain_in.at[fr], gain_send.at[k], gain_recv.at[k], fr=there
        )
        copy.start()
        gain_copies.append(copy)
    gain_in[pl.ds(fr, 1)] = gain_split[pl.ds(fr, 1)]
    settle()

    rim_copy.wait()
    rim = jnp.where(fr == n_fr - 1, 0.0, rim_in[...])

    def shift(at, carry):
        after_one, after_two = carry
        rows = block_rows(blocks - 1 - at)
        grads = branch[rows, :]
        lag = lags[rows, :]
        one = jnp.where(lag == 1, grads, 0.0)
        two = jnp.where(lag == 2, grads, 0.0)
        moved = pltpu.roll(jnp.concatenate([one, after_one], 0), block + 7, 0)[:block]
        moved = moved + pltpu.roll(jnp.concatenate([two, after_two], 0), block + 6, 0)[:block]
        low_rows[rows, :] = (jnp.where(lag == 0, grads, 0.0) + moved).astype(BF16)
        return one[:8], two[:8]

    lax.fori_loop(0, blocks, shift, (jnp.zeros_like(rim), rim))
    out_copy = pltpu.make_async_copy(low_rows, input_grad, out_sem.at[0])
    out_copy.start()
    for copy in gain_copies:
        copy.wait()
    gain_sum = gain_in[0]
    for b in range(1, n_fr):
        gain_sum = gain_sum + gain_in[b]
    gains_out[...] = gain_sum

    for at in range(7):
        pltpu.make_async_copy(kept_out[at], kept_out[at], kept_sem.at[at]).wait()
        for k in range(1, chips):
            there = lax.rem(chip + k, chips)
            send(
                come_out[at].at[k - 1],
                come_out[at].at[k - 1],
                far_send.at[at, k],
                far_recv.at[at, k],
                fr=there * 2 + core,
            ).wait()
    out_copy.wait()


def backward_call(n_fr, n_pos, shard_shapes, *operands):
    cot = operands[3]
    frames, features = cot.shape
    part = frames // n_pos
    chips = n_fr // 2
    tile = column_tile(features)
    count = len(shard_shapes)
    shard_rows = [rows for rows, _ in shard_shapes]
    hidden_units = operands[4].shape[1]
    most = max(shard_rows)
    return pl.pallas_call(
        functools.partial(backward_kernel, n_fr, n_pos, shard_rows),
        name="backward",
        out_shape=[jax.ShapeDtypeStruct(shape, BF16) for shape in shard_shapes]
        + [jax.ShapeDtypeStruct((chips - 1, *shape), BF16) for shape in shard_shapes]
        + [
            jax.ShapeDtypeStruct((frames, features), BF16),
            jax.ShapeDtypeStruct((8, features // n_fr), F32),
        ],
        in_specs=[VMEM, VMEM] + [ANY] * (len(operands) - 2),
        out_specs=[ANY] * (2 * count + 1) + [VMEM],
        scratch_shapes=[
            pltpu.VMEM((columns // tile, chips, rows, tile), BF16) for rows, columns in shard_shapes
        ]
        + [
            pltpu.VMEM((2, 2, chips, most, tile), BF16),
            pltpu.VMEM((2, tile, features), BF16),
            pltpu.VMEM((2, features, tile), BF16),
            pltpu.VMEM((2, features, tile), BF16),
            pltpu.VMEM((3, features, features), BF16),
            pltpu.VMEM((hidden_units, frames), BF16),
            pltpu.VMEM((frames, features), BF16),
            pltpu.VMEM((frames, hidden_units), BF16),
            pltpu.VMEM((frames, hidden_units), BF16),
            pltpu.VMEM((features, frames), BF16),
            pltpu.VMEM((features, frames), BF16),
            pltpu.VMEM((features, frames), BF16),
            pltpu.VMEM((frames, features), F32),
            pltpu.VMEM((frames, features), BF16),
            pltpu.VMEM((frames, features), F32),
            pltpu.VMEM((frames, features), BF16),
            pltpu.VMEM((frames, features), BF16),
            pltpu.VMEM((4, n_pos, part, features), BF16),
            pltpu.VMEM((n_pos, n_pos, part, LANES), F32),
            pltpu.VMEM((n_pos, n_pos, part, LANES), BF16),
            pltpu.VMEM((n_pos, part, LANES), F32),
            pltpu.VMEM((part, features), F32),
            pltpu.VMEM((3, n_pos, part, features), BF16),
            pltpu.VMEM((3, frames, features), BF16),
            pltpu.VMEM((features, LANES), BF16),
            pltpu.VMEM((LANES, features), BF16),
            pltpu.VMEM((n_fr, 8, features // n_fr), F32),
            pltpu.VMEM((n_fr, 8, features // n_fr), F32),
            pltpu.VMEM((8, features), F32),
            pltpu.VMEM((8, features), F32),
            DMA((17,)),
            DMA((2, 3)),
            DMA((2,)),
            DMA((count, max(columns for _, columns in shard_shapes) // tile)),
            DMA((count, chips)),
            DMA((count, chips)),
            DMA((count,)),
            DMA((n_pos,)),
            DMA((n_pos,)),
            DMA((3, n_pos)),
            DMA((3, n_pos)),
            DMA((n_fr,)),
            DMA((n_fr,)),
            DMA((2,)),
            DMA((1,)),
        ],
        compiler_params=pltpu.CompilerParams(
            collective_id=1, has_side_effects=True, vmem_limit_bytes=VMEM_BYTES
        ),
    )(*operands)


def on_device(
    inputs,
    delays,
    query_weight,
    key_weight,
    value_weight,
    out_weight,
    gate_weight,
    up_weight,
    down_weight,
    attention_gain,
    feed_gain,
    cotangent,
):
    n_fr = lax.axis_size("fr")
    n_pos = lax.axis_size("pos")
    own_rows = inputs[0]
    frames, features = own_rows.shape
    lags = jnp.repeat(delays[:, 0], frames // delays.shape[0])[:, None]
    gains = jnp.pad(jnp.concatenate([attention_gain, feed_gain], 0).astype(F32), ((0, 6), (0, 0)))
    shards = [
        weight[0]
        for weight in (
            query_weight,
            key_weight,
            value_weight,
            out_weight,
            gate_weight,
            up_weight,
            down_weight,
        )
    ]
    results = forward_call(n_fr, n_pos, own_rows, lags, gains, shards)
    full, output, saved, gain_rows = results[:7], results[7], results[8:20], results[20]
    inner_t, *saved = saved
    grads = backward_call(
        n_fr,
        n_pos,
        [shard.shape for shard in shards],
        lags,
        gain_rows,
        inner_t,
        cotangent[0],
        *saved,
        *full,
    )
    kept, come, (input_grad, gain_grads) = grads[:7], grads[7:14], grads[14:]
    return (
        output[None],
        input_grad[None],
        *(
            (own.astype(F32) + jnp.sum(others.astype(F32), 0))[None]
            for own, others in zip(kept, come)
        ),
        gain_grads[0:1],
        gain_grads[1:2],
    )


def solution(mesh):
    matrix = P("pos", "fr", None)
    vector = P("pos", "fr")
    return jax.shard_map(
        on_device,
        mesh=mesh,
        in_specs=(matrix, P("fr", "pos")) + (matrix,) * 7 + (vector, vector, matrix),
        out_specs=(matrix,) * 9 + (vector, vector),
        check_vma=False,
    )
```

```python
import functools

import jax
import jax.numpy as jnp
from jax import lax
from jax.experimental import pallas as pl
from jax.experimental.pallas import tpu as pltpu
from jax.sharding import PartitionSpec as P

HEAD = 64
LANES = 128
EPSILON = 1e-06
LATE = 37
TERMS_HELD = 2750000
MESH = pl.DeviceIdType.MESH
F32 = jnp.float32
BF16 = jnp.bfloat16
ANY = pl.BlockSpec(memory_space=pl.ANY)
VMEM = pl.BlockSpec(memory_space=pltpu.VMEM)
DMA = pltpu.SemaphoreType.DMA
VMEM_BYTES = 64 * 1024 * 1024 - 65536


def greet(n_fr, n_pos):
    fr = lax.axis_index("fr")
    pos = lax.axis_index("pos")
    barrier = pltpu.get_barrier_semaphore()
    for k in range(1, n_fr):
        pl.semaphore_signal(
            barrier, inc=1, device_id={"fr": lax.rem(fr + k, n_fr)}, device_id_type=MESH
        )
    for k in range(1, n_pos):
        pl.semaphore_signal(
            barrier, inc=1, device_id={"pos": lax.rem(pos + k, n_pos)}, device_id_type=MESH
        )
    pl.semaphore_wait(barrier, n_fr + n_pos - 2)


def send(src, dst, send_sem, recv_sem, **device):
    return pltpu.make_async_remote_copy(
        src_ref=src,
        dst_ref=dst,
        send_sem=send_sem,
        recv_sem=recv_sem,
        device_id=device,
        device_id_type=MESH,
    )


def rows_of(index, rows):
    return pl.ds(pl.multiple_of(index * rows, rows), rows)


def lag_of(delays, at):
    here = lax.broadcasted_iota(jnp.int32, delays.shape, 1) == at
    return jnp.sum(jnp.where(here, delays[...].astype(F32), 0.0), 1, keepdims=True)


def head_sums(shape, feature_dim):
    features = lax.broadcasted_iota(jnp.int32, shape, feature_dim)
    heads = lax.broadcasted_iota(jnp.int32, shape, 1 - feature_dim)
    return (features // HEAD == heads).astype(BF16)


def sum_heads(product, sums):
    high = product.astype(BF16)
    low = (product - high.astype(F32)).astype(BF16)
    return jnp.dot(high, sums, preferred_element_type=F32) + jnp.dot(
        low, sums, preferred_element_type=F32
    )


def rms_scaling(values):
    return lax.rsqrt(jnp.mean(values * values, -1, keepdims=True) + EPSILON)


def product(operand, weight):
    return jnp.dot(operand, weight, preferred_element_type=F32)


def column_tile(columns):
    return 256 if columns % 256 == 0 else LANES


def multiply(rows_ref, weight_ref, out_ref):
    tile = column_tile(weight_ref.shape[1])

    def step(at, carry):
        columns = pl.ds(pl.multiple_of(at * tile, tile), tile)
        out_ref[:, columns] = jnp.dot(
            rows_ref[...], weight_ref[:, columns], preferred_element_type=F32
        ).astype(out_ref.dtype)
        return carry

    lax.fori_loop(0, weight_ref.shape[1] // tile, step, 0)


def peer_of(pos, k, n_pos):
    return lax.rem(pos + k, n_pos)


def forward_kernel(n_fr, n_pos, pieces, late, steps, *refs):
    (
        own_rows,
        delays,
        gain_one,
        gain_two,
        w0,
        w1,
        w2,
        w3,
        w4,
        w5,
        w6,
        o0,
        o1,
        o2,
        o3,
        o4,
        o5,
        o6,
        inner_out,
        inner_rows_out,
        gate_out,
        up_out,
        normed_two_out,
        attended_out,
        normed_out,
        branch_out,
        hidden_out,
        queries_out,
        keys_out,
        values_out,
        soft_out,
        gains_out,
        f0,
        f1,
        f2,
        f3,
        f4,
        f5,
        f6,
        rim,
        gains,
        gain_slots,
        hidden,
        normed,
        proj,
        turned,
        mixed,
        attended,
        normed_t,
        attended_t,
        normed_two_t,
        normed_two,
        inner,
        inner_t,
        gate_low,
        up_low,
        branch,
        score_slots,
        soft_slots,
        total,
        sums,
        spread,
        far_send,
        far_recv,
        near_send,
        near_recv,
        own_sem,
        out_sem,
        rim_sem,
        gain_send,
        gain_recv,
        turn_send,
        turn_recv,
        back_send,
        back_recv,
        act_sem,
    ) = refs
    shards = (w0, w1, w2, w3, w4, w5, w6)
    full_out = (o0, o1, o2, o3, o4, o5, o6)
    full = (f0, f1, f2, f3, f4, f5, f6)
    turned_out = (queries_out, keys_out, values_out)
    fr = lax.axis_index("fr")
    pos = lax.axis_index("pos")
    chips = n_fr // 2
    chip = fr // 2
    core = lax.rem(fr, 2)
    partner = chip * 2 + 1 - core
    frames, features = own_rows.shape
    part = frames // n_pos
    greet(n_fr, n_pos)

    edge = own_rows.shape[0] - rim.shape[0]
    rim_copy = send(
        own_rows.at[pl.ds(edge, rim.shape[0])],
        rim,
        rim_sem.at[0],
        rim_sem.at[1],
        fr=lax.rem(fr + 1, n_fr),
    )
    rim_copy.start()
    gains[...] = jnp.concatenate(
        [
            gain_one[...].astype(F32),
            gain_two[...].astype(F32),
            jnp.zeros((6, gains.shape[1]), F32),
        ],
        0,
    )
    gain_copies = []
    for k in range(1, n_fr):
        copy = send(
            gains,
            gain_slots.at[fr],
            gain_send.at[k],
            gain_recv.at[k],
            fr=lax.rem(fr + k, n_fr),
        )
        copy.start()
        gain_copies.append(copy)
    far = {}
    near = {}
    own = {}
    def piece_rows(at, origin, piece):
        rows = shards[at].shape[0]
        size = rows // pieces[at]
        return pl.ds(pl.multiple_of(origin * rows + piece * size, size), size)

    tile = column_tile(features)
    tiles = features // tile
    spare = sum(steps) * (chips - 1)

    def slot(at, k, piece):
        return (sum(steps[:at]) + piece) * (chips - 1) + k - 1


    def columns_of(t):
        return pl.ds(pl.multiple_of(t * tile, tile), tile)

    for t in range(tiles):
        for k in range(1, chips):
            far[0, k, t] = send(
                w0.at[:, columns_of(t)],
                f0.at[rows_of(fr, w0.shape[0]), columns_of(t)],
                far_send.at[slot(0, k, t)],
                far_recv.at[slot(0, k, t)],
                fr=lax.rem(chip + k, chips) * 2 + core,
            )
            far[0, k, t].start()
    up_tiles = w5.shape[1] // tile

    def up_far(t, k):
        return send(
            w5.at[:, columns_of(t)],
            f5.at[rows_of(fr, w5.shape[0]), columns_of(t)],
            far_send.at[slot(5, k, t)],
            far_recv.at[slot(5, k, t)],
            fr=lax.rem(chip + k, chips) * 2 + core,
        )

    def up_near(t, k):
        there = f5.at[
            rows_of(lax.rem(chip - k + chips, chips) * 2 + core, w5.shape[0]), columns_of(t)
        ]
        return send(there, there, near_send.at[slot(5, k, t)], near_recv.at[slot(5, k, t)], fr=partner)

    def up_start(t, carry):
        for k in range(1, chips):
            up_far(t, k).start()
        return carry

    for at, (shard, whole) in enumerate(zip(shards, full)):
        if at == 5:
            lax.fori_loop(0, up_tiles, up_start, 0)
        mine = rows_of(fr, shard.shape[0])
        size = shard.shape[0] // pieces[at]
        for piece in range(0 if at in (0, 5) else pieces[at] - late[at]):
            for k in range(1, chips):
                far[at, k, piece] = send(
                    shard.at[piece * size : (piece + 1) * size],
                    whole.at[piece_rows(at, fr, piece)],
                    far_send.at[slot(at, k, piece)],
                    far_recv.at[slot(at, k, piece)],
                    fr=lax.rem(chip + k, chips) * 2 + core,
                )
                far[at, k, piece].start()
        near[at, 0, 0] = send(
            shard, whole.at[mine], near_send.at[spare + at], near_recv.at[spare + at], fr=partner
        )
        if at < 3:
            near[at, 0, 0].start()
        own[at] = pltpu.make_async_copy(shard, whole.at[mine], own_sem.at[at])
        own[at].start()

    sums[...] = head_sums(sums.shape, 0)
    spread[...] = head_sums(spread.shape, 1)
    gain_slots[pl.ds(fr, 1)] = gains[...][None]
    for copy in gain_copies:
        copy.wait()
    gain_row = jnp.concatenate([gain_slots[at, 0:1, :] for at in range(n_fr)], 1)
    gains_out[...] = jnp.concatenate([gain_slots[at] for at in range(n_fr)], 1)
    rim_copy.wait()

    block = frames // delays.shape[1]
    rim_rows = rim.shape[0]
    rim_all = jnp.where(fr == 0, 0.0, rim[...].astype(F32))[rim_rows - 8 :]

    def norm_block(at, carry):
        rows = pl.ds(pl.multiple_of(at * block, block), block)
        here = own_rows[rows, :].astype(F32)
        window = jnp.concatenate([carry, here], 0)
        once = pltpu.roll(window, 1, 0)[8:]
        twice = pltpu.roll(window, 2, 0)[8:]
        lag = lag_of(delays, at)
        values = jnp.where(lag == 0, here, jnp.where(lag == 1, once, twice))
        hidden[rows, :] = values.astype(BF16)
        scaling = lax.rsqrt(jnp.mean(values * values, -1, keepdims=True) + EPSILON)
        normed[rows, :] = (values * scaling * gain_row).astype(BF16)
        return here[block - 8 :]

    lax.fori_loop(0, frames // block, norm_block, rim_all)
    act_copies = []

    def put(src, dst):
        act_copies.append(pltpu.make_async_copy(src, dst, act_sem.at[len(act_copies)]))
        act_copies[-1].start()

    put(hidden, hidden_out)

    outs = {}

    def pass_on(at, piece=0):
        for k in range(1, chips):
            far[at, k, piece].wait_recv()
            origin = lax.rem(chip - k + chips, chips) * 2 + core
            rows = piece_rows(at, origin, piece)
            near[at, k, piece] = send(
                full[at].at[rows],
                full[at].at[rows],
                near_send.at[slot(at, k, piece)],
                near_recv.at[slot(at, k, piece)],
                fr=partner,
            )
            near[at, k, piece].start()

    def complete(at):
        own[at].wait()
        for k in range(chips):
            near[at, k, 0].wait_recv()
        outs[at] = pltpu.make_async_copy(full[at], full_out[at], out_sem.at[at])
        outs[at].start()

    def finish_pieces(at):
        early = range(pieces[at] - late[at])
        rows = shards[at].shape[0]
        size = rows // pieces[at]

        def put_rows(where):
            pltpu.make_async_copy(
                full[at].at[where], full_out[at].at[where], out_sem.at[at]
            ).start()

        own[at].wait()
        put_rows(rows_of(fr, rows))
        near[at, 0, 0].wait_recv()
        put_rows(rows_of(partner, rows))
        for piece in early:
            pass_on(at, piece)
            for k in range(1, chips):
                put_rows(piece_rows(at, lax.rem(chip - k + chips, chips) * 2 + core, piece))
        for piece in early:
            for k in range(1, chips):
                near[at, k, piece].wait_recv()
                put_rows(piece_rows(at, lax.rem(chip - k + chips, chips) * 2 + 1 - core, piece))
        written = full_out[at].at[0 : n_fr * rows - 2 * (chips - 1) * late[at] * size]
        outs[at] = pltpu.make_async_copy(written, written, out_sem.at[at])

    def turn(which, k):
        peer = peer_of(pos, k, n_pos)
        return send(
            proj.at[which, rows_of(peer, part)],
            turned.at[which, pos],
            turn_send.at[which, k],
            turn_recv.at[which, k],
            pos=peer,
        )

    own[0].wait()
    near[0, 0, 0].wait_recv()
    for t in range(tiles):
        for k in range(1, chips):
            far[0, k, t].wait_recv()
            origin = lax.rem(chip - k + chips, chips) * 2 + core
            there = f0.at[rows_of(origin, w0.shape[0]), columns_of(t)]
            near[0, k, t] = send(
                there, there, near_send.at[slot(0, k, t)], near_recv.at[slot(0, k, t)], fr=partner
            )
            near[0, k, t].start()
        for k in range(1, chips):
            near[0, k, t].wait_recv()
        proj[0, :, columns_of(t)] = product(normed[...], f0[:, columns_of(t)]).astype(BF16)

        def start_tile(k, carry):
            peer = peer_of(pos, k, n_pos)
            send(
                proj.at[0, rows_of(peer, part), columns_of(t)],
                turned.at[0, pos, :, columns_of(t)],
                turn_send.at[0, k],
                turn_recv.at[0, k],
                pos=peer,
            ).start()
            return carry

        lax.fori_loop(1, n_pos, start_tile, 0)
    turned[0, pl.ds(pos, 1)] = proj[0, rows_of(pos, part), :][None]
    outs[0] = pltpu.make_async_copy(f0, o0, out_sem.at[0])
    outs[0].start()
    for which in (1, 2):
        pass_on(which)
        complete(which)
        multiply(normed, full[which], proj.at[which])

        def start_turn(k, carry):
            turn(which, k).start()
            return carry

        lax.fori_loop(1, n_pos, start_turn, 0)
        turned[which, pl.ds(pos, 1)] = proj[which, rows_of(pos, part), :][None]

    for at in range(3, 7):
        near[at, 0, 0].start()

    def transpose(src, dst):
        tile = column_tile(src.shape[1])

        def step(t, carry):
            at = pl.ds(pl.multiple_of(t * tile, tile), tile)
            dst[at, :] = src[:, at].T
            return carry

        lax.fori_loop(0, src.shape[1] // tile, step, 0)

    transpose(normed, normed_t)
    put(normed_t, normed_out)
    pass_on(3)

    def end_turns(which):
        def end_turn(k, carry):
            turn(which, k).wait()
            return carry

        lax.fori_loop(1, n_pos, end_turn, 0)
        put(turned.at[which], turned_out[which])

    end_turns(0)
    end_turns(1)

    def score_rows(p, carry):
        query = turned[0, p].astype(F32) * HEAD ** (-0.5)

        def score(j, highest):
            scores = sum_heads(query * turned[1, j].astype(F32), sums[...])
            score_slots[j] = scores
            return jnp.maximum(highest, scores)

        highest = lax.fori_loop(0, p + 1, score, jnp.full((part, LANES), -1e30, F32))

        def weigh(j, mass):
            return mass + jnp.exp(score_slots[j] - highest)

        mass = lax.fori_loop(0, p + 1, weigh, jnp.zeros((part, LANES), F32))
        logsum = highest + jnp.log(mass)

        def level(j, carry):
            soft_slots[p, j] = jnp.exp(score_slots[j] - logsum)
            return carry

        return lax.fori_loop(0, p + 1, level, carry)

    lax.fori_loop(0, n_pos, score_rows, 0)
    put(soft_slots, soft_out)
    pass_on(4)
    end_turns(2)

    def back(p):
        return send(
            mixed.at[p],
            attended.at[rows_of(pos, part)],
            back_send.at[p],
            back_recv.at[pos],
            pos=p,
        )

    def mix_rows(k, carry):
        p = peer_of(pos, k, n_pos)
        total[...] = jnp.zeros_like(total)

        def mix(j, carry):
            total[...] += product(soft_slots[p, j].astype(BF16), spread[...]) * turned[
                2, j
            ].astype(F32)
            return carry

        lax.fori_loop(0, p + 1, mix, 0)
        mixed[p] = total[...].astype(BF16)

        @pl.when(p != pos)
        def _():
            back(p).start()

        @pl.when(p == pos)
        def _():
            attended[rows_of(pos, part), :] = mixed[p]

        return carry

    lax.fori_loop(1, n_pos + 1, mix_rows, 0)
    complete(3)
    complete(4)

    def end_back(k, carry):
        peer = peer_of(pos, k, n_pos)
        send(
            mixed.at[peer],
            attended.at[rows_of(peer, part)],
            back_send.at[peer],
            back_recv.at[peer],
            pos=peer,
        ).wait()
        return carry

    lax.fori_loop(1, n_pos, end_back, 0)
    def leave(t, carry):
        columns = columns_of(t)
        branch[:, columns] = hidden[:, columns].astype(F32) + product(
            attended[...], full[3][:, columns]
        )
        return carry

    lax.fori_loop(0, features // tile, leave, 0)
    put(branch, branch_out)
    feed_gain = gains_out[1:2, :]

    def norm_two(at, carry):
        rows = pl.ds(pl.multiple_of(at * block, block), block)
        here = branch[rows, :]
        normed_two[rows, :] = (here * rms_scaling(here) * feed_gain).astype(BF16)
        return carry

    lax.fori_loop(0, frames // block, norm_two, 0)

    transpose(attended, attended_t)
    put(attended_t, attended_out)
    transpose(normed_two, normed_two_t)
    put(normed_two_t, normed_two_out)

    def up_pass(t):
        for k in range(1, chips):
            up_far(t, k).wait_recv()
            up_near(t, k).start()

    def up_put(t):
        return pltpu.make_async_copy(
            f5.at[:, columns_of(t)], o5.at[:, columns_of(t)], out_sem.at[5]
        )

    own[5].wait()
    near[5, 0, 0].wait_recv()
    up_pass(0)

    def feed(t, carry):
        columns = columns_of(t)

        @pl.when(t + 1 < up_tiles)
        def _():
            up_pass(t + 1)

        for k in range(1, chips):
            up_near(t, k).wait_recv()
        up_put(t).start()
        gate = product(normed_two[...], full[4][:, columns])
        up = product(normed_two[...], full[5][:, columns])
        gate_low[:, columns] = gate.astype(BF16)
        up_low[:, columns] = up.astype(BF16)
        low = (gate * jax.nn.sigmoid(gate) * up).astype(BF16)
        inner[:, columns] = low
        inner_t[columns, :] = low.T
        return carry

    lax.fori_loop(0, inner.shape[1] // tile, feed, 0)
    put(gate_low, gate_out)
    put(up_low, up_out)
    put(inner_t, inner_out)
    put(inner, inner_rows_out)
    finish_pieces(6)

    def up_sent(t, carry):
        for k in range(1, chips):
            up_far(t, k).wait_send()
            up_near(t, k).wait_send()
        return carry

    lax.fori_loop(0, up_tiles, up_sent, 0)
    pltpu.make_async_copy(o5, o5, out_sem.at[5]).wait()
    for copy in far.values():
        copy.wait_send()
    for copy in near.values():
        copy.wait_send()
    for copy in outs.values():
        copy.wait()
    for copy in act_copies:
        copy.wait()


def down_pieces(rows):
    return next(cuts for cuts in (11, 8, 4, 2, 1) if rows % (16 * cuts) == 0)


def forward_call(n_fr, n_pos, own_rows, delays, gain_one, gain_two, shards):
    frames, features = own_rows.shape
    part = frames // n_pos
    count = len(shards)
    chips = n_fr // 2
    width = gain_one.shape[1]
    last = down_pieces(shards[-1].shape[0])
    pieces = [1] * (count - 1) + [last]
    late = [0] * (count - 1) + [last * LATE // 100]
    tile = column_tile(features)
    steps = [1] * (count - 1) + [last - late[-1]]
    steps[0] = features // tile
    steps[5] = shards[5].shape[1] // tile
    copies = sum(steps) * (chips - 1)
    full = [(n_fr * shard.shape[0], shard.shape[1]) for shard in shards]
    hidden_units = shards[4].shape[1]
    act = jax.ShapeDtypeStruct((frames, features), BF16)
    act_t = jax.ShapeDtypeStruct((features, frames), BF16)
    wide = jax.ShapeDtypeStruct((frames, hidden_units), BF16)
    wide_t = jax.ShapeDtypeStruct((hidden_units, frames), BF16)
    turned = jax.ShapeDtypeStruct((n_pos, part, features), BF16)
    return pl.pallas_call(
        functools.partial(forward_kernel, n_fr, n_pos, pieces, late, steps),
        name="forward",
        out_shape=[jax.ShapeDtypeStruct(shape, BF16) for shape in full]
        + [wide_t, wide, wide, wide, act_t, act_t, act_t]
        + [jax.ShapeDtypeStruct((frames, features), F32), act, turned, turned, turned]
        + [
            jax.ShapeDtypeStruct((n_pos, n_pos, part, LANES), F32),
            jax.ShapeDtypeStruct((8, features), F32),
        ],
        in_specs=[VMEM] * 4 + [ANY] * count,
        out_specs=[ANY] * (count + 13) + [VMEM],
        scratch_shapes=[pltpu.VMEM(shape, BF16) for shape in full]
        + [
            pltpu.VMEM((16, features), BF16),
            pltpu.VMEM((8, width), F32),
            pltpu.VMEM((n_fr, 8, width), F32),
            pltpu.VMEM((frames, features), BF16),
            pltpu.VMEM((frames, features), BF16),
            pltpu.VMEM((3, frames, features), BF16),
            pltpu.VMEM((3, n_pos, part, features), BF16),
            pltpu.VMEM((n_pos, part, features), BF16),
            pltpu.VMEM((frames, features), BF16),
            pltpu.VMEM((features, frames), BF16),
            pltpu.VMEM((features, frames), BF16),
            pltpu.VMEM((features, frames), BF16),
            pltpu.VMEM((frames, features), BF16),
            pltpu.VMEM((frames, hidden_units), BF16),
            pltpu.VMEM((hidden_units, frames), BF16),
            pltpu.VMEM((frames, hidden_units), BF16),
            pltpu.VMEM((frames, hidden_units), BF16),
            pltpu.VMEM((frames, features), F32),
            pltpu.VMEM((n_pos, part, LANES), F32),
            pltpu.VMEM((n_pos, n_pos, part, LANES), F32),
            pltpu.VMEM((part, features), F32),
            pltpu.VMEM((features, LANES), BF16),
            pltpu.VMEM((LANES, features), BF16),
            DMA((copies,)),
            DMA((copies,)),
            DMA((copies + count,)),
            DMA((copies + count,)),
            DMA((count,)),
            DMA((count,)),
            DMA((2,)),
            DMA((n_fr,)),
            DMA((n_fr,)),
            DMA((3, n_pos)),
            DMA((3, n_pos)),
            DMA((n_pos,)),
            DMA((n_pos,)),
            DMA((14,)),
        ],
        compiler_params=pltpu.CompilerParams(
            collective_id=0, has_side_effects=True, vmem_limit_bytes=VMEM_BYTES
        ),
    )(own_rows, delays, gain_one, gain_two, *shards)


def back_product(grad_rows, weight):
    return lax.dot_general(grad_rows, weight, (((1,), (1,)), ((), ())), preferred_element_type=F32)


def sublane_sums(values):
    rows, features = values.shape
    return jnp.sum(values.reshape(rows // 8, 8, features), 0)


def split_terms(chips, spread_rows, shapes):
    early = []
    room = TERMS_HELD + 3 * LANES * (4096 - spread_rows)
    for at in (6, 4, 5, 3, 2):
        room -= (chips - 1) * shapes[at][0] * shapes[at][1]
        if room < 0:
            break
        early.append(at)
    return early, [at for at in range(len(shapes)) if at not in early]


def backward_kernel(n_fr, n_pos, shard_rows, early, late, *refs):
    (
        delays,
        gain_rows,
        inner_t,
        cot,
        inner_rows,
        gate_low,
        up_low,
        normed_two_t,
        attended_t,
        normed_t,
        branch_in,
        hidden_in,
        queries,
        keys,
        values,
        soft_in,
        *weights,
    ) = refs[:24]
    kept_out = refs[24:31]
    refs = refs[31:]
    come_out, refs = dict(zip(late, refs)), refs[len(late) :]
    output, input_grad, down_w, gains_out, *refs = refs
    held, refs = refs[:7], refs[7:]
    come, refs = dict(zip(early, refs)), refs[len(early) :]
    come.update(come_out)
    (
        made,
        down_slots,
        gate_slots,
        up_slots,
        small,
        inner_v,
        cot_v,
        gate_v,
        up_v,
        normed_two_v,
        attended_v,
        branch,
        total,
        low_rows,
        grad_rows,
        turned,
        soft,
        soft_grads,
        score_slots,
        sum_rows,
        leaving,
        arrived,
        sums,
        spread,
        gain_split,
        gain_in,
        rim_out,
        rim_in,
        load_sem,
        stream_sem,
        give_send,
        take_recv,
        far_send,
        far_recv,
        kept_sem,
        turn_send,
        turn_recv,
        back_send,
        back_recv,
        gain_send,
        gain_recv,
        rim_sem,
        out_sem,
        late_far_send,
        late_far_recv,
        late_near_send,
        late_near_recv,
    ) = refs
    query_w, key_w, value_w, out_w, gate_w, up_w, _, down_shard = weights
    fr = lax.axis_index("fr")
    pos = lax.axis_index("pos")
    chips = n_fr // 2
    chip = fr // 2
    core = lax.rem(fr, 2)
    partner = chip * 2 + 1 - core
    frames, features = cot.shape
    part = frames // n_pos
    tile = made.shape[-1]
    greet(n_fr, n_pos)

    down_rows = down_shard.shape[0]
    cuts = down_pieces(down_rows)
    size = down_rows // cuts
    late_count = cuts * LATE // 100
    late_far = {}
    late_near = {}

    def late_rows(origin, piece):
        start = origin * down_rows + (cuts - late_count + piece) * size
        return pl.ds(pl.multiple_of(start, size), size)

    for piece in range(late_count):
        for k in range(1, chips):
            late_far[piece, k] = send(
                down_shard.at[pl.ds((cuts - late_count + piece) * size, size)],
                down_w.at[late_rows(fr, piece)],
                late_far_send.at[piece * (chips - 1) + k - 1],
                late_far_recv.at[piece * (chips - 1) + k - 1],
                fr=lax.rem(chip + k, chips) * 2 + core,
            )
            late_far[piece, k].start()

    loads = {}

    def load(name, src, dst):
        loads[name] = pltpu.make_async_copy(src, dst, load_sem.at[len(loads)])
        loads[name].start()

    def columns_of(t):
        return pl.ds(pl.multiple_of(t * tile, tile), tile)

    def feed_copies(t):
        slot = lax.rem(t, 2)
        return (
            pltpu.make_async_copy(
                down_w.at[columns_of(t)], down_slots.at[slot], stream_sem.at[slot, 0]
            ),
            pltpu.make_async_copy(
                gate_w.at[:, columns_of(t)], gate_slots.at[slot], stream_sem.at[slot, 1]
            ),
            pltpu.make_async_copy(
                up_w.at[:, columns_of(t)], up_slots.at[slot], stream_sem.at[slot, 2]
            ),
        )

    load("inner", inner_t, inner_v)
    load("cot", cot, cot_v)
    load("gate", gate_low, gate_v)
    load("up", up_low, up_v)
    load("branch", branch_in, branch)
    load("out", out_w, small.at[0])
    load("normed_two", normed_two_t, normed_two_v)
    load("attended", attended_t, attended_v)
    load("queries", queries, turned.at[0])
    load("keys", keys, turned.at[1])
    load("values", values, turned.at[2])
    load("soft", soft_in, soft)
    load("value_w", value_w, small.at[1])
    load("key_w", key_w, small.at[2])
    sums[...] = head_sums(sums.shape, 0)
    spread[...] = head_sums(spread.shape, 1)

    pending = []
    done = [0]

    def settle():
        while pending:
            pending.pop(0)()

    def keep(at, t):
        pltpu.make_async_copy(
            held[at].at[t, chip], kept_out[at].at[:, columns_of(t)], kept_sem.at[at]
        ).start()

    def arrivals(at, k):
        return send(
            come[at].at[k - 1],
            come[at].at[k - 1],
            far_send.at[at * (chips - 1) + k - 1],
            far_recv.at[at * (chips - 1) + k - 1],
            fr=lax.rem(chip + k, chips) * 2 + core,
        )

    def gather_terms(at):
        for k in range(1, chips):
            arrivals(at, k).wait_recv()

        def add(t, carry):
            value = held[at][t, chip].astype(F32)
            for k in range(1, chips):
                value = value + come[at][k - 1, :, columns_of(t)].astype(F32)
            held[at][t, chip] = value.astype(BF16)
            keep(at, t)
            return carry

        lax.fori_loop(0, held[at].shape[0], add, 0)

    def reduce_weight(at, left_t, right):
        rows = shard_rows[at]
        tiles = right.shape[1] // tile
        base = done[0]
        done[0] += tiles
        group = max(1, 1024 // rows)

        def outgoing(t):
            slot = lax.rem(t + base, 2)
            return send(
                made.at[slot, 1 - core, :, pl.ds(0, rows)],
                held[at].at[t],
                give_send.at[slot],
                take_recv.at[sum(held[w].shape[0] for w in range(at)) + t],
                fr=partner,
            )

        def consume(t):
            slot = lax.rem(t + base, 2)
            outgoing(t).wait_recv()
            for there in range(chips):
                held[at][t, there] = (
                    held[at][t, there].astype(F32) + made[slot, core, there, 0:rows].astype(F32)
                ).astype(BF16)
            if at in come_out:
                keep(at, t)
            for k in range(1, chips):
                there = lax.rem(chip + k, chips)
                send(
                    held[at].at[t, there],
                    come[at].at[k - 1, :, columns_of(t)],
                    far_send.at[at * (chips - 1) + k - 1],
                    far_recv.at[at * (chips - 1) + k - 1],
                    fr=there * 2 + core,
                ).start()

        def step(t, carry):
            slot = lax.rem(t + base, 2)

            @pl.when(t >= 2)
            def _():
                outgoing(t - 2).wait_send()

            for first in range(0, n_fr, group):
                last = min(first + group, n_fr)
                grads = product(left_t[first * rows : last * rows], right[:, columns_of(t)])
                for b in range(first, last):
                    made[slot, b % 2, b // 2, 0:rows] = grads[
                        (b - first) * rows : (b - first + 1) * rows
                    ].astype(BF16)
            outgoing(t).start()

            @pl.when(t >= 1)
            def _():
                consume(t - 1)

            return carry

        settle()
        lax.fori_loop(0, tiles, step, 0)

        def finish():
            consume(tiles - 1)
            outgoing(tiles - 2).wait_send()
            outgoing(tiles - 1).wait_send()

        pending.append(finish)

    loads["inner"].wait()
    loads["cot"].wait()
    reduce_weight(6, inner_v, cot_v)

    for piece in range(late_count):
        for k in range(1, chips):
            late_far[piece, k].wait_recv()
            rows = late_rows(lax.rem(chip - k + chips, chips) * 2 + core, piece)
            late_near[piece, k] = send(
                down_w.at[rows],
                down_w.at[rows],
                late_near_send.at[piece * (chips - 1) + k - 1],
                late_near_recv.at[piece * (chips - 1) + k - 1],
                fr=partner,
            )
            late_near[piece, k].start()
    for copy in late_near.values():
        copy.wait_recv()
    for copy in feed_copies(0):
        copy.start()
    loads["gate"].wait()
    loads["up"].wait()
    feed_tiles = gate_v.shape[1] // tile
    total[...] = jnp.zeros_like(total)

    def feed(t, carry):
        slot = lax.rem(t, 2)

        @pl.when(t + 1 < feed_tiles)
        def _():
            for copy in feed_copies(t + 1):
                copy.start()

        for copy in feed_copies(t):
            copy.wait()
        columns = columns_of(t)
        grad_inner = back_product(cot_v[...], down_slots[slot])
        gate = gate_v[:, columns].astype(F32)
        sigmoid = jax.nn.sigmoid(gate)
        scaled = grad_inner * sigmoid
        gate_v[:, columns] = (
            scaled * up_v[:, columns].astype(F32) * (1.0 + gate * (1.0 - sigmoid))
        ).astype(BF16)
        up_v[:, columns] = (scaled * gate).astype(BF16)
        for at in range(features // tile):
            rows = slice(at * tile, (at + 1) * tile)
            total[:, rows] += back_product(
                gate_v[:, columns], gate_slots[slot, rows, :]
            ) + back_product(up_v[:, columns], up_slots[slot, rows, :])
        return carry

    lax.fori_loop(0, feed_tiles, feed, 0)
    settle()

    blocks = delays.shape[1]
    block = frames // blocks
    loads["branch"].wait()

    def block_rows(at):
        return pl.ds(pl.multiple_of(at * block, block), block)

    def feed_norm(at, carry):
        rows = block_rows(at)
        here = branch[rows, :]
        grads = total[rows, :]
        scaling = rms_scaling(here)
        weighted = gain_rows[1:2, :] * grads
        back = scaling * weighted - here * scaling**3 * jnp.mean(weighted * here, -1, keepdims=True)
        back = cot_v[rows, :].astype(F32) + back
        branch[rows, :] = back
        low_rows[rows, :] = back.astype(BF16)
        return carry + sublane_sums(grads * here * scaling)

    feed_gain = lax.fori_loop(0, blocks, feed_norm, jnp.zeros((8, features), F32))
    feed_gain = jnp.sum(feed_gain, 0, keepdims=True)

    loads["out"].wait()

    def turn_back(t, carry):
        columns = columns_of(t)
        grad_rows[:, columns] = back_product(low_rows[...], small[0, columns, :]).astype(BF16)
        return carry

    lax.fori_loop(0, features // tile, turn_back, 0)

    def turn(k):
        peer = peer_of(pos, k, n_pos)
        return send(
            grad_rows.at[rows_of(peer, part)],
            turned.at[3, pos],
            turn_send.at[k],
            turn_recv.at[k],
            pos=peer,
        )

    def start_turn(k, carry):
        turn(k).start()
        return carry

    lax.fori_loop(1, n_pos, start_turn, 0)
    turned[3, pl.ds(pos, 1)] = grad_rows[rows_of(pos, part), :][None]
    load("query_w", query_w, small.at[0])
    load("branch_again", branch_in, total)
    load("hidden", hidden_in, cot_v)

    loads["normed_two"].wait()
    reduce_weight(4, normed_two_v, gate_v)
    load("inner_rows", inner_rows, gate_v)
    reduce_weight(5, normed_two_v, up_v)
    load("normed", normed_t, normed_two_v)
    loads["attended"].wait()
    reduce_weight(3, attended_v, low_rows)

    for name in ("queries", "keys", "values", "soft"):
        loads[name].wait()

    def end_turn(k, carry):
        turn(k).wait()
        return carry

    lax.fori_loop(1, n_pos, end_turn, 0)
    settle()

    def give_back(which, j):
        return send(
            leaving.at[which, j],
            arrived.at[which, rows_of(pos, part)],
            back_send.at[which, j],
            back_recv.at[which, pos],
            pos=j,
        )

    def part_sum(which, j, low, high, weight_of, other, scale):
        sum_rows[...] = jnp.zeros_like(sum_rows)

        def add(at, carry):
            sum_rows[...] += product(weight_of(at), spread[...]) * turned[other, at].astype(F32)
            return carry

        lax.fori_loop(low, high, add, 0)
        leaving[which, j] = (sum_rows[...] * scale).astype(BF16)

        @pl.when(j != pos)
        def _():
            give_back(which, j).start()

        @pl.when(j == pos)
        def _():
            arrived[which, rows_of(pos, part), :] = leaving[which, j]

    def value_part(k, carry):
        j = peer_of(pos, k, n_pos)
        part_sum(2, j, j, n_pos, lambda p: soft[p, j].astype(BF16), 3, 1.0)
        return carry

    lax.fori_loop(1, n_pos + 1, value_part, 0)

    def score_part(p, carry):
        grads = turned[3, p].astype(F32)

        def score(j, centre):
            scores = sum_heads(grads * turned[2, j].astype(F32), sums[...])
            score_slots[j] = scores
            return centre + scores * soft[p, j]

        centre = lax.fori_loop(0, p + 1, score, jnp.zeros((part, LANES), F32))

        def level(j, carry):
            soft_grads[p, j] = (soft[p, j] * (score_slots[j] - centre)).astype(BF16)
            return carry

        return lax.fori_loop(0, p + 1, level, carry)

    lax.fori_loop(0, n_pos, score_part, 0)

    def key_part(k, carry):
        j = peer_of(pos, k, n_pos)
        part_sum(1, j, j, n_pos, lambda p: soft_grads[p, j], 0, HEAD ** (-0.5))
        return carry

    lax.fori_loop(1, n_pos + 1, key_part, 0)

    def query_part(k, carry):
        p = peer_of(pos, k, n_pos)
        part_sum(0, p, 0, p + 1, lambda j: soft_grads[p, j], 1, HEAD ** (-0.5))
        return carry

    lax.fori_loop(1, n_pos + 1, query_part, 0)

    def down_copy(t):
        return feed_copies(t)[0]

    def close(t, carry):
        @pl.when(t + 1 < feed_tiles)
        def _():
            down_copy(t + 1).start()

        down_copy(t).wait()
        units = gate_v[:, columns_of(t)]
        for at in range(features // tile):
            columns = slice(at * tile, (at + 1) * tile)
            total[:, columns] += product(units, down_slots[lax.rem(t, 2), :, columns])
        return carry

    loads["normed"].wait()
    for which, slot, name in ((2, 1, "value_w"), (1, 2, "key_w"), (0, 0, "query_w")):

        def end_back(k, carry):
            peer = peer_of(pos, k, n_pos)
            send(
                leaving.at[which, peer],
                arrived.at[which, rows_of(peer, part)],
                back_send.at[which, peer],
                back_recv.at[which, peer],
                pos=peer,
            ).wait()
            return carry

        lax.fori_loop(1, n_pos, end_back, 0)
        reduce_weight(which, normed_two_v, arrived.at[which])
        if which == 2:
            loads["inner_rows"].wait()
            loads["branch_again"].wait()
            down_copy(0).start()
            lax.fori_loop(0, feed_tiles, close, 0)
            grad_rows[...] = total[...].astype(BF16)
            output_copy = pltpu.make_async_copy(grad_rows, output, out_sem.at[1])
            output_copy.start()
            if 6 in early:
                gather_terms(6)
        loads[name].wait()

        def add_normed(t, carry):
            columns = columns_of(t)
            grads = back_product(arrived[which], small[slot, columns, :])
            total[:, columns] = grads if which == 2 else total[:, columns] + grads
            return carry

        lax.fori_loop(0, features // tile, add_normed, 0)
        if which == 1 and 4 in early:
            gather_terms(4)

    loads["hidden"].wait()

    def attention_norm(at, carry):
        rows = block_rows(at)
        here = cot_v[rows, :].astype(F32)
        grads = total[rows, :]
        scaling = rms_scaling(here)
        weighted = gain_rows[0:1, :] * grads
        back = scaling * weighted - here * scaling**3 * jnp.mean(weighted * here, -1, keepdims=True)
        branch[rows, :] = branch[rows, :] + back
        return carry + sublane_sums(grads * here * scaling)

    gain = lax.fori_loop(0, blocks, attention_norm, jnp.zeros((8, features), F32))
    gain = jnp.sum(gain, 0, keepdims=True)

    first_lags = lag_of(delays, 0)
    once = jnp.where(first_lags == 1, branch[0:8, :], 0.0)
    once = jnp.where(
        lax.broadcasted_iota(jnp.int32, once.shape, 0) == 0, 0.0, pltpu.roll(once, 1, 0)
    )
    rim_out[...] = once + jnp.where(first_lags == 2, branch[0:8, :], 0.0)
    rim_copy = send(
        rim_out, rim_in, rim_sem.at[0], rim_sem.at[1], fr=lax.rem(fr + n_fr - 1, n_fr)
    )
    rim_copy.start()
    gain_pair = jnp.concatenate([gain, feed_gain, jnp.zeros((6, features), F32)], 0)
    width = features // n_fr
    for b in range(n_fr):
        gain_split[b] = gain_pair[:, b * width : (b + 1) * width]
    gain_copies = []
    for k in range(1, n_fr):
        there = lax.rem(fr + k, n_fr)
        copy = send(
            gain_split.at[there], gain_in.at[fr], gain_send.at[k], gain_recv.at[k], fr=there
        )
        copy.start()
        gain_copies.append(copy)
    gain_in[pl.ds(fr, 1)] = gain_split[pl.ds(fr, 1)]
    settle()
    for at in early:
        if at not in (6, 4):
            gather_terms(at)

    rim_copy.wait()
    rim = jnp.where(fr == n_fr - 1, 0.0, rim_in[...])

    def shift(at, carry):
        after_one, after_two = carry
        rows = block_rows(blocks - 1 - at)
        grads = branch[rows, :]
        lag = lag_of(delays, blocks - 1 - at)
        one = jnp.where(lag == 1, grads, 0.0)
        two = jnp.where(lag == 2, grads, 0.0)
        moved = pltpu.roll(jnp.concatenate([one, after_one], 0), block + 7, 0)[:block]
        moved = moved + pltpu.roll(jnp.concatenate([two, after_two], 0), block + 6, 0)[:block]
        low_rows[rows, :] = (jnp.where(lag == 0, grads, 0.0) + moved).astype(BF16)
        return one[:8], two[:8]

    lax.fori_loop(0, blocks, shift, (jnp.zeros_like(rim), rim))
    out_copy = pltpu.make_async_copy(low_rows, input_grad, out_sem.at[0])
    out_copy.start()
    for copy in gain_copies:
        copy.wait()
    gain_sum = gain_in[0]
    for b in range(1, n_fr):
        gain_sum = gain_sum + gain_in[b]
    gains_out[...] = gain_sum

    for at in range(7):
        pltpu.make_async_copy(kept_out[at], kept_out[at], kept_sem.at[at]).wait()
        for k in range(1, chips):
            arrivals(at, k).wait_send()
            if at in come_out:
                arrivals(at, k).wait_recv()
    for copy in late_far.values():
        copy.wait_send()
    for copy in late_near.values():
        copy.wait_send()
    out_copy.wait()
    output_copy.wait()


def backward_call(n_fr, n_pos, shard_shapes, *operands):
    cot = operands[3]
    frames, features = cot.shape
    part = frames // n_pos
    chips = n_fr // 2
    tile = column_tile(features)
    count = len(shard_shapes)
    shard_rows = [rows for rows, _ in shard_shapes]
    hidden_units = operands[4].shape[1]
    act = jax.ShapeDtypeStruct((frames, features), BF16)
    most = max(shard_rows)
    down = operands[-2]
    late_count = max(1, down_pieces(shard_rows[-1]) * LATE // 100)
    early, late = split_terms(chips, n_pos * frames, shard_shapes)
    come_shapes = [(chips - 1, *shape) for shape in shard_shapes]
    return pl.pallas_call(
        functools.partial(backward_kernel, n_fr, n_pos, shard_rows, early, late),
        name="backward",
        out_shape=[jax.ShapeDtypeStruct(shape, BF16) for shape in shard_shapes]
        + [jax.ShapeDtypeStruct(come_shapes[at], BF16) for at in late]
        + [act, act, jax.ShapeDtypeStruct(down.shape, BF16)]
        + [jax.ShapeDtypeStruct((8, features // n_fr), F32)],
        in_specs=[VMEM, VMEM] + [ANY] * (len(operands) - 2),
        out_specs=[ANY] * (count + len(late) + 3) + [VMEM],
        input_output_aliases={len(operands) - 2: count + len(late) + 2},
        scratch_shapes=[
            pltpu.VMEM((columns // tile, chips, rows, tile), BF16) for rows, columns in shard_shapes
        ]
        + [pltpu.VMEM(come_shapes[at], BF16) for at in early]
        + [
            pltpu.VMEM((2, 2, chips, most, tile), BF16),
            pltpu.VMEM((2, tile, features), BF16),
            pltpu.VMEM((2, features, tile), BF16),
            pltpu.VMEM((2, features, tile), BF16),
            pltpu.VMEM((3, features, features), BF16),
            pltpu.VMEM((hidden_units, frames), BF16),
            pltpu.VMEM((frames, features), BF16),
            pltpu.VMEM((frames, hidden_units), BF16),
            pltpu.VMEM((frames, hidden_units), BF16),
            pltpu.VMEM((features, frames), BF16),
            pltpu.VMEM((features, frames), BF16),
            pltpu.VMEM((frames, features), F32),
            pltpu.VMEM((frames, features), F32),
            pltpu.VMEM((frames, features), BF16),
            pltpu.VMEM((frames, features), BF16),
            pltpu.VMEM((4, n_pos, part, features), BF16),
            pltpu.VMEM((n_pos, n_pos, part, LANES), F32),
            pltpu.VMEM((n_pos, n_pos, part, LANES), BF16),
            pltpu.VMEM((n_pos, part, LANES), F32),
            pltpu.VMEM((part, features), F32),
            pltpu.VMEM((3, n_pos, part, features), BF16),
            pltpu.VMEM((3, frames, features), BF16),
            pltpu.VMEM((features, LANES), BF16),
            pltpu.VMEM((LANES, features), BF16),
            pltpu.VMEM((n_fr, 8, features // n_fr), F32),
            pltpu.VMEM((n_fr, 8, features // n_fr), F32),
            pltpu.VMEM((8, features), F32),
            pltpu.VMEM((8, features), F32),
            DMA((19,)),
            DMA((2, 3)),
            DMA((2,)),
            DMA((sum(columns // tile for _, columns in shard_shapes),)),
            DMA((count * (chips - 1),)),
            DMA((count * (chips - 1),)),
            DMA((count,)),
            DMA((n_pos,)),
            DMA((n_pos,)),
            DMA((3, n_pos)),
            DMA((3, n_pos)),
            DMA((n_fr,)),
            DMA((n_fr,)),
            DMA((2,)),
            DMA((2,)),
            DMA((late_count * (chips - 1),)),
            DMA((late_count * (chips - 1),)),
            DMA((late_count * (chips - 1),)),
            DMA((late_count * (chips - 1),)),
        ],
        compiler_params=pltpu.CompilerParams(
            collective_id=1, has_side_effects=True, vmem_limit_bytes=VMEM_BYTES
        ),
    )(*operands)


def finish_kernel(count, late, *refs):
    kept, refs = refs[:count], refs[count:]
    come, refs = dict(zip(late, refs)), refs[len(late) :]
    output_in, input_grad_in, gains, *refs = refs
    sums, refs = refs[:count], refs[count:]
    output, input_grad, gain_one, gain_two, *refs = refs
    kept_v, refs = refs[:count], refs[count:]
    come_v, refs = dict(zip(late, refs)), refs[len(late) :]
    sums_v, refs = refs[:count], refs[count:]
    through, load_sem, store_sem, through_sem = refs
    chunks = []
    for at in range(count):
        rows, columns = kept[at].shape
        cuts = next(
            cuts
            for cuts in (4, 2, 1)
            if rows % (16 * cuts) == 0 and (cuts == 1 or rows * columns >= cuts * 131072)
        )
        size = rows // cuts
        chunks += [(at, pl.ds(piece * size, size), piece) for piece in range(cuts)]

    order = {(at, piece): i for i, (at, _, piece) in enumerate(chunks)}

    def loads(at, rows, piece):
        copies = [
            pltpu.make_async_copy(kept[at].at[rows], kept_v[at].at[rows], load_sem.at[order[at, piece]])
        ]
        if at in come:
            copies.append(
                pltpu.make_async_copy(
                    come[at].at[:, rows], come_v[at].at[:, rows], load_sem.at[len(order) + order[at, piece]]
                )
            )
        return copies

    for chunk in chunks:
        for copy in loads(*chunk):
            copy.start()
    acts = [
        pltpu.make_async_copy(output_in, through.at[0], through_sem.at[0]),
        pltpu.make_async_copy(input_grad_in, through.at[1], through_sem.at[1]),
    ]
    for copy in acts:
        copy.start()
    gain_one[...] = gains[0:1, :]
    gain_two[...] = gains[1:2, :]
    stores = []
    for at, rows, piece in chunks:
        for copy in loads(at, rows, piece):
            copy.wait()
        step = 16

        def add(i, carry):
            here = pl.ds(pl.multiple_of(rows.start + i * step, step), step)
            value = kept_v[at][here, :].astype(F32)
            for k in range(come_v[at].shape[0] if at in come else 0):
                value = value + come_v[at][k, here, :].astype(F32)
            sums_v[at][here, :] = value
            return carry

        lax.fori_loop(0, rows.size // step, add, 0)
        stores.append(
            pltpu.make_async_copy(sums_v[at].at[rows], sums[at].at[rows], store_sem.at[order[at, piece]])
        )
        stores[-1].start()
    for copy, leaving, slot in zip(acts, (output, input_grad), range(2)):
        copy.wait()
        stores.append(pltpu.make_async_copy(through.at[slot], leaving, through_sem.at[2 + slot]))
        stores[-1].start()
    for copy in stores:
        copy.wait()


def finish_call(late, kept, come, output, input_grad, gains):
    count = len(kept)
    gain = jax.ShapeDtypeStruct((1, gains.shape[1]), F32)
    return pl.pallas_call(
        functools.partial(finish_kernel, count, late),
        name="finish",
        out_shape=[jax.ShapeDtypeStruct(own.shape, F32) for own in kept]
        + [jax.ShapeDtypeStruct(output.shape, BF16)] * 2
        + [gain, gain],
        in_specs=[ANY] * (count + len(come) + 2) + [VMEM],
        out_specs=[ANY] * (count + 2) + [VMEM, VMEM],
        scratch_shapes=[pltpu.VMEM(own.shape, BF16) for own in kept]
        + [pltpu.VMEM(others.shape, BF16) for others in come]
        + [pltpu.VMEM(own.shape, F32) for own in kept]
        + [
            pltpu.VMEM((2, *output.shape), BF16),
            DMA((2 * 3 * count,)),
            DMA((3 * count,)),
            DMA((4,)),
        ],
        compiler_params=pltpu.CompilerParams(vmem_limit_bytes=VMEM_BYTES),
    )(*kept, *come, output, input_grad, gains)


def on_device(
    inputs,
    delays,
    query_weight,
    key_weight,
    value_weight,
    out_weight,
    gate_weight,
    up_weight,
    down_weight,
    attention_gain,
    feed_gain,
    cotangent,
):
    n_fr = lax.axis_size("fr")
    n_pos = lax.axis_size("pos")
    shards = [
        weight[0]
        for weight in (
            query_weight,
            key_weight,
            value_weight,
            out_weight,
            gate_weight,
            up_weight,
            down_weight,
        )
    ]
    delays = delays.T
    results = forward_call(n_fr, n_pos, inputs[0], delays, attention_gain, feed_gain, shards)
    full, saved, gain_rows = results[:7], results[7:20], results[20]
    inner_t, *saved = saved
    grads = backward_call(
        n_fr,
        n_pos,
        [shard.shape for shard in shards],
        delays,
        gain_rows,
        inner_t,
        cotangent[0],
        *saved,
        *full,
        shards[-1],
    )
    late = split_terms(
        n_fr // 2, n_pos * inputs.shape[1], [shard.shape for shard in shards]
    )[1]
    kept, come = grads[:7], grads[7 : 7 + len(late)]
    output, input_grad, _, gain_grads = grads[7 + len(late) :]
    *sums, output, input_grad, attention_gain_grad, feed_gain_grad = finish_call(
        late, kept, come, output, input_grad, gain_grads
    )
    return (
        output[None],
        input_grad[None],
        *(total[None] for total in sums),
        attention_gain_grad,
        feed_gain_grad,
    )


def solution(mesh):
    matrix = P("pos", "fr", None)
    vector = P("pos", "fr")
    return jax.shard_map(
        on_device,
        mesh=mesh,
        in_specs=(matrix, P("fr", "pos")) + (matrix,) * 7 + (vector, vector, matrix),
        out_specs=(matrix,) * 9 + (vector, vector),
        check_vma=False,
    )
```

```python
import functools

import jax
import jax.numpy as jnp
from jax import lax
from jax.experimental import pallas as pl
from jax.experimental.pallas import tpu as pltpu
from jax.sharding import PartitionSpec as P

HEAD = 64
LANES = 128
EPSILON = 1e-06
LATE = 37
TERMS_HELD = 2750000
MESH = pl.DeviceIdType.MESH
F32 = jnp.float32
BF16 = jnp.bfloat16
ANY = pl.BlockSpec(memory_space=pl.ANY)
VMEM = pl.BlockSpec(memory_space=pltpu.VMEM)
DMA = pltpu.SemaphoreType.DMA
VMEM_BYTES = 64 * 1024 * 1024 - 65536


def greet(n_fr, n_pos):
    fr = lax.axis_index("fr")
    pos = lax.axis_index("pos")
    barrier = pltpu.get_barrier_semaphore()
    for k in range(1, n_fr):
        pl.semaphore_signal(
            barrier, inc=1, device_id={"fr": lax.rem(fr + k, n_fr)}, device_id_type=MESH
        )
    for k in range(1, n_pos):
        pl.semaphore_signal(
            barrier, inc=1, device_id={"pos": lax.rem(pos + k, n_pos)}, device_id_type=MESH
        )
    pl.semaphore_wait(barrier, n_fr + n_pos - 2)


def send(src, dst, send_sem, recv_sem, **device):
    return pltpu.make_async_remote_copy(
        src_ref=src,
        dst_ref=dst,
        send_sem=send_sem,
        recv_sem=recv_sem,
        device_id=device,
        device_id_type=MESH,
    )


def rows_of(index, rows):
    return pl.ds(pl.multiple_of(index * rows, rows), rows)


def lag_of(delays, at):
    here = lax.broadcasted_iota(jnp.int32, delays.shape, 1) == at
    return jnp.sum(jnp.where(here, delays[...].astype(F32), 0.0), 1, keepdims=True)


def head_sums(shape, feature_dim):
    features = lax.broadcasted_iota(jnp.int32, shape, feature_dim)
    heads = lax.broadcasted_iota(jnp.int32, shape, 1 - feature_dim)
    return (features // HEAD == heads).astype(BF16)


def sum_heads(product, sums):
    high = product.astype(BF16)
    low = (product - high.astype(F32)).astype(BF16)
    return jnp.dot(high, sums, preferred_element_type=F32) + jnp.dot(
        low, sums, preferred_element_type=F32
    )


def rms_scaling(values):
    return lax.rsqrt(jnp.mean(values * values, -1, keepdims=True) + EPSILON)


def product(operand, weight):
    return jnp.dot(operand, weight, preferred_element_type=F32)


def column_tile(columns):
    return 256 if columns % 256 == 0 else LANES


def multiply(rows_ref, weight_ref, out_ref):
    tile = column_tile(weight_ref.shape[1])

    def step(at, carry):
        columns = pl.ds(pl.multiple_of(at * tile, tile), tile)
        out_ref[:, columns] = jnp.dot(
            rows_ref[...], weight_ref[:, columns], preferred_element_type=F32
        ).astype(out_ref.dtype)
        return carry

    lax.fori_loop(0, weight_ref.shape[1] // tile, step, 0)


def peer_of(pos, k, n_pos):
    return lax.rem(pos + k, n_pos)


def forward_kernel(n_fr, n_pos, pieces, late, steps, *refs):
    (
        rows_in,
        delays,
        gain_one,
        gain_two,
        w0,
        w1,
        w2,
        w3,
        w4,
        w5,
        w6,
        o0,
        o1,
        o2,
        o3,
        o4,
        o5,
        o6,
        inner_out,
        inner_rows_out,
        gate_out,
        up_out,
        normed_two_out,
        attended_out,
        normed_out,
        branch_out,
        hidden_out,
        queries_out,
        keys_out,
        values_out,
        soft_out,
        gains_out,
        f0,
        f1,
        f2,
        f3,
        f4,
        f5,
        f6,
        own_rows,
        rim,
        gains,
        gain_slots,
        hidden,
        normed,
        proj,
        turned,
        mixed,
        attended,
        normed_t,
        attended_t,
        normed_two_t,
        normed_two,
        inner,
        inner_t,
        gate_low,
        up_low,
        branch,
        score_slots,
        soft_slots,
        total,
        sums,
        spread,
        far_send,
        far_recv,
        near_send,
        near_recv,
        own_sem,
        out_sem,
        rim_sem,
        gain_send,
        gain_recv,
        turn_send,
        turn_recv,
        back_send,
        back_recv,
        act_sem,
    ) = refs
    shards = (w0, w1, w2, w3, w4, w5, w6)
    full_out = (o0, o1, o2, o3, o4, o5, o6)
    full = (f0, f1, f2, f3, f4, f5, f6)
    turned_out = (queries_out, keys_out, values_out)
    fr = lax.axis_index("fr")
    pos = lax.axis_index("pos")
    chips = n_fr // 2
    chip = fr // 2
    core = lax.rem(fr, 2)
    partner = chip * 2 + 1 - core
    frames, features = own_rows.shape
    part = frames // n_pos
    greet(n_fr, n_pos)
    own_load = pltpu.make_async_copy(rows_in, own_rows, own_sem.at[len(shards)])
    own_load.start()

    edge = own_rows.shape[0] - rim.shape[0]
    rim_copy = send(
        rows_in.at[pl.ds(edge, rim.shape[0])],
        rim,
        rim_sem.at[0],
        rim_sem.at[1],
        fr=lax.rem(fr + 1, n_fr),
    )
    rim_copy.start()
    gains[...] = jnp.concatenate(
        [
            gain_one[...].astype(F32),
            gain_two[...].astype(F32),
            jnp.zeros((6, gains.shape[1]), F32),
        ],
        0,
    )
    gain_copies = []
    for k in range(1, n_fr):
        copy = send(
            gains,
            gain_slots.at[fr],
            gain_send.at[k],
            gain_recv.at[k],
            fr=lax.rem(fr + k, n_fr),
        )
        copy.start()
        gain_copies.append(copy)
    far = {}
    near = {}
    own = {}
    def piece_rows(at, origin, piece):
        rows = shards[at].shape[0]
        size = rows // pieces[at]
        return pl.ds(pl.multiple_of(origin * rows + piece * size, size), size)

    tile = column_tile(features)
    tiles = features // tile
    spare = sum(steps) * (chips - 1)

    def slot(at, k, piece):
        return (sum(steps[:at]) + piece) * (chips - 1) + k - 1


    def columns_of(t):
        return pl.ds(pl.multiple_of(t * tile, tile), tile)

    for t in range(tiles):
        for k in range(1, chips):
            far[0, k, t] = send(
                w0.at[:, columns_of(t)],
                f0.at[rows_of(fr, w0.shape[0]), columns_of(t)],
                far_send.at[0],
                far_recv.at[slot(0, k, t)],
                fr=lax.rem(chip + k, chips) * 2 + core,
            )
            far[0, k, t].start()
    up_tiles = w5.shape[1] // tile

    def up_far(t, k):
        return send(
            w5.at[:, columns_of(t)],
            f5.at[rows_of(fr, w5.shape[0]), columns_of(t)],
            far_send.at[5],
            far_recv.at[slot(5, k, t)],
            fr=lax.rem(chip + k, chips) * 2 + core,
        )

    def up_near(t, k):
        there = f5.at[
            rows_of(lax.rem(chip - k + chips, chips) * 2 + core, w5.shape[0]), columns_of(t)
        ]
        return send(there, there, near_send.at[5], near_recv.at[slot(5, k, t)], fr=partner)

    def up_start(t, carry):
        for k in range(1, chips):
            up_far(t, k).start()
        return carry

    for at, (shard, whole) in enumerate(zip(shards, full)):
        if at == 5:
            lax.fori_loop(0, up_tiles, up_start, 0)
        mine = rows_of(fr, shard.shape[0])
        size = shard.shape[0] // pieces[at]
        for piece in range(0 if at in (0, 5) else pieces[at] - late[at]):
            for k in range(1, chips):
                far[at, k, piece] = send(
                    shard.at[piece * size : (piece + 1) * size],
                    whole.at[piece_rows(at, fr, piece)],
                    far_send.at[at],
                    far_recv.at[slot(at, k, piece)],
                    fr=lax.rem(chip + k, chips) * 2 + core,
                )
                far[at, k, piece].start()
        near[at, 0, 0] = send(
            shard, whole.at[mine], near_send.at[at], near_recv.at[spare + at], fr=partner
        )
        if at < 3:
            near[at, 0, 0].start()
        own[at] = pltpu.make_async_copy(shard, whole.at[mine], own_sem.at[at])
        own[at].start()

    sums[...] = head_sums(sums.shape, 0)
    spread[...] = head_sums(spread.shape, 1)
    gain_slots[pl.ds(fr, 1)] = gains[...][None]
    for copy in gain_copies:
        copy.wait()
    gain_row = jnp.concatenate([gain_slots[at, 0:1, :] for at in range(n_fr)], 1)
    gains_out[...] = jnp.concatenate([gain_slots[at] for at in range(n_fr)], 1)
    rim_copy.wait()
    own_load.wait()

    block = frames // delays.shape[1]
    rim_rows = rim.shape[0]
    rim_all = jnp.where(fr == 0, 0.0, rim[...].astype(F32))[rim_rows - 8 :]

    def norm_block(at, carry):
        rows = pl.ds(pl.multiple_of(at * block, block), block)
        here = own_rows[rows, :].astype(F32)
        window = jnp.concatenate([carry, here], 0)
        once = pltpu.roll(window, 1, 0)[8:]
        twice = pltpu.roll(window, 2, 0)[8:]
        lag = lag_of(delays, at)
        values = jnp.where(lag == 0, here, jnp.where(lag == 1, once, twice))
        hidden[rows, :] = values.astype(BF16)
        scaling = lax.rsqrt(jnp.mean(values * values, -1, keepdims=True) + EPSILON)
        normed[rows, :] = (values * scaling * gain_row).astype(BF16)
        return here[block - 8 :]

    lax.fori_loop(0, frames // block, norm_block, rim_all)
    act_copies = []

    def put(src, dst):
        act_copies.append(pltpu.make_async_copy(src, dst, act_sem.at[len(act_copies)]))
        act_copies[-1].start()

    put(hidden, hidden_out)

    outs = {}

    def pass_on(at, piece=0):
        for k in range(1, chips):
            far[at, k, piece].wait_recv()
            origin = lax.rem(chip - k + chips, chips) * 2 + core
            rows = piece_rows(at, origin, piece)
            near[at, k, piece] = send(
                full[at].at[rows],
                full[at].at[rows],
                near_send.at[at],
                near_recv.at[slot(at, k, piece)],
                fr=partner,
            )
            near[at, k, piece].start()

    def complete(at):
        own[at].wait()
        for k in range(chips):
            near[at, k, 0].wait_recv()
        outs[at] = pltpu.make_async_copy(full[at], full_out[at], out_sem.at[at])
        outs[at].start()

    def finish_pieces(at):
        early = range(pieces[at] - late[at])
        rows = shards[at].shape[0]
        size = rows // pieces[at]

        def put_rows(where):
            pltpu.make_async_copy(
                full[at].at[where], full_out[at].at[where], out_sem.at[at]
            ).start()

        own[at].wait()
        put_rows(rows_of(fr, rows))
        near[at, 0, 0].wait_recv()
        put_rows(rows_of(partner, rows))
        for piece in early:
            pass_on(at, piece)
            for k in range(1, chips):
                put_rows(piece_rows(at, lax.rem(chip - k + chips, chips) * 2 + core, piece))
        for piece in early:
            for k in range(1, chips):
                near[at, k, piece].wait_recv()
                put_rows(piece_rows(at, lax.rem(chip - k + chips, chips) * 2 + 1 - core, piece))
        written = full_out[at].at[0 : n_fr * rows - 2 * (chips - 1) * late[at] * size]
        outs[at] = pltpu.make_async_copy(written, written, out_sem.at[at])

    def turn(which, k):
        peer = peer_of(pos, k, n_pos)
        return send(
            proj.at[which, rows_of(peer, part)],
            turned.at[which, pos],
            turn_send.at[which],
            turn_recv.at[which],
            pos=peer,
        )

    own[0].wait()
    near[0, 0, 0].wait_recv()
    for t in range(tiles):
        for k in range(1, chips):
            far[0, k, t].wait_recv()
            origin = lax.rem(chip - k + chips, chips) * 2 + core
            there = f0.at[rows_of(origin, w0.shape[0]), columns_of(t)]
            near[0, k, t] = send(
                there, there, near_send.at[0], near_recv.at[slot(0, k, t)], fr=partner
            )
            near[0, k, t].start()
        for k in range(1, chips):
            near[0, k, t].wait_recv()
        proj[0, :, columns_of(t)] = product(normed[...], f0[:, columns_of(t)]).astype(BF16)

        def start_tile(k, carry):
            peer = peer_of(pos, k, n_pos)
            send(
                proj.at[0, rows_of(peer, part), columns_of(t)],
                turned.at[0, pos, :, columns_of(t)],
                turn_send.at[0],
                turn_recv.at[0],
                pos=peer,
            ).start()
            return carry

        lax.fori_loop(1, n_pos, start_tile, 0)
    turned[0, pl.ds(pos, 1)] = proj[0, rows_of(pos, part), :][None]
    outs[0] = pltpu.make_async_copy(f0, o0, out_sem.at[0])
    outs[0].start()
    for which in (1, 2):
        pass_on(which)
        complete(which)
        multiply(normed, full[which], proj.at[which])

        def start_turn(k, carry):
            turn(which, k).start()
            return carry

        lax.fori_loop(1, n_pos, start_turn, 0)
        turned[which, pl.ds(pos, 1)] = proj[which, rows_of(pos, part), :][None]

    for at in range(3, 7):
        near[at, 0, 0].start()

    def transpose(src, dst):
        tile = column_tile(src.shape[1])

        def step(t, carry):
            at = pl.ds(pl.multiple_of(t * tile, tile), tile)
            dst[at, :] = src[:, at].T
            return carry

        lax.fori_loop(0, src.shape[1] // tile, step, 0)

    transpose(normed, normed_t)
    put(normed_t, normed_out)
    pass_on(3)

    def end_turns(which):
        landed = turned.at[which, 0 : n_pos - 1]
        send(
            landed,
            landed,
            turn_send.at[which],
            turn_recv.at[which],
            pos=peer_of(pos, 1, n_pos),
        ).wait()
        put(turned.at[which], turned_out[which])

    end_turns(0)
    end_turns(1)

    def score_rows(p, carry):
        query = turned[0, p].astype(F32) * HEAD ** (-0.5)

        def score(j, highest):
            scores = sum_heads(query * turned[1, j].astype(F32), sums[...])
            score_slots[j] = scores
            return jnp.maximum(highest, scores)

        highest = lax.fori_loop(0, p + 1, score, jnp.full((part, LANES), -1e30, F32))

        def weigh(j, mass):
            return mass + jnp.exp(score_slots[j] - highest)

        mass = lax.fori_loop(0, p + 1, weigh, jnp.zeros((part, LANES), F32))
        logsum = highest + jnp.log(mass)

        def level(j, carry):
            soft_slots[p, j] = jnp.exp(score_slots[j] - logsum)
            return carry

        return lax.fori_loop(0, p + 1, level, carry)

    lax.fori_loop(0, n_pos, score_rows, 0)
    put(soft_slots, soft_out)
    pass_on(4)
    end_turns(2)

    def back(p):
        return send(
            mixed.at[p],
            attended.at[rows_of(pos, part)],
            back_send.at[0],
            back_recv.at[0],
            pos=p,
        )

    def mix_rows(k, carry):
        p = peer_of(pos, k, n_pos)
        total[...] = jnp.zeros_like(total)

        def mix(j, carry):
            total[...] += product(soft_slots[p, j].astype(BF16), spread[...]) * turned[
                2, j
            ].astype(F32)
            return carry

        lax.fori_loop(0, p + 1, mix, 0)
        mixed[p] = total[...].astype(BF16)

        @pl.when(p != pos)
        def _():
            back(p).start()

        @pl.when(p == pos)
        def _():
            attended[rows_of(pos, part), :] = mixed[p]

        return carry

    lax.fori_loop(1, n_pos + 1, mix_rows, 0)
    complete(3)
    complete(4)

    landed = mixed.at[0 : n_pos - 1]
    send(
        landed, landed, back_send.at[0], back_recv.at[0], pos=peer_of(pos, 1, n_pos)
    ).wait()
    def leave(t, carry):
        columns = columns_of(t)
        branch[:, columns] = hidden[:, columns].astype(F32) + product(
            attended[...], full[3][:, columns]
        )
        return carry

    lax.fori_loop(0, features // tile, leave, 0)
    put(branch, branch_out)
    feed_gain = gains_out[1:2, :]

    def norm_two(at, carry):
        rows = pl.ds(pl.multiple_of(at * block, block), block)
        here = branch[rows, :]
        normed_two[rows, :] = (here * rms_scaling(here) * feed_gain).astype(BF16)
        return carry

    lax.fori_loop(0, frames // block, norm_two, 0)

    transpose(attended, attended_t)
    put(attended_t, attended_out)
    transpose(normed_two, normed_two_t)
    put(normed_two_t, normed_two_out)

    def up_pass(t):
        for k in range(1, chips):
            up_far(t, k).wait_recv()
            up_near(t, k).start()

    def up_put(t):
        return pltpu.make_async_copy(
            f5.at[:, columns_of(t)], o5.at[:, columns_of(t)], out_sem.at[5]
        )

    own[5].wait()
    near[5, 0, 0].wait_recv()
    up_pass(0)

    def feed(t, carry):
        columns = columns_of(t)

        @pl.when(t + 1 < up_tiles)
        def _():
            up_pass(t + 1)

        for k in range(1, chips):
            up_near(t, k).wait_recv()
        up_put(t).start()
        gate = product(normed_two[...], full[4][:, columns])
        up = product(normed_two[...], full[5][:, columns])
        gate_low[:, columns] = gate.astype(BF16)
        up_low[:, columns] = up.astype(BF16)
        low = (gate * jax.nn.sigmoid(gate) * up).astype(BF16)
        inner[:, columns] = low
        inner_t[columns, :] = low.T
        return carry

    lax.fori_loop(0, inner.shape[1] // tile, feed, 0)
    put(gate_low, gate_out)
    put(up_low, up_out)
    put(inner_t, inner_out)
    put(inner, inner_rows_out)
    finish_pieces(6)
    pltpu.make_async_copy(o5, o5, out_sem.at[5]).wait()
    for at in range(len(shards)):
        rows = shards[at].shape[0]
        early = (chips - 1) * (rows - late[at] * (rows // pieces[at]))
        gone = full[at].at[0:early]
        send(gone, gone, far_send.at[at], near_recv.at[0], fr=partner).wait_send()
        gone = full[at].at[0 : early + rows]
        send(gone, gone, near_send.at[at], near_recv.at[0], fr=partner).wait_send()
    for copy in outs.values():
        copy.wait()
    for copy in act_copies:
        copy.wait()


def down_pieces(rows):
    return next(cuts for cuts in (11, 8, 4, 2, 1) if rows % (16 * cuts) == 0)


def forward_call(n_fr, n_pos, own_rows, delays, gain_one, gain_two, shards):
    frames, features = own_rows.shape
    part = frames // n_pos
    count = len(shards)
    chips = n_fr // 2
    width = gain_one.shape[1]
    last = down_pieces(shards[-1].shape[0])
    pieces = [1] * (count - 1) + [last]
    late = [0] * (count - 1) + [last * LATE // 100]
    tile = column_tile(features)
    steps = [1] * (count - 1) + [last - late[-1]]
    steps[0] = features // tile
    steps[5] = shards[5].shape[1] // tile
    copies = sum(steps) * (chips - 1)
    full = [(n_fr * shard.shape[0], shard.shape[1]) for shard in shards]
    hidden_units = shards[4].shape[1]
    act = jax.ShapeDtypeStruct((frames, features), BF16)
    act_t = jax.ShapeDtypeStruct((features, frames), BF16)
    wide = jax.ShapeDtypeStruct((frames, hidden_units), BF16)
    wide_t = jax.ShapeDtypeStruct((hidden_units, frames), BF16)
    turned = jax.ShapeDtypeStruct((n_pos, part, features), BF16)
    return pl.pallas_call(
        functools.partial(forward_kernel, n_fr, n_pos, pieces, late, steps),
        name="forward",
        out_shape=[jax.ShapeDtypeStruct(shape, BF16) for shape in full]
        + [wide_t, wide, wide, wide, act_t, act_t, act_t]
        + [jax.ShapeDtypeStruct((frames, features), F32), act, turned, turned, turned]
        + [
            jax.ShapeDtypeStruct((n_pos, n_pos, part, LANES), F32),
            jax.ShapeDtypeStruct((8, features), F32),
        ],
        in_specs=[ANY] + [VMEM] * 3 + [ANY] * count,
        out_specs=[ANY] * (count + 13) + [VMEM],
        scratch_shapes=[pltpu.VMEM(shape, BF16) for shape in full]
        + [
            pltpu.VMEM((frames, features), BF16),
            pltpu.VMEM((16, features), BF16),
            pltpu.VMEM((8, width), F32),
            pltpu.VMEM((n_fr, 8, width), F32),
            pltpu.VMEM((frames, features), BF16),
            pltpu.VMEM((frames, features), BF16),
            pltpu.VMEM((3, frames, features), BF16),
            pltpu.VMEM((3, n_pos, part, features), BF16),
            pltpu.VMEM((n_pos, part, features), BF16),
            pltpu.VMEM((frames, features), BF16),
            pltpu.VMEM((features, frames), BF16),
            pltpu.VMEM((features, frames), BF16),
            pltpu.VMEM((features, frames), BF16),
            pltpu.VMEM((frames, features), BF16),
            pltpu.VMEM((frames, hidden_units), BF16),
            pltpu.VMEM((hidden_units, frames), BF16),
            pltpu.VMEM((frames, hidden_units), BF16),
            pltpu.VMEM((frames, hidden_units), BF16),
            pltpu.VMEM((frames, features), F32),
            pltpu.VMEM((n_pos, part, LANES), F32),
            pltpu.VMEM((n_pos, n_pos, part, LANES), F32),
            pltpu.VMEM((part, features), F32),
            pltpu.VMEM((features, LANES), BF16),
            pltpu.VMEM((LANES, features), BF16),
            DMA((count,)),
            DMA((copies,)),
            DMA((count,)),
            DMA((copies + count,)),
            DMA((count + 1,)),
            DMA((count,)),
            DMA((2,)),
            DMA((n_fr,)),
            DMA((n_fr,)),
            DMA((3,)),
            DMA((3,)),
            DMA((1,)),
            DMA((1,)),
            DMA((14,)),
        ],
        compiler_params=pltpu.CompilerParams(
            collective_id=0, has_side_effects=True, vmem_limit_bytes=VMEM_BYTES
        ),
    )(own_rows, delays, gain_one, gain_two, *shards)


def back_product(grad_rows, weight):
    return lax.dot_general(grad_rows, weight, (((1,), (1,)), ((), ())), preferred_element_type=F32)


def sublane_sums(values):
    rows, features = values.shape
    return jnp.sum(values.reshape(rows // 8, 8, features), 0)


def split_terms(chips, spread_rows, shapes):
    early = []
    room = TERMS_HELD + 3 * LANES * (4096 - spread_rows)
    for at in (6, 4, 5, 3, 2):
        room -= (chips - 1) * shapes[at][0] * shapes[at][1]
        if room < 0:
            break
        early.append(at)
    return early, [at for at in range(len(shapes)) if at not in early]


def backward_kernel(n_fr, n_pos, shard_rows, early, late, *refs):
    (
        delays,
        gain_rows,
        inner_t,
        cot,
        inner_rows,
        gate_low,
        up_low,
        normed_two_t,
        attended_t,
        normed_t,
        branch_in,
        hidden_in,
        queries,
        keys,
        values,
        soft_in,
        *weights,
    ) = refs[:24]
    kept_out = refs[24:31]
    refs = refs[31:]
    come_out, refs = dict(zip(late, refs)), refs[len(late) :]
    output, input_grad, down_w, gains_out, *refs = refs
    held, refs = refs[:7], refs[7:]
    come, refs = dict(zip(early, refs)), refs[len(early) :]
    come.update(come_out)
    (
        made,
        down_slots,
        gate_slots,
        up_slots,
        small,
        inner_v,
        cot_v,
        gate_v,
        up_v,
        normed_two_v,
        attended_v,
        branch,
        total,
        low_rows,
        grad_rows,
        turned,
        soft,
        soft_grads,
        score_slots,
        sum_rows,
        leaving,
        arrived,
        sums,
        spread,
        gain_split,
        gain_in,
        rim_out,
        rim_in,
        load_sem,
        stream_sem,
        give_send,
        take_recv,
        far_send,
        far_recv,
        kept_sem,
        turn_send,
        turn_recv,
        back_send,
        back_recv,
        gain_send,
        gain_recv,
        rim_sem,
        out_sem,
        late_far_send,
        late_far_recv,
        late_near_send,
        late_near_recv,
    ) = refs
    query_w, key_w, value_w, out_w, gate_w, up_w, _, down_shard = weights
    fr = lax.axis_index("fr")
    pos = lax.axis_index("pos")
    chips = n_fr // 2
    chip = fr // 2
    core = lax.rem(fr, 2)
    partner = chip * 2 + 1 - core
    frames, features = cot.shape
    part = frames // n_pos
    tile = made.shape[-1]
    greet(n_fr, n_pos)

    down_rows = down_shard.shape[0]
    cuts = down_pieces(down_rows)
    size = down_rows // cuts
    late_count = cuts * LATE // 100
    late_far = {}
    late_near = {}

    def late_rows(origin, piece):
        start = origin * down_rows + (cuts - late_count + piece) * size
        return pl.ds(pl.multiple_of(start, size), size)

    for piece in range(late_count):
        for k in range(1, chips):
            late_far[piece, k] = send(
                down_shard.at[pl.ds((cuts - late_count + piece) * size, size)],
                down_w.at[late_rows(fr, piece)],
                late_far_send.at[piece * (chips - 1) + k - 1],
                late_far_recv.at[piece * (chips - 1) + k - 1],
                fr=lax.rem(chip + k, chips) * 2 + core,
            )
            late_far[piece, k].start()

    loads = {}

    def load(name, src, dst):
        loads[name] = pltpu.make_async_copy(src, dst, load_sem.at[len(loads)])
        loads[name].start()

    def columns_of(t):
        return pl.ds(pl.multiple_of(t * tile, tile), tile)

    def feed_copies(t):
        slot = lax.rem(t, 2)
        return (
            pltpu.make_async_copy(
                down_w.at[columns_of(t)], down_slots.at[slot], stream_sem.at[slot, 0]
            ),
            pltpu.make_async_copy(
                gate_w.at[:, columns_of(t)], gate_slots.at[slot], stream_sem.at[slot, 1]
            ),
            pltpu.make_async_copy(
                up_w.at[:, columns_of(t)], up_slots.at[slot], stream_sem.at[slot, 2]
            ),
        )

    load("inner", inner_t, inner_v)
    load("cot", cot, cot_v)
    load("gate", gate_low, gate_v)
    load("up", up_low, up_v)
    load("branch", branch_in, branch)
    load("out", out_w, small.at[0])
    load("normed_two", normed_two_t, normed_two_v)
    load("attended", attended_t, attended_v)
    load("queries", queries, turned.at[0])
    load("keys", keys, turned.at[1])
    load("values", values, turned.at[2])
    load("soft", soft_in, soft)
    load("value_w", value_w, small.at[1])
    load("key_w", key_w, small.at[2])
    sums[...] = head_sums(sums.shape, 0)
    spread[...] = head_sums(spread.shape, 1)

    pending = []
    done = [0]

    def settle():
        while pending:
            pending.pop(0)()

    def keep(at, t):
        pltpu.make_async_copy(
            held[at].at[t, chip], kept_out[at].at[:, columns_of(t)], kept_sem.at[at]
        ).start()

    def arrivals(at, k):
        return send(
            come[at].at[k - 1],
            come[at].at[k - 1],
            far_send.at[at * (chips - 1) + k - 1],
            far_recv.at[at * (chips - 1) + k - 1],
            fr=lax.rem(chip + k, chips) * 2 + core,
        )

    def gather_terms(at):
        for k in range(1, chips):
            arrivals(at, k).wait_recv()

        def add(t, carry):
            value = held[at][t, chip].astype(F32)
            for k in range(1, chips):
                value = value + come[at][k - 1, :, columns_of(t)].astype(F32)
            held[at][t, chip] = value.astype(BF16)
            keep(at, t)
            return carry

        lax.fori_loop(0, held[at].shape[0], add, 0)

    def reduce_weight(at, left_t, right, first=0, last=None):
        rows = shard_rows[at]
        last = last or right.shape[1] // tile
        base = done[0] + first
        done[0] += last - first
        group = max(1, 1024 // rows)

        def outgoing(t):
            slot = lax.rem(t + base, 2)
            return send(
                made.at[slot, 1 - core, :, pl.ds(0, rows)],
                held[at].at[t],
                give_send.at[slot],
                take_recv.at[sum(held[w].shape[0] for w in range(at)) + t],
                fr=partner,
            )

        def consume(t):
            slot = lax.rem(t + base, 2)
            outgoing(t).wait_recv()
            for there in range(chips):
                held[at][t, there] = (
                    held[at][t, there].astype(F32) + made[slot, core, there, 0:rows].astype(F32)
                ).astype(BF16)
            if at in come_out:
                keep(at, t)
            for k in range(1, chips):
                there = lax.rem(chip + k, chips)
                send(
                    held[at].at[t, there],
                    come[at].at[k - 1, :, columns_of(t)],
                    far_send.at[at * (chips - 1) + k - 1],
                    far_recv.at[at * (chips - 1) + k - 1],
                    fr=there * 2 + core,
                ).start()

        def step(t, carry):
            slot = lax.rem(t + base, 2)

            @pl.when(t >= first + 2)
            def _():
                outgoing(t - 2).wait_send()

            for low in range(0, n_fr, group):
                high = min(low + group, n_fr)
                grads = product(left_t[low * rows : high * rows], right[:, columns_of(t)])
                for b in range(low, high):
                    made[slot, b % 2, b // 2, 0:rows] = grads[
                        (b - low) * rows : (b - low + 1) * rows
                    ].astype(BF16)
            outgoing(t).start()

            @pl.when(t >= first + 1)
            def _():
                consume(t - 1)

            return carry

        settle()
        lax.fori_loop(first, last, step, 0)

        def finish():
            consume(last - 1)
            outgoing(last - 2).wait_send()
            outgoing(last - 1).wait_send()

        pending.append(finish)

    loads["inner"].wait()
    loads["cot"].wait()
    reduce_weight(6, inner_v, cot_v)

    for piece in range(late_count):
        for k in range(1, chips):
            late_far[piece, k].wait_recv()
            rows = late_rows(lax.rem(chip - k + chips, chips) * 2 + core, piece)
            late_near[piece, k] = send(
                down_w.at[rows],
                down_w.at[rows],
                late_near_send.at[piece * (chips - 1) + k - 1],
                late_near_recv.at[piece * (chips - 1) + k - 1],
                fr=partner,
            )
            late_near[piece, k].start()
    for copy in late_near.values():
        copy.wait_recv()
    for copy in feed_copies(0):
        copy.start()
    loads["gate"].wait()
    loads["up"].wait()
    feed_tiles = gate_v.shape[1] // tile
    total[...] = jnp.zeros_like(total)

    def feed(t, carry):
        slot = lax.rem(t, 2)

        @pl.when(t + 1 < feed_tiles)
        def _():
            for copy in feed_copies(t + 1):
                copy.start()

        for copy in feed_copies(t):
            copy.wait()
        columns = columns_of(t)
        grad_inner = back_product(cot_v[...], down_slots[slot])
        gate = gate_v[:, columns].astype(F32)
        sigmoid = jax.nn.sigmoid(gate)
        scaled = grad_inner * sigmoid
        gate_v[:, columns] = (
            scaled * up_v[:, columns].astype(F32) * (1.0 + gate * (1.0 - sigmoid))
        ).astype(BF16)
        up_v[:, columns] = (scaled * gate).astype(BF16)
        for at in range(features // tile):
            rows = slice(at * tile, (at + 1) * tile)
            total[:, rows] += back_product(
                gate_v[:, columns], gate_slots[slot, rows, :]
            ) + back_product(up_v[:, columns], up_slots[slot, rows, :])
        return carry

    lax.fori_loop(0, feed_tiles, feed, 0)
    settle()

    blocks = delays.shape[1]
    block = frames // blocks
    loads["branch"].wait()

    def block_rows(at):
        return pl.ds(pl.multiple_of(at * block, block), block)

    def feed_norm(at, carry):
        rows = block_rows(at)
        here = branch[rows, :]
        grads = total[rows, :]
        scaling = rms_scaling(here)
        weighted = gain_rows[1:2, :] * grads
        back = scaling * weighted - here * scaling**3 * jnp.mean(weighted * here, -1, keepdims=True)
        back = cot_v[rows, :].astype(F32) + back
        branch[rows, :] = back
        low_rows[rows, :] = back.astype(BF16)
        return carry + sublane_sums(grads * here * scaling)

    feed_gain = lax.fori_loop(0, blocks, feed_norm, jnp.zeros((8, features), F32))
    feed_gain = jnp.sum(feed_gain, 0, keepdims=True)

    loads["out"].wait()

    def turn_back(t, carry):
        columns = columns_of(t)
        grad_rows[:, columns] = back_product(low_rows[...], small[0, columns, :]).astype(BF16)
        return carry

    lax.fori_loop(0, features // tile, turn_back, 0)

    def turn(k):
        peer = peer_of(pos, k, n_pos)
        return send(
            grad_rows.at[rows_of(peer, part)],
            turned.at[3, pos],
            turn_send.at[0],
            turn_recv.at[0],
            pos=peer,
        )

    def start_turn(k, carry):
        turn(k).start()
        return carry

    lax.fori_loop(1, n_pos, start_turn, 0)
    turned[3, pl.ds(pos, 1)] = grad_rows[rows_of(pos, part), :][None]
    load("query_w", query_w, small.at[0])
    load("branch_again", branch_in, total)
    load("hidden", hidden_in, cot_v)

    loads["normed_two"].wait()
    reduce_weight(4, normed_two_v, gate_v)
    load("inner_rows", inner_rows, gate_v)
    reduce_weight(5, normed_two_v, up_v)
    load("normed", normed_t, normed_two_v)
    loads["attended"].wait()
    reduce_weight(3, attended_v, low_rows)

    for name in ("queries", "keys", "values", "soft"):
        loads[name].wait()

    landed = turned.at[3, 0 : n_pos - 1]
    send(
        landed, landed, turn_send.at[0], turn_recv.at[0], pos=peer_of(pos, 1, n_pos)
    ).wait()
    settle()

    half = features // 2
    every = slice(0, features)
    groups = ((2, every), (1, every), (0, slice(0, half)), (0, slice(half, features)))

    def part_sum(group, j, low, high, weight_of, other, scale):
        which, columns = groups[group]
        sum_rows[:, columns] = jnp.zeros_like(sum_rows[:, columns])

        def add(at, carry):
            sum_rows[:, columns] += product(weight_of(at), spread[:, columns]) * turned[
                other, at, :, columns
            ].astype(F32)
            return carry

        lax.fori_loop(low, high, add, 0)
        leaving[which, j, :, columns] = (sum_rows[:, columns] * scale).astype(BF16)

        @pl.when(j != pos)
        def _():
            send(
                leaving.at[which, j, :, columns],
                arrived.at[which, rows_of(pos, part), columns],
                back_send.at[group],
                back_recv.at[group],
                pos=j,
            ).start()

        @pl.when(j == pos)
        def _():
            arrived[which, rows_of(pos, part), columns] = leaving[which, j, :, columns]

    def value_part(k, carry):
        j = peer_of(pos, k, n_pos)
        part_sum(0, j, j, n_pos, lambda p: soft[p, j].astype(BF16), 3, 1.0)
        return carry

    lax.fori_loop(1, n_pos + 1, value_part, 0)

    def score_part(p, carry):
        grads = turned[3, p].astype(F32)

        def score(j, centre):
            scores = sum_heads(grads * turned[2, j].astype(F32), sums[...])
            score_slots[j] = scores
            return centre + scores * soft[p, j]

        centre = lax.fori_loop(0, p + 1, score, jnp.zeros((part, LANES), F32))

        def level(j, carry):
            soft_grads[p, j] = (soft[p, j] * (score_slots[j] - centre)).astype(BF16)
            return carry

        return lax.fori_loop(0, p + 1, level, carry)

    lax.fori_loop(0, n_pos, score_part, 0)

    def key_part(k, carry):
        j = peer_of(pos, k, n_pos)
        part_sum(1, j, j, n_pos, lambda p: soft_grads[p, j], 0, HEAD ** (-0.5))
        return carry

    lax.fori_loop(1, n_pos + 1, key_part, 0)

    for group in (2, 3):

        def query_part(k, carry):
            p = peer_of(pos, k, n_pos)
            part_sum(group, p, 0, p + 1, lambda j: soft_grads[p, j], 1, HEAD ** (-0.5))
            return carry

        lax.fori_loop(1, n_pos + 1, query_part, 0)

    def down_copy(t):
        return feed_copies(t)[0]

    def close(t, carry):
        @pl.when(t + 1 < feed_tiles)
        def _():
            down_copy(t + 1).start()

        down_copy(t).wait()
        units = gate_v[:, columns_of(t)]
        for at in range(features // tile):
            columns = slice(at * tile, (at + 1) * tile)
            total[:, columns] += product(units, down_slots[lax.rem(t, 2), :, columns])
        return carry

    loads["normed"].wait()
    for group, slot, name in ((0, 1, "value_w"), (1, 2, "key_w"), (2, 0, "query_w"), (3, 0, None)):
        which, across = groups[group]
        landed = arrived.at[which, 0 : (n_pos - 1) * part, across]
        send(
            landed, landed, back_send.at[group], back_recv.at[group], pos=peer_of(pos, 1, n_pos)
        ).wait()
        reduce_weight(
            which, normed_two_v, arrived.at[which], across.start // tile, across.stop // tile
        )
        if which == 2:
            loads["inner_rows"].wait()
            loads["branch_again"].wait()
            down_copy(0).start()
            lax.fori_loop(0, feed_tiles, close, 0)
            grad_rows[...] = total[...].astype(BF16)
            output_copy = pltpu.make_async_copy(grad_rows, output, out_sem.at[1])
            output_copy.start()
            if 6 in early:
                gather_terms(6)
        if name:
            loads[name].wait()

        def add_normed(t, carry):
            columns = columns_of(t)
            grads = back_product(arrived[which, :, across], small[slot, columns, across])
            total[:, columns] = grads if group == 0 else total[:, columns] + grads
            return carry

        lax.fori_loop(0, features // tile, add_normed, 0)
        if which == 1 and 4 in early:
            gather_terms(4)

    loads["hidden"].wait()

    def attention_norm(at, carry):
        rows = block_rows(at)
        here = cot_v[rows, :].astype(F32)
        grads = total[rows, :]
        scaling = rms_scaling(here)
        weighted = gain_rows[0:1, :] * grads
        back = scaling * weighted - here * scaling**3 * jnp.mean(weighted * here, -1, keepdims=True)
        branch[rows, :] = branch[rows, :] + back
        return carry + sublane_sums(grads * here * scaling)

    gain = lax.fori_loop(0, blocks, attention_norm, jnp.zeros((8, features), F32))
    gain = jnp.sum(gain, 0, keepdims=True)

    first_lags = lag_of(delays, 0)
    once = jnp.where(first_lags == 1, branch[0:8, :], 0.0)
    once = jnp.where(
        lax.broadcasted_iota(jnp.int32, once.shape, 0) == 0, 0.0, pltpu.roll(once, 1, 0)
    )
    rim_out[...] = once + jnp.where(first_lags == 2, branch[0:8, :], 0.0)
    rim_copy = send(
        rim_out, rim_in, rim_sem.at[0], rim_sem.at[1], fr=lax.rem(fr + n_fr - 1, n_fr)
    )
    rim_copy.start()
    gain_pair = jnp.concatenate([gain, feed_gain, jnp.zeros((6, features), F32)], 0)
    width = features // n_fr
    for b in range(n_fr):
        gain_split[b] = gain_pair[:, b * width : (b + 1) * width]
    gain_copies = []
    for k in range(1, n_fr):
        there = lax.rem(fr + k, n_fr)
        copy = send(
            gain_split.at[there], gain_in.at[fr], gain_send.at[k], gain_recv.at[k], fr=there
        )
        copy.start()
        gain_copies.append(copy)
    gain_in[pl.ds(fr, 1)] = gain_split[pl.ds(fr, 1)]
    settle()
    for at in early:
        if at not in (6, 4):
            gather_terms(at)

    rim_copy.wait()
    rim = jnp.where(fr == n_fr - 1, 0.0, rim_in[...])

    def shift(at, carry):
        after_one, after_two = carry
        rows = block_rows(blocks - 1 - at)
        grads = branch[rows, :]
        lag = lag_of(delays, blocks - 1 - at)
        one = jnp.where(lag == 1, grads, 0.0)
        two = jnp.where(lag == 2, grads, 0.0)
        moved = pltpu.roll(jnp.concatenate([one, after_one], 0), block + 7, 0)[:block]
        moved = moved + pltpu.roll(jnp.concatenate([two, after_two], 0), block + 6, 0)[:block]
        low_rows[rows, :] = (jnp.where(lag == 0, grads, 0.0) + moved).astype(BF16)
        return one[:8], two[:8]

    lax.fori_loop(0, blocks, shift, (jnp.zeros_like(rim), rim))
    out_copy = pltpu.make_async_copy(low_rows, input_grad, out_sem.at[0])
    out_copy.start()
    for copy in gain_copies:
        copy.wait()
    gain_sum = gain_in[0]
    for b in range(1, n_fr):
        gain_sum = gain_sum + gain_in[b]
    gains_out[...] = gain_sum

    for at in range(7):
        pltpu.make_async_copy(kept_out[at], kept_out[at], kept_sem.at[at]).wait()
        for k in range(1, chips):
            arrivals(at, k).wait_send()
            if at in come_out:
                arrivals(at, k).wait_recv()
    for copy in late_far.values():
        copy.wait_send()
    for copy in late_near.values():
        copy.wait_send()
    out_copy.wait()
    output_copy.wait()


def backward_call(n_fr, n_pos, shard_shapes, *operands):
    cot = operands[3]
    frames, features = cot.shape
    part = frames // n_pos
    chips = n_fr // 2
    tile = column_tile(features)
    count = len(shard_shapes)
    shard_rows = [rows for rows, _ in shard_shapes]
    hidden_units = operands[4].shape[1]
    act = jax.ShapeDtypeStruct((frames, features), BF16)
    most = max(shard_rows)
    down = operands[-2]
    late_count = max(1, down_pieces(shard_rows[-1]) * LATE // 100)
    early, late = split_terms(chips, n_pos * frames, shard_shapes)
    come_shapes = [(chips - 1, *shape) for shape in shard_shapes]
    return pl.pallas_call(
        functools.partial(backward_kernel, n_fr, n_pos, shard_rows, early, late),
        name="backward",
        out_shape=[jax.ShapeDtypeStruct(shape, BF16) for shape in shard_shapes]
        + [jax.ShapeDtypeStruct(come_shapes[at], BF16) for at in late]
        + [act, act, jax.ShapeDtypeStruct(down.shape, BF16)]
        + [jax.ShapeDtypeStruct((8, features // n_fr), F32)],
        in_specs=[VMEM, VMEM] + [ANY] * (len(operands) - 2),
        out_specs=[ANY] * (count + len(late) + 3) + [VMEM],
        input_output_aliases={len(operands) - 2: count + len(late) + 2},
        scratch_shapes=[
            pltpu.VMEM((columns // tile, chips, rows, tile), BF16) for rows, columns in shard_shapes
        ]
        + [pltpu.VMEM(come_shapes[at], BF16) for at in early]
        + [
            pltpu.VMEM((2, 2, chips, most, tile), BF16),
            pltpu.VMEM((2, tile, features), BF16),
            pltpu.VMEM((2, features, tile), BF16),
            pltpu.VMEM((2, features, tile), BF16),
            pltpu.VMEM((3, features, features), BF16),
            pltpu.VMEM((hidden_units, frames), BF16),
            pltpu.VMEM((frames, features), BF16),
            pltpu.VMEM((frames, hidden_units), BF16),
            pltpu.VMEM((frames, hidden_units), BF16),
            pltpu.VMEM((features, frames), BF16),
            pltpu.VMEM((features, frames), BF16),
            pltpu.VMEM((frames, features), F32),
            pltpu.VMEM((frames, features), F32),
            pltpu.VMEM((frames, features), BF16),
            pltpu.VMEM((frames, features), BF16),
            pltpu.VMEM((4, n_pos, part, features), BF16),
            pltpu.VMEM((n_pos, n_pos, part, LANES), F32),
            pltpu.VMEM((n_pos, n_pos, part, LANES), BF16),
            pltpu.VMEM((n_pos, part, LANES), F32),
            pltpu.VMEM((part, features), F32),
            pltpu.VMEM((3, n_pos, part, features), BF16),
            pltpu.VMEM((3, frames, features), BF16),
            pltpu.VMEM((features, LANES), BF16),
            pltpu.VMEM((LANES, features), BF16),
            pltpu.VMEM((n_fr, 8, features // n_fr), F32),
            pltpu.VMEM((n_fr, 8, features // n_fr), F32),
            pltpu.VMEM((8, features), F32),
            pltpu.VMEM((8, features), F32),
            DMA((19,)),
            DMA((2, 3)),
            DMA((2,)),
            DMA((sum(columns // tile for _, columns in shard_shapes),)),
            DMA((count * (chips - 1),)),
            DMA((count * (chips - 1),)),
            DMA((count,)),
            DMA((1,)),
            DMA((1,)),
            DMA((4,)),
            DMA((4,)),
            DMA((n_fr,)),
            DMA((n_fr,)),
            DMA((2,)),
            DMA((2,)),
            DMA((late_count * (chips - 1),)),
            DMA((late_count * (chips - 1),)),
            DMA((late_count * (chips - 1),)),
            DMA((late_count * (chips - 1),)),
        ],
        compiler_params=pltpu.CompilerParams(
            collective_id=1, has_side_effects=True, vmem_limit_bytes=VMEM_BYTES
        ),
    )(*operands)


def finish_kernel(count, late, *refs):
    kept, refs = refs[:count], refs[count:]
    come, refs = dict(zip(late, refs)), refs[len(late) :]
    output_in, input_grad_in, gains, *refs = refs
    sums, refs = refs[:count], refs[count:]
    output, input_grad, gain_one, gain_two, *refs = refs
    kept_v, refs = refs[:count], refs[count:]
    come_v, refs = dict(zip(late, refs)), refs[len(late) :]
    sums_v, refs = refs[:count], refs[count:]
    through, load_sem, store_sem, through_sem = refs
    chunks = []
    for at in range(count):
        rows, columns = kept[at].shape
        cuts = next(
            cuts
            for cuts in (4, 2, 1)
            if rows % (16 * cuts) == 0 and (cuts == 1 or rows * columns >= cuts * 131072)
        )
        size = rows // cuts
        chunks += [(at, pl.ds(piece * size, size), piece) for piece in range(cuts)]

    order = {(at, piece): i for i, (at, _, piece) in enumerate(chunks)}

    def loads(at, rows, piece):
        copies = [
            pltpu.make_async_copy(kept[at].at[rows], kept_v[at].at[rows], load_sem.at[order[at, piece]])
        ]
        if at in come:
            copies.append(
                pltpu.make_async_copy(
                    come[at].at[:, rows], come_v[at].at[:, rows], load_sem.at[len(order) + order[at, piece]]
                )
            )
        return copies

    acts = [
        pltpu.make_async_copy(output_in, through.at[0], through_sem.at[0]),
        pltpu.make_async_copy(input_grad_in, through.at[1], through_sem.at[1]),
    ]
    for copy in acts:
        copy.start()
    for chunk in chunks:
        for copy in loads(*chunk):
            copy.start()
    gain_one[...] = gains[0:1, :]
    gain_two[...] = gains[1:2, :]
    stores = []
    for copy, leaving, slot in zip(acts, (output, input_grad), range(2)):
        copy.wait()
        stores.append(pltpu.make_async_copy(through.at[slot], leaving, through_sem.at[2 + slot]))
        stores[-1].start()
    for at, rows, piece in chunks:
        for copy in loads(at, rows, piece):
            copy.wait()
        step = 16

        def add(i, carry):
            here = pl.ds(pl.multiple_of(rows.start + i * step, step), step)
            value = kept_v[at][here, :].astype(F32)
            for k in range(come_v[at].shape[0] if at in come else 0):
                value = value + come_v[at][k, here, :].astype(F32)
            sums_v[at][here, :] = value
            return carry

        lax.fori_loop(0, rows.size // step, add, 0)
        stores.append(
            pltpu.make_async_copy(sums_v[at].at[rows], sums[at].at[rows], store_sem.at[order[at, piece]])
        )
        stores[-1].start()
    for copy in stores:
        copy.wait()


def finish_call(late, kept, come, output, input_grad, gains):
    count = len(kept)
    gain = jax.ShapeDtypeStruct((1, gains.shape[1]), F32)
    return pl.pallas_call(
        functools.partial(finish_kernel, count, late),
        name="finish",
        out_shape=[jax.ShapeDtypeStruct(own.shape, F32) for own in kept]
        + [jax.ShapeDtypeStruct(output.shape, BF16)] * 2
        + [gain, gain],
        in_specs=[ANY] * (count + len(come) + 2) + [VMEM],
        out_specs=[ANY] * (count + 2) + [VMEM, VMEM],
        scratch_shapes=[pltpu.VMEM(own.shape, BF16) for own in kept]
        + [pltpu.VMEM(others.shape, BF16) for others in come]
        + [pltpu.VMEM(own.shape, F32) for own in kept]
        + [
            pltpu.VMEM((2, *output.shape), BF16),
            DMA((2 * 3 * count,)),
            DMA((3 * count,)),
            DMA((4,)),
        ],
        compiler_params=pltpu.CompilerParams(vmem_limit_bytes=VMEM_BYTES),
    )(*kept, *come, output, input_grad, gains)


def on_device(
    inputs,
    delays,
    query_weight,
    key_weight,
    value_weight,
    out_weight,
    gate_weight,
    up_weight,
    down_weight,
    attention_gain,
    feed_gain,
    cotangent,
):
    n_fr = lax.axis_size("fr")
    n_pos = lax.axis_size("pos")
    shards = [
        weight[0]
        for weight in (
            query_weight,
            key_weight,
            value_weight,
            out_weight,
            gate_weight,
            up_weight,
            down_weight,
        )
    ]
    delays = delays.T
    results = forward_call(n_fr, n_pos, inputs[0], delays, attention_gain, feed_gain, shards)
    full, saved, gain_rows = results[:7], results[7:20], results[20]
    inner_t, *saved = saved
    grads = backward_call(
        n_fr,
        n_pos,
        [shard.shape for shard in shards],
        delays,
        gain_rows,
        inner_t,
        cotangent[0],
        *saved,
        *full,
        shards[-1],
    )
    late = split_terms(
        n_fr // 2, n_pos * inputs.shape[1], [shard.shape for shard in shards]
    )[1]
    kept, come = grads[:7], grads[7 : 7 + len(late)]
    output, input_grad, _, gain_grads = grads[7 + len(late) :]
    *sums, output, input_grad, attention_gain_grad, feed_gain_grad = finish_call(
        late, kept, come, output, input_grad, gain_grads
    )
    return (
        output[None],
        input_grad[None],
        *(total[None] for total in sums),
        attention_gain_grad,
        feed_gain_grad,
    )


def solution(mesh):
    matrix = P("pos", "fr", None)
    vector = P("pos", "fr")
    return jax.shard_map(
        on_device,
        mesh=mesh,
        in_specs=(matrix, P("fr", "pos")) + (matrix,) * 7 + (vector, vector, matrix),
        out_specs=(matrix,) * 9 + (vector, vector),
        check_vma=False,
    )
```

```python
import functools

import jax
import jax.numpy as jnp
from jax import lax
from jax.experimental import pallas as pl
from jax.experimental.pallas import tpu as pltpu
from jax.sharding import PartitionSpec as P

HEAD = 64
LANES = 128
EPSILON = 1e-06
LATE = 37
TERMS_HELD = 2750000
MESH = pl.DeviceIdType.MESH
F32 = jnp.float32
BF16 = jnp.bfloat16
ANY = pl.BlockSpec(memory_space=pl.ANY)
VMEM = pl.BlockSpec(memory_space=pltpu.VMEM)
DMA = pltpu.SemaphoreType.DMA
VMEM_BYTES = 64 * 1024 * 1024 - 65536


def greet(n_fr, n_pos):
    fr = lax.axis_index("fr")
    pos = lax.axis_index("pos")
    barrier = pltpu.get_barrier_semaphore()
    for k in range(1, n_fr):
        pl.semaphore_signal(
            barrier, inc=1, device_id={"fr": lax.rem(fr + k, n_fr)}, device_id_type=MESH
        )
    for k in range(1, n_pos):
        pl.semaphore_signal(
            barrier, inc=1, device_id={"pos": lax.rem(pos + k, n_pos)}, device_id_type=MESH
        )
    pl.semaphore_wait(barrier, n_fr + n_pos - 2)


def send(src, dst, send_sem, recv_sem, **device):
    return pltpu.make_async_remote_copy(
        src_ref=src,
        dst_ref=dst,
        send_sem=send_sem,
        recv_sem=recv_sem,
        device_id=device,
        device_id_type=MESH,
    )


def rows_of(index, rows):
    return pl.ds(pl.multiple_of(index * rows, rows), rows)


def lag_of(delays, at):
    here = lax.broadcasted_iota(jnp.int32, delays.shape, 1) == at
    return jnp.sum(jnp.where(here, delays[...].astype(F32), 0.0), 1, keepdims=True)


def head_sums(shape, feature_dim):
    features = lax.broadcasted_iota(jnp.int32, shape, feature_dim)
    heads = lax.broadcasted_iota(jnp.int32, shape, 1 - feature_dim)
    return (features // HEAD == heads).astype(BF16)


def sum_heads(product, sums):
    high = product.astype(BF16)
    low = (product - high.astype(F32)).astype(BF16)
    return jnp.dot(high, sums, preferred_element_type=F32) + jnp.dot(
        low, sums, preferred_element_type=F32
    )


def rms_scaling(values):
    return lax.rsqrt(jnp.mean(values * values, -1, keepdims=True) + EPSILON)


def product(operand, weight):
    return jnp.dot(operand, weight, preferred_element_type=F32)


def column_tile(columns):
    return 256 if columns % 256 == 0 else LANES


def multiply(rows_ref, weight_ref, out_ref):
    tile = column_tile(weight_ref.shape[1])

    def step(at, carry):
        columns = pl.ds(pl.multiple_of(at * tile, tile), tile)
        out_ref[:, columns] = jnp.dot(
            rows_ref[...], weight_ref[:, columns], preferred_element_type=F32
        ).astype(out_ref.dtype)
        return carry

    lax.fori_loop(0, weight_ref.shape[1] // tile, step, 0)


def peer_of(pos, k, n_pos):
    return lax.rem(pos + k, n_pos)


def forward_kernel(n_fr, n_pos, pieces, late, steps, *refs):
    (
        rows_in,
        delays_in,
        gain_one_in,
        gain_two_in,
        w0,
        w1,
        w2,
        w3,
        w4,
        w5,
        w6,
        o0,
        o1,
        o2,
        o3,
        o4,
        o5,
        o6,
        inner_out,
        inner_rows_out,
        gate_out,
        up_out,
        normed_two_out,
        attended_out,
        normed_out,
        branch_out,
        hidden_out,
        queries_out,
        keys_out,
        values_out,
        soft_out,
        gains_sent,
        f0,
        f1,
        f2,
        f3,
        f4,
        f5,
        f6,
        own_rows,
        rim,
        gains,
        gain_slots,
        hidden,
        normed,
        proj,
        turned,
        mixed,
        attended,
        normed_t,
        attended_t,
        normed_two_t,
        normed_two,
        inner,
        inner_t,
        gate_low,
        up_low,
        branch,
        score_slots,
        soft_slots,
        total,
        sums,
        spread,
        far_send,
        far_recv,
        near_send,
        near_recv,
        own_sem,
        out_sem,
        rim_sem,
        gain_send,
        gain_recv,
        turn_send,
        turn_recv,
        back_send,
        back_recv,
        act_sem,
        delays,
        gain_one,
        gain_two,
        gains_out,
        small_sem,
    ) = refs
    shards = (w0, w1, w2, w3, w4, w5, w6)
    full_out = (o0, o1, o2, o3, o4, o5, o6)
    full = (f0, f1, f2, f3, f4, f5, f6)
    turned_out = (queries_out, keys_out, values_out)
    fr = lax.axis_index("fr")
    pos = lax.axis_index("pos")
    chips = n_fr // 2
    chip = fr // 2
    core = lax.rem(fr, 2)
    partner = chip * 2 + 1 - core
    frames, features = own_rows.shape
    part = frames // n_pos
    smalls = [
        pltpu.make_async_copy(delays_in, delays, small_sem.at[0]),
        pltpu.make_async_copy(gain_one_in, gain_one, small_sem.at[1]),
        pltpu.make_async_copy(gain_two_in, gain_two, small_sem.at[2]),
    ]
    for copy in smalls:
        copy.start()
    greet(n_fr, n_pos)
    own_load = pltpu.make_async_copy(rows_in, own_rows, own_sem.at[len(shards)])
    own_load.start()

    edge = own_rows.shape[0] - rim.shape[0]
    rim_copy = send(
        rows_in.at[pl.ds(edge, rim.shape[0])],
        rim,
        rim_sem.at[0],
        rim_sem.at[1],
        fr=lax.rem(fr + 1, n_fr),
    )
    rim_copy.start()
    for copy in smalls:
        copy.wait()
    gains[...] = jnp.concatenate(
        [
            gain_one[...].astype(F32),
            gain_two[...].astype(F32),
            jnp.zeros((6, gains.shape[1]), F32),
        ],
        0,
    )
    gain_copies = []
    for k in range(1, n_fr):
        copy = send(
            gains,
            gain_slots.at[fr],
            gain_send.at[k],
            gain_recv.at[k],
            fr=lax.rem(fr + k, n_fr),
        )
        copy.start()
        gain_copies.append(copy)
    far = {}
    near = {}
    own = {}
    def piece_rows(at, origin, piece):
        rows = shards[at].shape[0]
        size = rows // pieces[at]
        return pl.ds(pl.multiple_of(origin * rows + piece * size, size), size)

    tile = column_tile(features)
    tiles = features // tile
    spare = sum(steps) * (chips - 1)

    def slot(at, k, piece):
        return (sum(steps[:at]) + piece) * (chips - 1) + k - 1


    def columns_of(t):
        return pl.ds(pl.multiple_of(t * tile, tile), tile)

    for t in range(tiles):
        for k in range(1, chips):
            far[0, k, t] = send(
                w0.at[:, columns_of(t)],
                f0.at[rows_of(fr, w0.shape[0]), columns_of(t)],
                far_send.at[0],
                far_recv.at[slot(0, k, t)],
                fr=lax.rem(chip + k, chips) * 2 + core,
            )
            far[0, k, t].start()
    up_tiles = w5.shape[1] // tile

    def up_far(t, k):
        return send(
            w5.at[:, columns_of(t)],
            f5.at[rows_of(fr, w5.shape[0]), columns_of(t)],
            far_send.at[5],
            far_recv.at[slot(5, k, t)],
            fr=lax.rem(chip + k, chips) * 2 + core,
        )

    def up_near(t, k):
        there = f5.at[
            rows_of(lax.rem(chip - k + chips, chips) * 2 + core, w5.shape[0]), columns_of(t)
        ]
        return send(there, there, near_send.at[5], near_recv.at[slot(5, k, t)], fr=partner)

    def up_start(t, carry):
        for k in range(1, chips):
            up_far(t, k).start()
        return carry

    for at, (shard, whole) in enumerate(zip(shards, full)):
        if at == 5:
            lax.fori_loop(0, up_tiles, up_start, 0)
        mine = rows_of(fr, shard.shape[0])
        size = shard.shape[0] // pieces[at]
        for piece in range(0 if at in (0, 5) else pieces[at] - late[at]):
            for k in range(1, chips):
                far[at, k, piece] = send(
                    shard.at[piece * size : (piece + 1) * size],
                    whole.at[piece_rows(at, fr, piece)],
                    far_send.at[at],
                    far_recv.at[slot(at, k, piece)],
                    fr=lax.rem(chip + k, chips) * 2 + core,
                )
                far[at, k, piece].start()
        near[at, 0, 0] = send(
            shard, whole.at[mine], near_send.at[at], near_recv.at[spare + at], fr=partner
        )
        if at < 3:
            near[at, 0, 0].start()
        own[at] = pltpu.make_async_copy(shard, whole.at[mine], own_sem.at[at])
        own[at].start()

    sums[...] = head_sums(sums.shape, 0)
    spread[...] = head_sums(spread.shape, 1)
    gain_slots[pl.ds(fr, 1)] = gains[...][None]
    for copy in gain_copies:
        copy.wait()
    gain_row = jnp.concatenate([gain_slots[at, 0:1, :] for at in range(n_fr)], 1)
    gains_out[...] = jnp.concatenate([gain_slots[at] for at in range(n_fr)], 1)
    rim_copy.wait()
    own_load.wait()

    block = frames // delays.shape[1]
    rim_rows = rim.shape[0]
    rim_all = jnp.where(fr == 0, 0.0, rim[...].astype(F32))[rim_rows - 8 :]

    def norm_block(at, carry):
        rows = pl.ds(pl.multiple_of(at * block, block), block)
        here = own_rows[rows, :].astype(F32)
        window = jnp.concatenate([carry, here], 0)
        once = pltpu.roll(window, 1, 0)[8:]
        twice = pltpu.roll(window, 2, 0)[8:]
        lag = lag_of(delays, at)
        values = jnp.where(lag == 0, here, jnp.where(lag == 1, once, twice))
        hidden[rows, :] = values.astype(BF16)
        scaling = lax.rsqrt(jnp.mean(values * values, -1, keepdims=True) + EPSILON)
        normed[rows, :] = (values * scaling * gain_row).astype(BF16)
        return here[block - 8 :]

    lax.fori_loop(0, frames // block, norm_block, rim_all)
    act_copies = []

    def put(src, dst):
        act_copies.append(pltpu.make_async_copy(src, dst, act_sem.at[len(act_copies)]))
        act_copies[-1].start()

    put(hidden, hidden_out)
    put(gains_out, gains_sent)

    outs = {}

    def pass_on(at, piece=0):
        for k in range(1, chips):
            far[at, k, piece].wait_recv()
            origin = lax.rem(chip - k + chips, chips) * 2 + core
            rows = piece_rows(at, origin, piece)
            near[at, k, piece] = send(
                full[at].at[rows],
                full[at].at[rows],
                near_send.at[at],
                near_recv.at[slot(at, k, piece)],
                fr=partner,
            )
            near[at, k, piece].start()

    def complete(at):
        own[at].wait()
        for k in range(chips):
            near[at, k, 0].wait_recv()
        outs[at] = pltpu.make_async_copy(full[at], full_out[at], out_sem.at[at])
        outs[at].start()

    def finish_pieces(at):
        early = range(pieces[at] - late[at])
        rows = shards[at].shape[0]
        size = rows // pieces[at]

        def put_rows(where):
            pltpu.make_async_copy(
                full[at].at[where], full_out[at].at[where], out_sem.at[at]
            ).start()

        own[at].wait()
        put_rows(rows_of(fr, rows))
        near[at, 0, 0].wait_recv()
        put_rows(rows_of(partner, rows))
        for piece in early:
            pass_on(at, piece)
            for k in range(1, chips):
                put_rows(piece_rows(at, lax.rem(chip - k + chips, chips) * 2 + core, piece))
        for piece in early:
            for k in range(1, chips):
                near[at, k, piece].wait_recv()
                put_rows(piece_rows(at, lax.rem(chip - k + chips, chips) * 2 + 1 - core, piece))
        written = full_out[at].at[0 : n_fr * rows - 2 * (chips - 1) * late[at] * size]
        outs[at] = pltpu.make_async_copy(written, written, out_sem.at[at])

    def turn(which, k):
        peer = peer_of(pos, k, n_pos)
        return send(
            proj.at[which, rows_of(peer, part)],
            turned.at[which, pos],
            turn_send.at[which],
            turn_recv.at[which],
            pos=peer,
        )

    own[0].wait()
    near[0, 0, 0].wait_recv()
    for t in range(tiles):
        for k in range(1, chips):
            far[0, k, t].wait_recv()
            origin = lax.rem(chip - k + chips, chips) * 2 + core
            there = f0.at[rows_of(origin, w0.shape[0]), columns_of(t)]
            near[0, k, t] = send(
                there, there, near_send.at[0], near_recv.at[slot(0, k, t)], fr=partner
            )
            near[0, k, t].start()
        for k in range(1, chips):
            near[0, k, t].wait_recv()
        proj[0, :, columns_of(t)] = product(normed[...], f0[:, columns_of(t)]).astype(BF16)

        def start_tile(k, carry):
            peer = peer_of(pos, k, n_pos)
            send(
                proj.at[0, rows_of(peer, part), columns_of(t)],
                turned.at[0, pos, :, columns_of(t)],
                turn_send.at[0],
                turn_recv.at[0],
                pos=peer,
            ).start()
            return carry

        lax.fori_loop(1, n_pos, start_tile, 0)
    turned[0, pl.ds(pos, 1)] = proj[0, rows_of(pos, part), :][None]
    outs[0] = pltpu.make_async_copy(f0, o0, out_sem.at[0])
    outs[0].start()
    for which in (1, 2):
        pass_on(which)
        complete(which)
        multiply(normed, full[which], proj.at[which])

        def start_turn(k, carry):
            turn(which, k).start()
            return carry

        lax.fori_loop(1, n_pos, start_turn, 0)
        turned[which, pl.ds(pos, 1)] = proj[which, rows_of(pos, part), :][None]

    for at in range(3, 7):
        near[at, 0, 0].start()

    def transpose(src, dst):
        tile = column_tile(src.shape[1])

        def step(t, carry):
            at = pl.ds(pl.multiple_of(t * tile, tile), tile)
            dst[at, :] = src[:, at].T
            return carry

        lax.fori_loop(0, src.shape[1] // tile, step, 0)

    transpose(normed, normed_t)
    put(normed_t, normed_out)
    pass_on(3)

    def end_turns(which):
        landed = turned.at[which, 0 : n_pos - 1]
        send(
            landed,
            landed,
            turn_send.at[which],
            turn_recv.at[which],
            pos=peer_of(pos, 1, n_pos),
        ).wait()
        put(turned.at[which], turned_out[which])

    end_turns(0)
    end_turns(1)

    def score_rows(p, carry):
        query = turned[0, p].astype(F32) * HEAD ** (-0.5)

        def score(j, highest):
            scores = sum_heads(query * turned[1, j].astype(F32), sums[...])
            score_slots[j] = scores
            return jnp.maximum(highest, scores)

        highest = lax.fori_loop(0, p + 1, score, jnp.full((part, LANES), -1e30, F32))

        def weigh(j, mass):
            return mass + jnp.exp(score_slots[j] - highest)

        mass = lax.fori_loop(0, p + 1, weigh, jnp.zeros((part, LANES), F32))
        logsum = highest + jnp.log(mass)

        def level(j, carry):
            soft_slots[p, j] = jnp.exp(score_slots[j] - logsum)
            return carry

        return lax.fori_loop(0, p + 1, level, carry)

    lax.fori_loop(0, n_pos, score_rows, 0)
    put(soft_slots, soft_out)
    pass_on(4)
    end_turns(2)

    def back(p):
        return send(
            mixed.at[p],
            attended.at[rows_of(pos, part)],
            back_send.at[0],
            back_recv.at[0],
            pos=p,
        )

    def mix_rows(k, carry):
        p = peer_of(pos, k, n_pos)
        total[...] = jnp.zeros_like(total)

        def mix(j, carry):
            total[...] += product(soft_slots[p, j].astype(BF16), spread[...]) * turned[
                2, j
            ].astype(F32)
            return carry

        lax.fori_loop(0, p + 1, mix, 0)
        mixed[p] = total[...].astype(BF16)

        @pl.when(p != pos)
        def _():
            back(p).start()

        @pl.when(p == pos)
        def _():
            attended[rows_of(pos, part), :] = mixed[p]

        return carry

    lax.fori_loop(1, n_pos + 1, mix_rows, 0)
    complete(3)
    complete(4)

    landed = mixed.at[0 : n_pos - 1]
    send(
        landed, landed, back_send.at[0], back_recv.at[0], pos=peer_of(pos, 1, n_pos)
    ).wait()
    def leave(t, carry):
        columns = columns_of(t)
        branch[:, columns] = hidden[:, columns].astype(F32) + product(
            attended[...], full[3][:, columns]
        )
        return carry

    lax.fori_loop(0, features // tile, leave, 0)
    put(branch, branch_out)
    feed_gain = gains_out[1:2, :]

    def norm_two(at, carry):
        rows = pl.ds(pl.multiple_of(at * block, block), block)
        here = branch[rows, :]
        normed_two[rows, :] = (here * rms_scaling(here) * feed_gain).astype(BF16)
        return carry

    lax.fori_loop(0, frames // block, norm_two, 0)

    transpose(attended, attended_t)
    put(attended_t, attended_out)
    transpose(normed_two, normed_two_t)
    put(normed_two_t, normed_two_out)

    def up_pass(t):
        for k in range(1, chips):
            up_far(t, k).wait_recv()
            up_near(t, k).start()

    def up_put(t):
        return pltpu.make_async_copy(
            f5.at[:, columns_of(t)], o5.at[:, columns_of(t)], out_sem.at[5]
        )

    own[5].wait()
    near[5, 0, 0].wait_recv()
    up_pass(0)

    def feed(t, carry):
        columns = columns_of(t)

        @pl.when(t + 1 < up_tiles)
        def _():
            up_pass(t + 1)

        for k in range(1, chips):
            up_near(t, k).wait_recv()
        up_put(t).start()
        gate = product(normed_two[...], full[4][:, columns])
        up = product(normed_two[...], full[5][:, columns])
        gate_low[:, columns] = gate.astype(BF16)
        up_low[:, columns] = up.astype(BF16)
        low = (gate * jax.nn.sigmoid(gate) * up).astype(BF16)
        inner[:, columns] = low
        inner_t[columns, :] = low.T
        return carry

    lax.fori_loop(0, inner.shape[1] // tile, feed, 0)
    put(gate_low, gate_out)
    put(up_low, up_out)
    put(inner_t, inner_out)
    put(inner, inner_rows_out)
    finish_pieces(6)
    pltpu.make_async_copy(o5, o5, out_sem.at[5]).wait()
    for at in range(len(shards)):
        rows = shards[at].shape[0]
        early = (chips - 1) * (rows - late[at] * (rows // pieces[at]))
        gone = full[at].at[0:early]
        send(gone, gone, far_send.at[at], near_recv.at[0], fr=partner).wait_send()
        gone = full[at].at[0 : early + rows]
        send(gone, gone, near_send.at[at], near_recv.at[0], fr=partner).wait_send()
    for copy in outs.values():
        copy.wait()
    for copy in act_copies:
        copy.wait()


def down_pieces(rows):
    return next(cuts for cuts in (11, 8, 4, 2, 1) if rows % (16 * cuts) == 0)


def forward_call(n_fr, n_pos, own_rows, delays, gain_one, gain_two, shards):
    frames, features = own_rows.shape
    part = frames // n_pos
    count = len(shards)
    chips = n_fr // 2
    width = gain_one.shape[1]
    last = down_pieces(shards[-1].shape[0])
    pieces = [1] * (count - 1) + [last]
    late = [0] * (count - 1) + [last * LATE // 100]
    tile = column_tile(features)
    steps = [1] * (count - 1) + [last - late[-1]]
    steps[0] = features // tile
    steps[5] = shards[5].shape[1] // tile
    copies = sum(steps) * (chips - 1)
    full = [(n_fr * shard.shape[0], shard.shape[1]) for shard in shards]
    hidden_units = shards[4].shape[1]
    act = jax.ShapeDtypeStruct((frames, features), BF16)
    act_t = jax.ShapeDtypeStruct((features, frames), BF16)
    wide = jax.ShapeDtypeStruct((frames, hidden_units), BF16)
    wide_t = jax.ShapeDtypeStruct((hidden_units, frames), BF16)
    turned = jax.ShapeDtypeStruct((n_pos, part, features), BF16)
    return pl.pallas_call(
        functools.partial(forward_kernel, n_fr, n_pos, pieces, late, steps),
        name="forward",
        out_shape=[jax.ShapeDtypeStruct(shape, BF16) for shape in full]
        + [wide_t, wide, wide, wide, act_t, act_t, act_t]
        + [jax.ShapeDtypeStruct((frames, features), F32), act, turned, turned, turned]
        + [
            jax.ShapeDtypeStruct((n_pos, n_pos, part, LANES), F32),
            jax.ShapeDtypeStruct((8, features), F32),
        ],
        in_specs=[ANY] * (count + 4),
        out_specs=[ANY] * (count + 14),
        scratch_shapes=[pltpu.VMEM(shape, BF16) for shape in full]
        + [
            pltpu.VMEM((frames, features), BF16),
            pltpu.VMEM((16, features), BF16),
            pltpu.VMEM((8, width), F32),
            pltpu.VMEM((n_fr, 8, width), F32),
            pltpu.VMEM((frames, features), BF16),
            pltpu.VMEM((frames, features), BF16),
            pltpu.VMEM((3, frames, features), BF16),
            pltpu.VMEM((3, n_pos, part, features), BF16),
            pltpu.VMEM((n_pos, part, features), BF16),
            pltpu.VMEM((frames, features), BF16),
            pltpu.VMEM((features, frames), BF16),
            pltpu.VMEM((features, frames), BF16),
            pltpu.VMEM((features, frames), BF16),
            pltpu.VMEM((frames, features), BF16),
            pltpu.VMEM((frames, hidden_units), BF16),
            pltpu.VMEM((hidden_units, frames), BF16),
            pltpu.VMEM((frames, hidden_units), BF16),
            pltpu.VMEM((frames, hidden_units), BF16),
            pltpu.VMEM((frames, features), F32),
            pltpu.VMEM((n_pos, part, LANES), F32),
            pltpu.VMEM((n_pos, n_pos, part, LANES), F32),
            pltpu.VMEM((part, features), F32),
            pltpu.VMEM((features, LANES), BF16),
            pltpu.VMEM((LANES, features), BF16),
            DMA((count,)),
            DMA((copies,)),
            DMA((count,)),
            DMA((copies + count,)),
            DMA((count + 1,)),
            DMA((count,)),
            DMA((2,)),
            DMA((n_fr,)),
            DMA((n_fr,)),
            DMA((3,)),
            DMA((3,)),
            DMA((1,)),
            DMA((1,)),
            DMA((15,)),
            pltpu.VMEM(delays.shape, jnp.int32),
            pltpu.VMEM(gain_one.shape, BF16),
            pltpu.VMEM(gain_two.shape, BF16),
            pltpu.VMEM((8, features), F32),
            DMA((3,)),
        ],
        compiler_params=pltpu.CompilerParams(
            collective_id=0, has_side_effects=True, vmem_limit_bytes=VMEM_BYTES
        ),
    )(own_rows, delays, gain_one, gain_two, *shards)


def back_product(grad_rows, weight):
    return lax.dot_general(grad_rows, weight, (((1,), (1,)), ((), ())), preferred_element_type=F32)


def sublane_sums(values):
    rows, features = values.shape
    return jnp.sum(values.reshape(rows // 8, 8, features), 0)


def split_terms(chips, spread_rows, shapes):
    early = []
    room = TERMS_HELD + 3 * LANES * (4096 - spread_rows)
    for at in (6, 4, 5, 3, 2):
        room -= (chips - 1) * shapes[at][0] * shapes[at][1]
        if room < 0:
            break
        early.append(at)
    return early, [at for at in range(len(shapes)) if at not in early]


def backward_kernel(n_fr, n_pos, shard_rows, early, late, *refs):
    (
        delays_in,
        gain_rows_in,
        inner_t,
        cot,
        inner_rows,
        gate_low,
        up_low,
        normed_two_t,
        attended_t,
        normed_t,
        branch_in,
        hidden_in,
        queries,
        keys,
        values,
        soft_in,
        *weights,
    ) = refs[:24]
    kept_out = refs[24:31]
    refs = refs[31:]
    come_out, refs = dict(zip(late, refs)), refs[len(late) :]
    output, input_grad, down_w, gains_sent, *refs = refs
    held, refs = refs[:7], refs[7:]
    come, refs = dict(zip(early, refs)), refs[len(early) :]
    come.update(come_out)
    (
        made,
        down_slots,
        gate_slots,
        up_slots,
        small,
        inner_v,
        cot_v,
        gate_v,
        up_v,
        normed_two_v,
        attended_v,
        branch,
        total,
        low_rows,
        grad_rows,
        turned,
        soft,
        soft_grads,
        score_slots,
        sum_rows,
        leaving,
        arrived,
        sums,
        spread,
        gain_split,
        gain_in,
        rim_out,
        rim_in,
        load_sem,
        stream_sem,
        give_send,
        take_recv,
        far_send,
        far_recv,
        kept_sem,
        turn_send,
        turn_recv,
        back_send,
        back_recv,
        gain_send,
        gain_recv,
        rim_sem,
        out_sem,
        late_far_send,
        late_far_recv,
        late_near_send,
        late_near_recv,
        delays,
        gain_rows,
        gains_out,
    ) = refs
    query_w, key_w, value_w, out_w, gate_w, up_w, _, down_shard = weights
    fr = lax.axis_index("fr")
    pos = lax.axis_index("pos")
    chips = n_fr // 2
    chip = fr // 2
    core = lax.rem(fr, 2)
    partner = chip * 2 + 1 - core
    frames, features = cot.shape
    part = frames // n_pos
    tile = made.shape[-1]
    greet(n_fr, n_pos)

    down_rows = down_shard.shape[0]
    cuts = down_pieces(down_rows)
    size = down_rows // cuts
    late_count = cuts * LATE // 100
    late_far = {}
    late_near = {}

    def late_rows(origin, piece):
        start = origin * down_rows + (cuts - late_count + piece) * size
        return pl.ds(pl.multiple_of(start, size), size)

    for piece in range(late_count):
        for k in range(1, chips):
            late_far[piece, k] = send(
                down_shard.at[pl.ds((cuts - late_count + piece) * size, size)],
                down_w.at[late_rows(fr, piece)],
                late_far_send.at[piece * (chips - 1) + k - 1],
                late_far_recv.at[piece * (chips - 1) + k - 1],
                fr=lax.rem(chip + k, chips) * 2 + core,
            )
            late_far[piece, k].start()

    loads = {}

    def load(name, src, dst):
        loads[name] = pltpu.make_async_copy(src, dst, load_sem.at[len(loads)])
        loads[name].start()

    def columns_of(t):
        return pl.ds(pl.multiple_of(t * tile, tile), tile)

    def feed_copies(t):
        slot = lax.rem(t, 2)
        return (
            pltpu.make_async_copy(
                down_w.at[columns_of(t)], down_slots.at[slot], stream_sem.at[slot, 0]
            ),
            pltpu.make_async_copy(
                gate_w.at[:, columns_of(t)], gate_slots.at[slot], stream_sem.at[slot, 1]
            ),
            pltpu.make_async_copy(
                up_w.at[:, columns_of(t)], up_slots.at[slot], stream_sem.at[slot, 2]
            ),
        )

    load("delays", delays_in, delays)
    load("gain_rows", gain_rows_in, gain_rows)
    load("inner", inner_t, inner_v)
    load("cot", cot, cot_v)
    load("gate", gate_low, gate_v)
    load("up", up_low, up_v)
    load("branch", branch_in, branch)
    load("out", out_w, small.at[0])
    load("normed_two", normed_two_t, normed_two_v)
    load("attended", attended_t, attended_v)
    load("queries", queries, turned.at[0])
    load("keys", keys, turned.at[1])
    load("values", values, turned.at[2])
    load("soft", soft_in, soft)
    load("value_w", value_w, small.at[1])
    load("key_w", key_w, small.at[2])
    sums[...] = head_sums(sums.shape, 0)
    spread[...] = head_sums(spread.shape, 1)

    pending = []
    done = [0]

    def settle():
        while pending:
            pending.pop(0)()

    def keep(at, t):
        pltpu.make_async_copy(
            held[at].at[t, chip], kept_out[at].at[:, columns_of(t)], kept_sem.at[at]
        ).start()

    def arrivals(at, k):
        return send(
            come[at].at[k - 1],
            come[at].at[k - 1],
            far_send.at[at * (chips - 1) + k - 1],
            far_recv.at[at * (chips - 1) + k - 1],
            fr=lax.rem(chip + k, chips) * 2 + core,
        )

    def gather_terms(at):
        for k in range(1, chips):
            arrivals(at, k).wait_recv()

        def add(t, carry):
            value = held[at][t, chip].astype(F32)
            for k in range(1, chips):
                value = value + come[at][k - 1, :, columns_of(t)].astype(F32)
            held[at][t, chip] = value.astype(BF16)
            keep(at, t)
            return carry

        lax.fori_loop(0, held[at].shape[0], add, 0)

    def reduce_weight(at, left_t, right, first=0, last=None):
        rows = shard_rows[at]
        last = last or right.shape[1] // tile
        base = done[0] + first
        done[0] += last - first
        group = max(1, 1024 // rows)

        def outgoing(t):
            slot = lax.rem(t + base, 2)
            return send(
                made.at[slot, 1 - core, :, pl.ds(0, rows)],
                held[at].at[t],
                give_send.at[slot],
                take_recv.at[sum(held[w].shape[0] for w in range(at)) + t],
                fr=partner,
            )

        def consume(t):
            slot = lax.rem(t + base, 2)
            outgoing(t).wait_recv()
            for there in range(chips):
                held[at][t, there] = (
                    held[at][t, there].astype(F32) + made[slot, core, there, 0:rows].astype(F32)
                ).astype(BF16)
            if at in come_out:
                keep(at, t)
            for k in range(1, chips):
                there = lax.rem(chip + k, chips)
                send(
                    held[at].at[t, there],
                    come[at].at[k - 1, :, columns_of(t)],
                    far_send.at[at * (chips - 1) + k - 1],
                    far_recv.at[at * (chips - 1) + k - 1],
                    fr=there * 2 + core,
                ).start()

        def step(t, carry):
            slot = lax.rem(t + base, 2)

            @pl.when(t >= first + 2)
            def _():
                outgoing(t - 2).wait_send()

            for low in range(0, n_fr, group):
                high = min(low + group, n_fr)
                grads = product(left_t[low * rows : high * rows], right[:, columns_of(t)])
                for b in range(low, high):
                    made[slot, b % 2, b // 2, 0:rows] = grads[
                        (b - low) * rows : (b - low + 1) * rows
                    ].astype(BF16)
            outgoing(t).start()

            @pl.when(t >= first + 1)
            def _():
                consume(t - 1)

            return carry

        settle()
        lax.fori_loop(first, last, step, 0)

        def finish():
            consume(last - 1)
            outgoing(last - 2).wait_send()
            outgoing(last - 1).wait_send()

        pending.append(finish)

    loads["delays"].wait()
    loads["gain_rows"].wait()
    loads["inner"].wait()
    loads["cot"].wait()
    reduce_weight(6, inner_v, cot_v)

    for piece in range(late_count):
        for k in range(1, chips):
            late_far[piece, k].wait_recv()
            rows = late_rows(lax.rem(chip - k + chips, chips) * 2 + core, piece)
            late_near[piece, k] = send(
                down_w.at[rows],
                down_w.at[rows],
                late_near_send.at[piece * (chips - 1) + k - 1],
                late_near_recv.at[piece * (chips - 1) + k - 1],
                fr=partner,
            )
            late_near[piece, k].start()
    for copy in late_near.values():
        copy.wait_recv()
    for copy in feed_copies(0):
        copy.start()
    loads["gate"].wait()
    loads["up"].wait()
    feed_tiles = gate_v.shape[1] // tile
    total[...] = jnp.zeros_like(total)

    def feed(t, carry):
        slot = lax.rem(t, 2)

        @pl.when(t + 1 < feed_tiles)
        def _():
            for copy in feed_copies(t + 1):
                copy.start()

        for copy in feed_copies(t):
            copy.wait()
        columns = columns_of(t)
        grad_inner = back_product(cot_v[...], down_slots[slot])
        gate = gate_v[:, columns].astype(F32)
        sigmoid = jax.nn.sigmoid(gate)
        scaled = grad_inner * sigmoid
        gate_v[:, columns] = (
            scaled * up_v[:, columns].astype(F32) * (1.0 + gate * (1.0 - sigmoid))
        ).astype(BF16)
        up_v[:, columns] = (scaled * gate).astype(BF16)
        for at in range(features // tile):
            rows = slice(at * tile, (at + 1) * tile)
            total[:, rows] += back_product(
                gate_v[:, columns], gate_slots[slot, rows, :]
            ) + back_product(up_v[:, columns], up_slots[slot, rows, :])
        return carry

    lax.fori_loop(0, feed_tiles, feed, 0)
    settle()

    blocks = delays.shape[1]
    block = frames // blocks
    loads["branch"].wait()

    def block_rows(at):
        return pl.ds(pl.multiple_of(at * block, block), block)

    def feed_norm(at, carry):
        rows = block_rows(at)
        here = branch[rows, :]
        grads = total[rows, :]
        scaling = rms_scaling(here)
        weighted = gain_rows[1:2, :] * grads
        back = scaling * weighted - here * scaling**3 * jnp.mean(weighted * here, -1, keepdims=True)
        back = cot_v[rows, :].astype(F32) + back
        branch[rows, :] = back
        low_rows[rows, :] = back.astype(BF16)
        return carry + sublane_sums(grads * here * scaling)

    feed_gain = lax.fori_loop(0, blocks, feed_norm, jnp.zeros((8, features), F32))
    feed_gain = jnp.sum(feed_gain, 0, keepdims=True)

    loads["out"].wait()

    def turn_back(t, carry):
        columns = columns_of(t)
        grad_rows[:, columns] = back_product(low_rows[...], small[0, columns, :]).astype(BF16)
        return carry

    lax.fori_loop(0, features // tile, turn_back, 0)

    def turn(k):
        peer = peer_of(pos, k, n_pos)
        return send(
            grad_rows.at[rows_of(peer, part)],
            turned.at[3, pos],
            turn_send.at[0],
            turn_recv.at[0],
            pos=peer,
        )

    def start_turn(k, carry):
        turn(k).start()
        return carry

    lax.fori_loop(1, n_pos, start_turn, 0)
    turned[3, pl.ds(pos, 1)] = grad_rows[rows_of(pos, part), :][None]
    load("query_w", query_w, small.at[0])
    load("branch_again", branch_in, total)
    load("hidden", hidden_in, cot_v)

    loads["normed_two"].wait()
    reduce_weight(4, normed_two_v, gate_v)
    load("inner_rows", inner_rows, gate_v)
    reduce_weight(5, normed_two_v, up_v)
    load("normed", normed_t, normed_two_v)
    loads["attended"].wait()
    reduce_weight(3, attended_v, low_rows)

    for name in ("queries", "keys", "values", "soft"):
        loads[name].wait()

    landed = turned.at[3, 0 : n_pos - 1]
    send(
        landed, landed, turn_send.at[0], turn_recv.at[0], pos=peer_of(pos, 1, n_pos)
    ).wait()
    settle()

    half = features // 2
    every = slice(0, features)
    groups = ((2, every), (1, every), (0, slice(0, half)), (0, slice(half, features)))

    def part_sum(group, j, low, high, weight_of, other, scale):
        which, columns = groups[group]
        sum_rows[:, columns] = jnp.zeros_like(sum_rows[:, columns])

        def add(at, carry):
            sum_rows[:, columns] += product(weight_of(at), spread[:, columns]) * turned[
                other, at, :, columns
            ].astype(F32)
            return carry

        lax.fori_loop(low, high, add, 0)
        leaving[which, j, :, columns] = (sum_rows[:, columns] * scale).astype(BF16)

        @pl.when(j != pos)
        def _():
            send(
                leaving.at[which, j, :, columns],
                arrived.at[which, rows_of(pos, part), columns],
                back_send.at[group],
                back_recv.at[group],
                pos=j,
            ).start()

        @pl.when(j == pos)
        def _():
            arrived[which, rows_of(pos, part), columns] = leaving[which, j, :, columns]

    def value_part(k, carry):
        j = peer_of(pos, k, n_pos)
        part_sum(0, j, j, n_pos, lambda p: soft[p, j].astype(BF16), 3, 1.0)
        return carry

    lax.fori_loop(1, n_pos + 1, value_part, 0)

    def score_part(p, carry):
        grads = turned[3, p].astype(F32)

        def score(j, centre):
            scores = sum_heads(grads * turned[2, j].astype(F32), sums[...])
            score_slots[j] = scores
            return centre + scores * soft[p, j]

        centre = lax.fori_loop(0, p + 1, score, jnp.zeros((part, LANES), F32))

        def level(j, carry):
            soft_grads[p, j] = (soft[p, j] * (score_slots[j] - centre)).astype(BF16)
            return carry

        return lax.fori_loop(0, p + 1, level, carry)

    lax.fori_loop(0, n_pos, score_part, 0)

    def key_part(k, carry):
        j = peer_of(pos, k, n_pos)
        part_sum(1, j, j, n_pos, lambda p: soft_grads[p, j], 0, HEAD ** (-0.5))
        return carry

    lax.fori_loop(1, n_pos + 1, key_part, 0)

    for group in (2, 3):

        def query_part(k, carry):
            p = peer_of(pos, k, n_pos)
            part_sum(group, p, 0, p + 1, lambda j: soft_grads[p, j], 1, HEAD ** (-0.5))
            return carry

        lax.fori_loop(1, n_pos + 1, query_part, 0)

    def down_copy(t):
        return feed_copies(t)[0]

    def close(t, carry):
        @pl.when(t + 1 < feed_tiles)
        def _():
            down_copy(t + 1).start()

        down_copy(t).wait()
        units = gate_v[:, columns_of(t)]
        for at in range(features // tile):
            columns = slice(at * tile, (at + 1) * tile)
            total[:, columns] += product(units, down_slots[lax.rem(t, 2), :, columns])
        return carry

    loads["normed"].wait()
    for group, slot, name in ((0, 1, "value_w"), (1, 2, "key_w"), (2, 0, "query_w"), (3, 0, None)):
        which, across = groups[group]
        landed = arrived.at[which, 0 : (n_pos - 1) * part, across]
        send(
            landed, landed, back_send.at[group], back_recv.at[group], pos=peer_of(pos, 1, n_pos)
        ).wait()
        reduce_weight(
            which, normed_two_v, arrived.at[which], across.start // tile, across.stop // tile
        )
        if which == 2:
            loads["inner_rows"].wait()
            loads["branch_again"].wait()
            down_copy(0).start()
            lax.fori_loop(0, feed_tiles, close, 0)
            grad_rows[...] = total[...].astype(BF16)
            output_copy = pltpu.make_async_copy(grad_rows, output, out_sem.at[1])
            output_copy.start()
            if 6 in early:
                gather_terms(6)
        if name:
            loads[name].wait()

        def add_normed(t, carry):
            columns = columns_of(t)
            grads = back_product(arrived[which, :, across], small[slot, columns, across])
            total[:, columns] = grads if group == 0 else total[:, columns] + grads
            return carry

        lax.fori_loop(0, features // tile, add_normed, 0)
        if which == 1 and 4 in early:
            gather_terms(4)

    loads["hidden"].wait()

    def attention_norm(at, carry):
        rows = block_rows(at)
        here = cot_v[rows, :].astype(F32)
        grads = total[rows, :]
        scaling = rms_scaling(here)
        weighted = gain_rows[0:1, :] * grads
        back = scaling * weighted - here * scaling**3 * jnp.mean(weighted * here, -1, keepdims=True)
        branch[rows, :] = branch[rows, :] + back
        return carry + sublane_sums(grads * here * scaling)

    gain = lax.fori_loop(0, blocks, attention_norm, jnp.zeros((8, features), F32))
    gain = jnp.sum(gain, 0, keepdims=True)

    first_lags = lag_of(delays, 0)
    once = jnp.where(first_lags == 1, branch[0:8, :], 0.0)
    once = jnp.where(
        lax.broadcasted_iota(jnp.int32, once.shape, 0) == 0, 0.0, pltpu.roll(once, 1, 0)
    )
    rim_out[...] = once + jnp.where(first_lags == 2, branch[0:8, :], 0.0)
    rim_copy = send(
        rim_out, rim_in, rim_sem.at[0], rim_sem.at[1], fr=lax.rem(fr + n_fr - 1, n_fr)
    )
    rim_copy.start()
    gain_pair = jnp.concatenate([gain, feed_gain, jnp.zeros((6, features), F32)], 0)
    width = features // n_fr
    for b in range(n_fr):
        gain_split[b] = gain_pair[:, b * width : (b + 1) * width]
    gain_copies = []
    for k in range(1, n_fr):
        there = lax.rem(fr + k, n_fr)
        copy = send(
            gain_split.at[there], gain_in.at[fr], gain_send.at[k], gain_recv.at[k], fr=there
        )
        copy.start()
        gain_copies.append(copy)
    gain_in[pl.ds(fr, 1)] = gain_split[pl.ds(fr, 1)]
    settle()
    for at in early:
        if at not in (6, 4):
            gather_terms(at)

    rim_copy.wait()
    rim = jnp.where(fr == n_fr - 1, 0.0, rim_in[...])

    def shift(at, carry):
        after_one, after_two = carry
        rows = block_rows(blocks - 1 - at)
        grads = branch[rows, :]
        lag = lag_of(delays, blocks - 1 - at)
        one = jnp.where(lag == 1, grads, 0.0)
        two = jnp.where(lag == 2, grads, 0.0)
        moved = pltpu.roll(jnp.concatenate([one, after_one], 0), block + 7, 0)[:block]
        moved = moved + pltpu.roll(jnp.concatenate([two, after_two], 0), block + 6, 0)[:block]
        low_rows[rows, :] = (jnp.where(lag == 0, grads, 0.0) + moved).astype(BF16)
        return one[:8], two[:8]

    lax.fori_loop(0, blocks, shift, (jnp.zeros_like(rim), rim))
    out_copy = pltpu.make_async_copy(low_rows, input_grad, out_sem.at[0])
    out_copy.start()
    for copy in gain_copies:
        copy.wait()
    gain_sum = gain_in[0]
    for b in range(1, n_fr):
        gain_sum = gain_sum + gain_in[b]
    gains_out[...] = gain_sum
    gains_copy = pltpu.make_async_copy(gains_out, gains_sent, out_sem.at[2])
    gains_copy.start()

    for at in range(7):
        pltpu.make_async_copy(kept_out[at], kept_out[at], kept_sem.at[at]).wait()
        for k in range(1, chips):
            arrivals(at, k).wait_send()
            if at in come_out:
                arrivals(at, k).wait_recv()
    for copy in late_far.values():
        copy.wait_send()
    for copy in late_near.values():
        copy.wait_send()
    out_copy.wait()
    output_copy.wait()
    gains_copy.wait()


def backward_call(n_fr, n_pos, shard_shapes, *operands):
    cot = operands[3]
    frames, features = cot.shape
    part = frames // n_pos
    chips = n_fr // 2
    tile = column_tile(features)
    count = len(shard_shapes)
    shard_rows = [rows for rows, _ in shard_shapes]
    hidden_units = operands[4].shape[1]
    act = jax.ShapeDtypeStruct((frames, features), BF16)
    most = max(shard_rows)
    down = operands[-2]
    late_count = max(1, down_pieces(shard_rows[-1]) * LATE // 100)
    early, late = split_terms(chips, n_pos * frames, shard_shapes)
    come_shapes = [(chips - 1, *shape) for shape in shard_shapes]
    return pl.pallas_call(
        functools.partial(backward_kernel, n_fr, n_pos, shard_rows, early, late),
        name="backward",
        out_shape=[jax.ShapeDtypeStruct(shape, BF16) for shape in shard_shapes]
        + [jax.ShapeDtypeStruct(come_shapes[at], BF16) for at in late]
        + [act, act, jax.ShapeDtypeStruct(down.shape, BF16)]
        + [jax.ShapeDtypeStruct((8, features // n_fr), F32)],
        in_specs=[ANY] * len(operands),
        out_specs=[ANY] * (count + len(late) + 4),
        input_output_aliases={len(operands) - 2: count + len(late) + 2},
        scratch_shapes=[
            pltpu.VMEM((columns // tile, chips, rows, tile), BF16) for rows, columns in shard_shapes
        ]
        + [pltpu.VMEM(come_shapes[at], BF16) for at in early]
        + [
            pltpu.VMEM((2, 2, chips, most, tile), BF16),
            pltpu.VMEM((2, tile, features), BF16),
            pltpu.VMEM((2, features, tile), BF16),
            pltpu.VMEM((2, features, tile), BF16),
            pltpu.VMEM((3, features, features), BF16),
            pltpu.VMEM((hidden_units, frames), BF16),
            pltpu.VMEM((frames, features), BF16),
            pltpu.VMEM((frames, hidden_units), BF16),
            pltpu.VMEM((frames, hidden_units), BF16),
            pltpu.VMEM((features, frames), BF16),
            pltpu.VMEM((features, frames), BF16),
            pltpu.VMEM((frames, features), F32),
            pltpu.VMEM((frames, features), F32),
            pltpu.VMEM((frames, features), BF16),
            pltpu.VMEM((frames, features), BF16),
            pltpu.VMEM((4, n_pos, part, features), BF16),
            pltpu.VMEM((n_pos, n_pos, part, LANES), F32),
            pltpu.VMEM((n_pos, n_pos, part, LANES), BF16),
            pltpu.VMEM((n_pos, part, LANES), F32),
            pltpu.VMEM((part, features), F32),
            pltpu.VMEM((3, n_pos, part, features), BF16),
            pltpu.VMEM((3, frames, features), BF16),
            pltpu.VMEM((features, LANES), BF16),
            pltpu.VMEM((LANES, features), BF16),
            pltpu.VMEM((n_fr, 8, features // n_fr), F32),
            pltpu.VMEM((n_fr, 8, features // n_fr), F32),
            pltpu.VMEM((8, features), F32),
            pltpu.VMEM((8, features), F32),
            DMA((21,)),
            DMA((2, 3)),
            DMA((2,)),
            DMA((sum(columns // tile for _, columns in shard_shapes),)),
            DMA((count * (chips - 1),)),
            DMA((count * (chips - 1),)),
            DMA((count,)),
            DMA((1,)),
            DMA((1,)),
            DMA((4,)),
            DMA((4,)),
            DMA((n_fr,)),
            DMA((n_fr,)),
            DMA((2,)),
            DMA((3,)),
            DMA((late_count * (chips - 1),)),
            DMA((late_count * (chips - 1),)),
            DMA((late_count * (chips - 1),)),
            DMA((late_count * (chips - 1),)),
            pltpu.VMEM(operands[0].shape, jnp.int32),
            pltpu.VMEM((8, features), F32),
            pltpu.VMEM((8, features // n_fr), F32),
        ],
        compiler_params=pltpu.CompilerParams(
            collective_id=1, has_side_effects=True, vmem_limit_bytes=VMEM_BYTES
        ),
    )(*operands)


def finish_kernel(count, late, *refs):
    kept, refs = refs[:count], refs[count:]
    come, refs = dict(zip(late, refs)), refs[len(late) :]
    output_in, input_grad_in, gains, *refs = refs
    sums, refs = refs[:count], refs[count:]
    output, input_grad, gain_one, gain_two, *refs = refs
    kept_v, refs = refs[:count], refs[count:]
    come_v, refs = dict(zip(late, refs)), refs[len(late) :]
    sums_v, refs = refs[:count], refs[count:]
    through, gains_v, load_sem, store_sem, through_sem = refs
    chunks = []
    for at in range(count):
        rows, columns = kept[at].shape
        cuts = next(
            cuts
            for cuts in (4, 2, 1)
            if rows % (16 * cuts) == 0 and (cuts == 1 or rows * columns >= cuts * 131072)
        )
        size = rows // cuts
        chunks += [(at, pl.ds(piece * size, size), piece) for piece in range(cuts)]

    order = {(at, piece): i for i, (at, _, piece) in enumerate(chunks)}

    def loads(at, rows, piece):
        copies = [
            pltpu.make_async_copy(kept[at].at[rows], kept_v[at].at[rows], load_sem.at[order[at, piece]])
        ]
        if at in come:
            copies.append(
                pltpu.make_async_copy(
                    come[at].at[:, rows], come_v[at].at[:, rows], load_sem.at[len(order) + order[at, piece]]
                )
            )
        return copies

    gains_copy = pltpu.make_async_copy(gains, gains_v, through_sem.at[4])
    gains_copy.start()
    acts = [
        pltpu.make_async_copy(output_in, through.at[0], through_sem.at[0]),
        pltpu.make_async_copy(input_grad_in, through.at[1], through_sem.at[1]),
    ]
    for copy in acts:
        copy.start()
    for chunk in chunks:
        for copy in loads(*chunk):
            copy.start()
    stores = []
    for copy, leaving, slot in zip(acts, (output, input_grad), range(2)):
        copy.wait()
        stores.append(pltpu.make_async_copy(through.at[slot], leaving, through_sem.at[2 + slot]))
        stores[-1].start()
    for at, rows, piece in chunks:
        for copy in loads(at, rows, piece):
            copy.wait()
        step = 16

        def add(i, carry):
            here = pl.ds(pl.multiple_of(rows.start + i * step, step), step)
            value = kept_v[at][here, :].astype(F32)
            for k in range(come_v[at].shape[0] if at in come else 0):
                value = value + come_v[at][k, here, :].astype(F32)
            sums_v[at][here, :] = value
            return carry

        lax.fori_loop(0, rows.size // step, add, 0)
        stores.append(
            pltpu.make_async_copy(sums_v[at].at[rows], sums[at].at[rows], store_sem.at[order[at, piece]])
        )
        stores[-1].start()
    gains_copy.wait()
    for row, gain in enumerate((gain_one, gain_two)):
        stores.append(
            pltpu.make_async_copy(gains_v.at[row : row + 1], gain, through_sem.at[5 + row])
        )
        stores[-1].start()
    for copy in stores:
        copy.wait()


def finish_call(late, kept, come, output, input_grad, gains):
    count = len(kept)
    gain = jax.ShapeDtypeStruct((1, gains.shape[1]), F32)
    return pl.pallas_call(
        functools.partial(finish_kernel, count, late),
        name="finish",
        out_shape=[jax.ShapeDtypeStruct(own.shape, F32) for own in kept]
        + [jax.ShapeDtypeStruct(output.shape, BF16)] * 2
        + [gain, gain],
        in_specs=[ANY] * (count + len(come) + 3),
        out_specs=[ANY] * (count + 4),
        scratch_shapes=[pltpu.VMEM(own.shape, BF16) for own in kept]
        + [pltpu.VMEM(others.shape, BF16) for others in come]
        + [pltpu.VMEM(own.shape, F32) for own in kept]
        + [
            pltpu.VMEM((2, *output.shape), BF16),
            pltpu.VMEM(gains.shape, F32),
            DMA((2 * 3 * count,)),
            DMA((3 * count,)),
            DMA((7,)),
        ],
        compiler_params=pltpu.CompilerParams(vmem_limit_bytes=VMEM_BYTES),
    )(*kept, *come, output, input_grad, gains)


def on_device(
    inputs,
    delays,
    query_weight,
    key_weight,
    value_weight,
    out_weight,
    gate_weight,
    up_weight,
    down_weight,
    attention_gain,
    feed_gain,
    cotangent,
):
    n_fr = lax.axis_size("fr")
    n_pos = lax.axis_size("pos")
    shards = [
        weight[0]
        for weight in (
            query_weight,
            key_weight,
            value_weight,
            out_weight,
            gate_weight,
            up_weight,
            down_weight,
        )
    ]
    delays = delays.T
    results = forward_call(n_fr, n_pos, inputs[0], delays, attention_gain, feed_gain, shards)
    full, saved, gain_rows = results[:7], results[7:20], results[20]
    inner_t, *saved = saved
    grads = backward_call(
        n_fr,
        n_pos,
        [shard.shape for shard in shards],
        delays,
        gain_rows,
        inner_t,
        cotangent[0],
        *saved,
        *full,
        shards[-1],
    )
    late = split_terms(
        n_fr // 2, n_pos * inputs.shape[1], [shard.shape for shard in shards]
    )[1]
    kept, come = grads[:7], grads[7 : 7 + len(late)]
    output, input_grad, _, gain_grads = grads[7 + len(late) :]
    *sums, output, input_grad, attention_gain_grad, feed_gain_grad = finish_call(
        late, kept, come, output, input_grad, gain_grads
    )
    return (
        output[None],
        input_grad[None],
        *(total[None] for total in sums),
        attention_gain_grad,
        feed_gain_grad,
    )


def solution(mesh):
    matrix = P("pos", "fr", None)
    vector = P("pos", "fr")
    return jax.shard_map(
        on_device,
        mesh=mesh,
        in_specs=(matrix, P("fr", "pos")) + (matrix,) * 7 + (vector, vector, matrix),
        out_specs=(matrix,) * 9 + (vector, vector),
        check_vma=False,
    )
```
